32 devices in a mesh: dp: 8 (over z, y), seq: 4 (over x, core).
Axes of the slice: x: 2, y: 2, z: 4, core: 2. Of those that a mesh axis runs over, the one named last changes fastest.
Arguments:
- x_long: bfloat16 [8, 512, 768], P('dp', 'seq'), may hold values from -6 to 6
- x_short: bfloat16 [8, 256, 768], P('dp', 'seq'), may hold values from -6 to 6
- len_long: int32 [8], P('dp'), may hold values from 64 to 512, as said below
- len_short: int32 [8], P('dp'), may hold values from 32 to 256, as said below
- w_attn_in: bfloat16 [2, 768, 2304], replicated, may hold values from -0.21875 to 0.21875
- w_attn_out: bfloat16 [2, 768, 768], replicated, may hold values from -3.5 to 3.5
- w_ffn_in: bfloat16 [2, 768, 3072], replicated, may hold values from -0.21875 to 0.21875
- w_ffn_out: bfloat16 [2, 3072, 768], replicated, may hold values from -0.109375 to 0.109375
- bias_vec: bfloat16 [2, 6, 768], replicated, may hold values from -1.796875 to 1.796875
- gain_vec: bfloat16 [2, 2, 768], replicated, may hold values from 0.5 to 1.5
- bias_ffn: bfloat16 [2, 3072], replicated, may hold values from -1.796875 to 1.796875
- cot_long: bfloat16 [8, 512, 768], P('dp', 'seq'), may hold values from -6 to 6
- cot_short: bfloat16 [8, 256, 768], P('dp', 'seq'), may hold values from -6 to 6
Outputs:
- y_long: bfloat16 [8, 512, 768], P('dp', 'seq')
- y_short: bfloat16 [8, 256, 768], P('dp', 'seq')
- dx_long: float32 [8, 512, 768], P('dp', 'seq')
- dx_short: float32 [8, 256, 768], P('dp', 'seq')
- g_attn_in: float32 [2, 768, 2304], P(None, 'seq', 'dp')
- g_attn_out: float32 [2, 768, 768], P(None, 'seq', 'dp')
- g_ffn_in: float32 [2, 768, 3072], P(None, 'seq', 'dp')
- g_ffn_out: float32 [2, 3072, 768], P(None, 'seq', 'dp')
- g_bias: float32 [2, 6, 768], P(None, None, 'dp')
- g_gain: float32 [2, 2, 768], P(None, None, 'dp')
- g_bias_ffn: float32 [2, 3072], P(None, 'dp')
The draws below stay inside these ranges and needn't reach their ends.
Inputs may be any that keep to these rules, and one draw needn't show every extreme that they name: `len_long`: valid positions of each long sequence; later positions are padding, and some sequence is full. `len_short`: valid positions of each short sequence; later positions are padding, and some sequence is full.
All inputs are finite; a program needn't handle non-finite values.
Results may differ from the reference program's by a relative error of at most 0.025.
Values may be sent and summed in bfloat16 or wider, within the bound.
A program may use at most 256 MiB of HBM per device.

```python
import jax
import jax.numpy as jnp
from jax import lax

D = 768
HEADS = 12
HD = 64
FF = 3072
LAYERS = 2
LONG_LEN = 512
SHORT_LEN = 256
SEQ_LONG = 1
SEQ_SHORT = 1
SL_ALL = 8
SS_ALL = 8


def ragged_lengths(key, count, longest):
    low_end = max(longest // 8, 1)
    key_values, key_place = jax.random.split(key)
    values = jax.random.randint(key_values, (count,), low_end, longest + 1)
    position = jax.random.randint(key_place, (), 0, count)
    values = values.at[position].set(longest)
    values = values.at[(position + 1) % count].set(low_end)
    return values.astype(jnp.int32)


def draw_len_long(key, part):
    return ragged_lengths(jax.random.fold_in(key, 11), SL_ALL, LONG_LEN)


def draw_len_short(key, part):
    return ragged_lengths(jax.random.fold_in(key, 23), SS_ALL, SHORT_LEN)


def strengthened(values, key, source, target, shards_of, factor):
    def block_of(dim):
        return (jnp.arange(values.shape[dim]) // (values.shape[dim] // shards_of)).reshape((-1,) + (1,) * (values.ndim - 1 - dim))

    one_side = jax.random.permutation(key, shards_of)[block_of(target)]
    other_side = (block_of(target) + shards_of // 2) % shards_of
    return jnp.where((block_of(source) == one_side) | (block_of(source) == other_side), factor * values, values)


def block_levels(rng, extent, cuts, least, top_value):
    gain, own = 1.0, jax.random.fold_in(rng, 6)
    for axis_at, shards_of in cuts:
        draws = jnp.exp(jax.random.uniform(jax.random.fold_in(own, axis_at), (shards_of,), jnp.float32, least / len(cuts), top_value / len(cuts)))
        gain = gain * jnp.repeat(draws, extent[axis_at] // shards_of).reshape([-1 if axis == axis_at else 1 for axis in range(len(extent))])
    return gain


def bell_draw(rng, extent, scale, reach, cuts=(), held_as=jnp.bfloat16):
    drawn = scale * jax.random.normal(rng, extent, jnp.float32)
    if cuts:
        drawn = drawn * block_levels(rng, extent, cuts, -0.22, 0.18)
    return jnp.clip(drawn, -reach, reach).astype(held_as)


def bell_draw_with(stream_key, dims, deviation, bound, cuts, heavy, kind=jnp.bfloat16):
    entries = deviation * jax.random.normal(stream_key, dims, jnp.float32)
    if cuts:
        entries = entries * block_levels(stream_key, dims, cuts, -0.22, 0.18)
    return jnp.clip(strengthened(entries, jax.random.fold_in(stream_key, 3), *heavy), -bound, bound).astype(kind)


def setup_inputs(seed: int = 0) -> dict:
    seeds = jax.random.split(jax.random.key(seed), 14)
    x_long = bell_draw(seeds[0], (SL_ALL, LONG_LEN, D), 1.0, 6.0, ((0, 8), (1, 4)))
    x_short = bell_draw(seeds[1], (SS_ALL, SHORT_LEN, D), 1.0, 6.0, ((0, 8), (1, 4)))
    len_long = draw_len_long(jax.random.fold_in(seeds[13], 71), 0)
    len_short = draw_len_short(jax.random.fold_in(seeds[13], 71), 0)
    w_attn_in = bell_draw(seeds[4], (LAYERS, D, 3 * D), D ** -0.5, 0.21875)
    w_attn_out = bell_draw(seeds[5], (LAYERS, D, D), (max(D // 256, 1)) ** -0.5, 3.5)
    w_ffn_in = bell_draw(seeds[6], (LAYERS, D, FF), D ** -0.5, 0.21875)
    w_ffn_out = bell_draw(seeds[7], (LAYERS, FF, D), FF ** -0.5, 0.109375)
    bias_vec = bell_draw(seeds[8], (LAYERS, 6, D), 0.3, 1.796875)
    gain_vec = jnp.clip(1.0 + 0.1 * jax.random.normal(seeds[9], (LAYERS, 2, D), jnp.float32), 0.5, 1.5).astype(jnp.bfloat16)
    bias_ffn = bell_draw(seeds[10], (LAYERS, FF), 0.3, 1.796875)
    cot_long = bell_draw_with(seeds[11], (SL_ALL, LONG_LEN, D), 1.0, 6.0, ((0, 8), (1, 4)), (0, 2, 8, 2.0))
    cot_short = bell_draw_with(seeds[12], (SS_ALL, SHORT_LEN, D), 1.0, 6.0, ((0, 8), (1, 4)), (0, 2, 8, 2.0))
    return dict(x_long=x_long, x_short=x_short, len_long=len_long, len_short=len_short, w_attn_in=w_attn_in, w_attn_out=w_attn_out, w_ffn_in=w_ffn_in, w_ffn_out=w_ffn_out, bias_vec=bias_vec, gain_vec=gain_vec, bias_ffn=bias_ffn, cot_long=cot_long, cot_short=cot_short)


@jax.custom_vjp
def low(v):
    return lax.optimization_barrier(v.astype(jnp.bfloat16)).astype(jnp.float32)

@jax.custom_vjp
def low_back(v):
    return v

def low_keep(v):
    return (low(v), None)

def low_pass(kept, grad):
    return (grad,)

def back_keep(v):
    return (v, None)

def back_low(kept, grad):
    return (low(grad),)
low.defvjp(low_keep, low_pass)
low_back.defvjp(back_keep, back_low)

def matmul(left_side, right_side):
    return jnp.dot(left_side, right_side, precision=lax.Precision.HIGHEST)

def layer_norm(values, gain_row, shift_row):
    centre = values - lax.optimization_barrier(jnp.mean(values, axis=-1, keepdims=True))
    spread = lax.optimization_barrier(jnp.mean(centre * centre, axis=-1, keepdims=True))
    return centre * lax.rsqrt(spread + 1e-12) * gain_row + shift_row

def attention(packed, lengths):
    seq_count, length, _ = packed.shape
    split_heads = packed.reshape(seq_count, length, 3, HEADS, HD)
    query_rows = split_heads[:, :, 0]
    key_rows = split_heads[:, :, 1]
    value_rows = split_heads[:, :, 2]
    scores = jnp.einsum('bqhd,bkhd->bhqk', query_rows, key_rows, precision=lax.Precision.HIGHEST) * HD ** (-0.5)
    places = jnp.arange(length, dtype=jnp.int32)
    key_valid = places[None, :] < lengths[:, None]
    scores = jnp.where(key_valid[:, None, None, :], scores, -1000000000.0)
    scores = low_back(scores)
    weights = low(jax.nn.softmax(scores, axis=-1))
    context = jnp.einsum('bhqk,bkhd->bqhd', weights, value_rows, precision=lax.Precision.HIGHEST)
    return context.reshape(seq_count, length, D)

def encoder_layer(long_rows, short_rows, lengths_long, lengths_short, layer_params):
    weight_in, weight_out, weight_up, weight_down, biases, gain_rows, bias_up = layer_params
    count_long = long_rows.shape[0] * long_rows.shape[1]
    token_rows = jnp.concatenate([long_rows.reshape(-1, D), short_rows.reshape(-1, D)], axis=0)
    packed_bias = jnp.concatenate([biases[0], jnp.zeros_like(biases[0]), biases[1]])
    packed = low_back(low(matmul(token_rows, weight_in) + packed_bias))
    packed_long = packed[:count_long].reshape(long_rows.shape[0], long_rows.shape[1], 3 * D)
    packed_short = packed[count_long:].reshape(short_rows.shape[0], short_rows.shape[1], 3 * D)
    context_long = jax.checkpoint(attention)(packed_long, lengths_long)
    context_short = jax.checkpoint(attention)(packed_short, lengths_short)
    context = jnp.concatenate([context_long.reshape(-1, D), context_short.reshape(-1, D)], axis=0)
    context = low_back(low(context))
    branch = low_back(matmul(context, weight_out) + biases[2])
    normed = low(layer_norm(token_rows + branch, gain_rows[0], biases[3]))
    hidden_pre = low_back(matmul(normed, weight_up) + bias_up)
    hidden = low(jax.nn.gelu(hidden_pre, approximate=False))
    feed_out = low_back(matmul(hidden, weight_down) + biases[4])
    layer_out = low(layer_norm(normed + feed_out, gain_rows[1], biases[5]))
    return (layer_out[:count_long].reshape(long_rows.shape), layer_out[count_long:].reshape(short_rows.shape))

def reference(x_long, x_short, len_long, len_short, w_attn_in, w_attn_out, w_ffn_in, w_ffn_out, bias_vec, gain_vec, bias_ffn, cot_long, cot_short):
    weights_all = tuple((array.astype(jnp.float32) for array in (w_attn_in, w_attn_out, w_ffn_in, w_ffn_out, bias_vec, gain_vec, bias_ffn)))
    groups = x_long.shape[0] // SEQ_LONG

    def regroup(array, count):
        return array.reshape((groups, count) + array.shape[1:])
    sliced = (regroup(x_long.astype(jnp.float32), SEQ_LONG), regroup(x_short.astype(jnp.float32), SEQ_SHORT), regroup(len_long, SEQ_LONG), regroup(len_short, SEQ_SHORT), regroup(cot_long.astype(jnp.float32), SEQ_LONG), regroup(cot_short.astype(jnp.float32), SEQ_SHORT))

    def group_step(running, pieces):
        long_in, short_in, lengths_long, lengths_short, grad_long_out, grad_short_out = pieces

        def forward(long_rows, short_rows, params):
            for layer_idx in range(LAYERS):
                layer_params = tuple((array[layer_idx] for array in params))
                long_rows, short_rows = encoder_layer(long_rows, short_rows, lengths_long, lengths_short, layer_params)
            return (long_rows, short_rows)
        outputs, pullback = jax.vjp(forward, long_in, short_in, weights_all)
        grad_long, grad_short, grad_params = pullback((grad_long_out, grad_short_out))
        running = tuple((before + gradient for before, gradient in zip(running, grad_params)))
        return (running, (outputs[0], outputs[1], grad_long, grad_short))
    initial = tuple((jnp.zeros_like(array) for array in weights_all))
    running, stacked = lax.scan(group_step, initial, sliced)
    y_long = stacked[0].reshape(x_long.shape).astype(jnp.bfloat16)
    y_short = stacked[1].reshape(x_short.shape).astype(jnp.bfloat16)
    dx_long = stacked[2].reshape(x_long.shape)
    dx_short = stacked[3].reshape(x_short.shape)
    return (y_long, y_short, dx_long, dx_short, running[0], running[1], running[2], running[3], running[4], running[5], running[6])
```

```python
from functools import partial

import jax
import jax.numpy as jnp
from jax import lax
from jax.experimental import pallas as pl
from jax.experimental.pallas import tpu as pltpu
from jax.sharding import PartitionSpec as P

HD = 64
LAYERS = 2
PAIR = 2 * HD
F32 = jnp.float32
BF16 = jnp.bfloat16
MESH = pl.DeviceIdType.MESH
VMEM_LIMIT = 58 << 20
ANY = pl.BlockSpec(memory_space=pl.ANY)
VMEM = pl.BlockSpec(memory_space=pltpu.VMEM)
SMEM = pl.BlockSpec(memory_space=pltpu.SMEM)


def dot(left, right):
    return jnp.dot(left, right, preferred_element_type=F32)


def dot_t(left, right):
    return lax.dot_general(left, right, (((1,), (1,)), ((), ())), preferred_element_type=F32)


def t_dot(left, right):
    return lax.dot_general(left, right, (((0,), (0,)), ((), ())), preferred_element_type=F32)


def row_mean(values):
    return jnp.mean(values, axis=-1, keepdims=True)


def col_sum(values):
    return jnp.sum(values, axis=0, keepdims=True)


def lane_masks():
    lane = lax.broadcasted_iota(jnp.int32, (1, PAIR), 1)
    low = lane < HD
    return low, low.astype(F32).astype(BF16), (~low).astype(F32).astype(BF16)


def attend_pair(query, keys, values, length):
    low, mask_low, mask_high = lane_masks()
    place = lax.broadcasted_iota(jnp.int32, (1, keys.shape[0]), 1)
    outs = []
    for mask in (mask_low, mask_high):
        scores = dot_t(query * mask, keys)
        scores = jnp.where(place < length, scores, -1e9)
        powers = jnp.exp(scores - jnp.max(scores, axis=1, keepdims=True))
        weights = powers * (1.0 / jnp.sum(powers, axis=1, keepdims=True))
        outs.append(dot(weights.astype(BF16), values))
    return jnp.where(low, outs[0], outs[1])


def forward_kernel(
    layer, tl, ts,
    lens, h_all, h_own, w_in, w_out, w_up, w_down, bias, gain, bias_up,
    q_o, k_o, v_o, ctx_o, xh1_o, inv1_o, nrm_o, slope_o, hid_o, xh2_o, inv2_o, h_o,
    w_in_v, w_out_v, w_up_v, w_down_v, rows_v, up_v, sems,
):
    copies = [
        pltpu.make_async_copy(src.at[layer], dst, sems.at[i])
        for i, (src, dst) in enumerate(
            ((w_in, w_in_v), (w_out, w_out_v), (w_up, w_up_v), (w_down, w_down_v))
        )
    ]
    for copy in copies:
        copy.start()
    n_seq, rows, width = h_all.shape
    biases = bias[layer].astype(F32)
    gains = gain[layer].astype(F32)
    up_v[...] = bias_up[...].astype(F32)
    rows_v[0:1, :] = biases[0:1]
    rows_v[1:2, :] = biases[1:2]
    copies[0].wait()
    step = 256

    @pl.loop(0, width // step)
    def _(i):
        cols = pl.ds(pl.multiple_of(i * step, step), step)
        kcols = pl.ds(pl.multiple_of(width + i * step, step), step)
        vcols = pl.ds(pl.multiple_of(2 * width + i * step, step), step)
        query = dot(h_own[...], w_in_v[:, cols]) + rows_v[0:1, cols]
        q_o[:, cols] = query.astype(BF16) * jnp.asarray(HD**-0.5, BF16)
        for s in range(n_seq):
            key = dot(h_all[s], w_in_v[:, kcols]).astype(BF16)
            value = (dot(h_all[s], w_in_v[:, vcols]) + rows_v[1:2, cols]).astype(BF16)
            for out, piece in ((k_o, key), (v_o, value)):
                out[tl * s : tl * (s + 1), cols] = piece[:tl]
                out[n_seq * tl + ts * s : n_seq * tl + ts * (s + 1), cols] = piece[tl:]

    @pl.loop(0, width // PAIR)
    def _(p):
        lanes = pl.ds(pl.multiple_of(p * PAIR, PAIR), PAIR)
        edge = n_seq * tl
        for own, keys, which in ((slice(0, tl), slice(0, edge), 0), (slice(tl, rows), slice(edge, n_seq * rows), 1)):
            ctx_o[own, lanes] = attend_pair(
                q_o[own, lanes], k_o[keys, lanes], v_o[keys, lanes], lens[which]
            ).astype(BF16)

    copies[1].wait()
    residual = h_own[...].astype(F32) + dot(ctx_o[...], w_out_v[...]) + biases[2:3]
    centre = residual - row_mean(residual)
    inverse = lax.rsqrt(row_mean(centre * centre) + 1e-12)
    scaled = centre * inverse
    xh1_o[...] = scaled
    inv1_o[...] = jnp.broadcast_to(inverse, inv1_o.shape)
    nrm_o[...] = (scaled * gains[0:1] + biases[3:4]).astype(BF16)

    copies[2].wait()

    @pl.loop(0, w_up_v.shape[1] // step)
    def _(i):
        cols = pl.ds(pl.multiple_of(i * step, step), step)
        pre = dot(nrm_o[...], w_up_v[:, cols]) + up_v[layer : layer + 1, cols]
        below = 0.5 + 0.5 * lax.erf(pre * (2.0**-0.5))
        hid_o[:, cols] = (pre * below).astype(BF16)
        slope_o[:, cols] = below + pre * (jnp.exp(pre * pre * -0.5) * 0.3989422804014327)

    copies[3].wait()
    residual = nrm_o[...].astype(F32) + dot(hid_o[...], w_down_v[...]) + biases[4:5]
    centre = residual - row_mean(residual)
    inverse = lax.rsqrt(row_mean(centre * centre) + 1e-12)
    scaled = centre * inverse
    xh2_o[...] = scaled
    inv2_o[...] = jnp.broadcast_to(inverse, inv2_o.shape)
    h_o[...] = (scaled * gains[1:2] + biases[5:6]).astype(BF16)


def forward_layer(layer, tl, ts, lens, h_all, h_own, weights, bias, gain, bias_up):
    n_seq, rows, width = h_all.shape
    hidden = weights[2].shape[2]
    shapes = [
        ((rows, width), BF16),
        ((n_seq * rows, width), BF16),
        ((n_seq * rows, width), BF16),
        ((rows, width), BF16),
        ((rows, width), F32),
        ((rows, 128), F32),
        ((rows, width), BF16),
        ((rows, hidden), F32),
        ((rows, hidden), BF16),
        ((rows, width), F32),
        ((rows, 128), F32),
        ((rows, width), BF16),
    ]
    return pl.pallas_call(
        partial(forward_kernel, layer, tl, ts),
        out_shape=[jax.ShapeDtypeStruct(shape, dtype) for shape, dtype in shapes],
        in_specs=[SMEM, VMEM, VMEM] + [ANY] * 4 + [VMEM] * 3,
        out_specs=[VMEM] * len(shapes),
        scratch_shapes=[pltpu.VMEM(w.shape[1:], BF16) for w in weights]
        + [pltpu.VMEM((8, width), F32), pltpu.VMEM((LAYERS, hidden), F32), pltpu.SemaphoreType.DMA((4,))],
        compiler_params=pltpu.CompilerParams(vmem_limit_bytes=VMEM_LIMIT),
        name=f"layer_forward_{layer}",
    )(lens, h_all, h_own, *weights, bias, gain, bias_up)


def norm_back(gradient, scaled, inverse, gain_row):
    inner = gradient * gain_row
    return inverse * (inner - row_mean(inner) - scaled * row_mean(inner * scaled))


def back_pair(query, keys, values, grad, length):
    low, mask_low, mask_high = lane_masks()
    place = lax.broadcasted_iota(jnp.int32, (keys.shape[0], 1), 0)
    outs = []
    for mask in (mask_low, mask_high):
        scores = dot_t(keys, query * mask)
        scores = jnp.where(place < length, scores, -1e9)
        powers = jnp.exp(scores - jnp.max(scores, axis=0, keepdims=True))
        probs = powers * (1.0 / jnp.sum(powers, axis=0, keepdims=True))
        grad_probs = dot_t(values, grad * mask)
        inner = col_sum(probs * grad_probs)
        grad_scores = (probs * (grad_probs - inner)).astype(BF16)
        outs.append(
            (
                t_dot(grad_scores, keys) * HD**-0.5,
                dot(grad_scores, query),
                dot(probs.astype(BF16), grad),
            )
        )
    return [jnp.where(low, first, second) for first, second in zip(*outs)]


def backward_kernel(
    layer, tl, ts,
    lens, g, q, k, v, xh1, inv1, slope, xh2, inv2, w_out, w_up, w_down, gain,
    feed_o, pre_o, branch_o, one_o, dq_o, dkv_o, small_o,
    w_out_v, w_up_v, w_down_v, two_v, ctx_v, sems,
):
    copies = [
        pltpu.make_async_copy(src.at[layer], dst, sems.at[i])
        for i, (src, dst) in enumerate(((w_down, w_down_v), (w_up, w_up_v), (w_out, w_out_v)))
    ]
    for copy in copies:
        copy.start()
    rows, width = g.shape
    n_seq = k.shape[0] // rows
    hidden = w_up_v.shape[1]
    gains = gain[layer].astype(F32)
    step = 256

    grad = g[...]
    small_o[5:6, :] = col_sum(grad)
    small_o[7:8, :] = col_sum(grad * xh2[...])
    two = norm_back(grad, xh2[...], inv2[:, 0:1], gains[1:2])
    two_v[...] = two
    feed_o[...] = two.astype(BF16)
    small_o[4:5, :] = col_sum(feed_o[...].astype(F32))

    copies[0].wait()
    per_row = width // step

    for part in range(hidden // width):

        @pl.loop(0, per_row)
        def _(i, part=part):
            cols = pl.ds(pl.multiple_of(part * width + i * step, step), step)
            back = dot_t(feed_o[...], w_down_v[cols, :]) * slope[:, cols]
            pre_o[:, cols] = back.astype(BF16)
            small_o[8 + part : 9 + part, pl.ds(pl.multiple_of(i * step, step), step)] = col_sum(
                pre_o[:, cols].astype(F32)
            )

    copies[1].wait()

    @pl.loop(0, per_row)
    def _(i):
        cols = pl.ds(pl.multiple_of(i * step, step), step)
        two_v[:, cols] = two_v[:, cols] + dot_t(pre_o[...], w_up_v[cols, :])

    grad = two_v[...]
    small_o[3:4, :] = col_sum(grad)
    small_o[6:7, :] = col_sum(grad * xh1[...])
    one = norm_back(grad, xh1[...], inv1[:, 0:1], gains[0:1])
    one_o[...] = one
    branch_o[...] = one.astype(BF16)
    small_o[2:3, :] = col_sum(branch_o[...].astype(F32))

    copies[2].wait()

    @pl.loop(0, per_row)
    def _(i):
        cols = pl.ds(pl.multiple_of(i * step, step), step)
        ctx_v[:, cols] = dot_t(branch_o[...], w_out_v[cols, :]).astype(BF16)

    edge = n_seq * tl

    @pl.loop(0, width // PAIR)
    def _(p):
        lanes = pl.ds(pl.multiple_of(p * PAIR, PAIR), PAIR)
        vlanes = pl.ds(pl.multiple_of(width + p * PAIR, PAIR), PAIR)
        sums_q = jnp.zeros((1, PAIR), F32)
        sums_v = jnp.zeros((1, PAIR), F32)
        for own, keys, which, count in (
            (slice(0, tl), slice(0, edge), 0, tl),
            (slice(tl, rows), slice(edge, n_seq * rows), 1, ts),
        ):
            grad_q, grad_k, grad_v = back_pair(
                q[own, lanes], k[keys, lanes], v[keys, lanes], ctx_v[own, lanes], lens[which]
            )
            grad_q = grad_q.astype(BF16)
            dq_o[own, lanes] = grad_q
            sums_q += col_sum(grad_q.astype(F32))
            sums_v += col_sum(grad_v)
            grad_k = grad_k.astype(BF16)
            grad_v = grad_v.astype(BF16)
            for s in range(n_seq):
                dkv_o[s, own, lanes] = grad_k[count * s : count * (s + 1)]
                dkv_o[s, own, vlanes] = grad_v[count * s : count * (s + 1)]
        small_o[0:1, lanes] = sums_q
        small_o[1:2, lanes] = sums_v


def backward_layer(layer, tl, ts, lens, g, saved, weights, gain):
    q, k, v, ctx, xh1, inv1, nrm, slope, hid, xh2, inv2 = saved
    rows, width = g.shape
    hidden = weights[2].shape[2]
    shapes = [
        ((rows, width), BF16),
        ((rows, hidden), BF16),
        ((rows, width), BF16),
        ((rows, width), F32),
        ((rows, width), BF16),
        ((k.shape[0] // rows, rows, 2 * width), BF16),
        ((8 + hidden // width, width), F32),
    ]
    return pl.pallas_call(
        partial(backward_kernel, layer, tl, ts),
        out_shape=[jax.ShapeDtypeStruct(shape, dtype) for shape, dtype in shapes],
        in_specs=[SMEM] + [VMEM] * 9 + [ANY] * 3 + [VMEM],
        out_specs=[VMEM] * len(shapes),
        scratch_shapes=[pltpu.VMEM(w.shape[1:], BF16) for w in weights[1:]]
        + [pltpu.VMEM((rows, width), F32), pltpu.VMEM((rows, width), BF16), pltpu.SemaphoreType.DMA((3,))],
        compiler_params=pltpu.CompilerParams(vmem_limit_bytes=VMEM_LIMIT),
        name=f"layer_backward_{layer}",
    )(lens, g, q, k, v, xh1, inv1, slope, xh2, inv2, *weights[1:], gain)


def slab_rows(model, hidden, n_dp):
    half = 2 * n_dp
    sizes = (3 * model // half, model // half, hidden // half, (hidden // model) * (model // half))
    starts = [0]
    for size in sizes:
        starts.append(starts[-1] + size)
    return sizes, starts


def weights_kernel(
    layer, n_dp,
    h_own, ctx, nrm, hid, dq, dkv, feed, pre, branch, one, w_in,
    g_o, slab_o,
    w_in_v, packed_v, slab_v, sems,
):
    rows, width = h_own.shape
    hidden = hid.shape[1]
    load = pltpu.make_async_copy(w_in.at[layer], w_in_v, sems.at[0])
    load.start()
    packed_v[:, 0:width] = dq[...]
    packed_v[:, width:] = dkv[...]
    half = width // 2
    sizes, starts = slab_rows(width, hidden, n_dp)
    step = 384
    pieces = (3 * width // (2 * n_dp), width // (2 * n_dp), hidden // (2 * n_dp), width // (2 * n_dp))

    def put(out, base, first, piece, start, count):
        row = 0
        while row < count:
            place = first + row
            take = min(piece - place % piece, count - row)
            block = base + place // (2 * piece)
            core = (place // piece) % 2
            at = start + place % piece
            yield block, core, at, row, take
            row += take

    def matrix(left_ref, right_ref, which):
        piece = pieces[which]
        n_rows = piece * 2 * n_dp
        group = step
        while group % (2 * piece):
            group += step
        blocks = group // (2 * piece)

        @pl.loop(0, n_rows // group)
        def _(i):
            for sub in range(group // step):
                cols = pl.ds(pl.multiple_of(i * group + sub * step, 128), step)
                out = t_dot(left_ref[:, cols], right_ref[...])
                for x in range(2):
                    value = out[:, half * x : half * (x + 1)].astype(BF16)
                    for block, core, at, row, take in put(value, i * blocks, sub * step, piece, starts[which], step):
                        slab_v[block, x, core, at : at + take, :] = value[row : row + take]

    matrix(pre, nrm, 2)
    matrix(branch, ctx, 1)
    piece = pieces[3]
    group = step
    blocks = group // (2 * piece)

    @pl.loop(0, width // group)
    def _(i):
        cols = pl.ds(pl.multiple_of(i * group, 128), group)
        for part in range(hidden // width):
            out = t_dot(feed[:, cols], hid[:, width * part : width * (part + 1)])
            for sub in range(2):
                strip = 2 * part + sub
                value = out[:, half * sub : half * (sub + 1)].astype(BF16)
                strips = hidden // half // 2
                at0 = starts[3] + piece * (strip % strips)
                for block, core, at, row, take in put(value, i * blocks, 0, piece, at0, group):
                    slab_v[block, strip // strips, core, at : at + take, :] = value[row : row + take]

    matrix(packed_v, h_own, 0)
    store = pltpu.make_async_copy(slab_v, slab_o, sems.at[1])
    store.start()
    load.wait()

    @pl.loop(0, width // 256)
    def _(i):
        cols = pl.ds(pl.multiple_of(i * 256, 256), 256)
        g_o[:, cols] = one[:, cols] + dot_t(packed_v[...], w_in_v[cols, :])

    store.wait()


def weights_layer(layer, n_dp, h_own, saved, back, dkv, weights):
    q, k, v, ctx, xh1, inv1, nrm, slope, hid, xh2, inv2 = saved
    feed, pre, branch, one, dq, _, _ = back
    rows, width = h_own.shape
    hidden = hid.shape[1]
    sizes, starts = slab_rows(width, hidden, n_dp)
    slab = (n_dp, 2, 2, starts[-1], width // 2)
    return pl.pallas_call(
        partial(weights_kernel, layer, n_dp),
        out_shape=[jax.ShapeDtypeStruct((rows, width), F32), jax.ShapeDtypeStruct(slab, BF16)],
        in_specs=[VMEM] * 10 + [ANY],
        out_specs=[VMEM, ANY],
        scratch_shapes=[
            pltpu.VMEM(weights[0].shape[1:], BF16),
            pltpu.VMEM((rows, 3 * width), BF16),
            pltpu.VMEM(slab, BF16),
            pltpu.SemaphoreType.DMA((2,)),
        ],
        compiler_params=pltpu.CompilerParams(vmem_limit_bytes=VMEM_LIMIT),
        name=f"layer_weights_{layer}",
    )(h_own, ctx, nrm, hid, dq, dkv, feed, pre, branch, one, weights[0])


def seq_place():
    d = lax.axis_index("dp")
    s = lax.axis_index("seq")
    x = s // 2
    c = lax.rem(s, 2)
    return d, x, c


def greet(peers):
    barrier = pltpu.get_barrier_semaphore()
    for peer in peers:
        pl.semaphore_signal(barrier, inc=1, device_id=peer, device_id_type=MESH)
    pl.semaphore_wait(barrier, len(peers))


def remote(src, dst, send, recv, peer):
    return pltpu.make_async_remote_copy(
        src_ref=src, dst_ref=dst, send_sem=send, recv_sem=recv, device_id=peer, device_id_type=MESH
    )


def gather_kernel(own, out, send, recv, local):
    d, x, c = seq_place()
    mine = 2 * x + c
    sibling = (d, 2 * x + 1 - c)
    across = (d, 2 * (1 - x) + c)
    far = 2 * (1 - x) + c
    greet((sibling, across))
    first = remote(own, out.at[mine], send.at[0], recv.at[0], across)
    second = remote(own, out.at[mine], send.at[1], recv.at[1], sibling)
    first.start()
    second.start()
    keep = pltpu.make_async_copy(own, out.at[mine], local)
    keep.start()
    first.wait_recv()
    third = remote(out.at[far], out.at[far], send.at[2], recv.at[2], sibling)
    third.start()
    keep.wait()
    first.wait_send()
    second.wait()
    third.wait()


def gather_rows(own, n_seq, collective):
    return pl.pallas_call(
        gather_kernel,
        out_shape=jax.ShapeDtypeStruct((n_seq,) + own.shape, own.dtype),
        in_specs=[VMEM],
        out_specs=VMEM,
        scratch_shapes=[
            pltpu.SemaphoreType.DMA((3,)),
            pltpu.SemaphoreType.DMA((3,)),
            pltpu.SemaphoreType.DMA,
        ],
        compiler_params=pltpu.CompilerParams(collective_id=collective, has_side_effects=True),
        name="gather_rows",
    )(own)


def scatter_kernel(parts, out, near, total, send, recv):
    d, x, c = seq_place()
    sibling = (d, 2 * x + 1 - c)
    across = (d, 2 * (1 - x) + c)
    greet((sibling, across))
    first = remote(parts.at[2 * (1 - x) + 1 - c], near.at[0], send.at[0], recv.at[0], sibling)
    second = remote(parts.at[2 * x + 1 - c], near.at[1], send.at[1], recv.at[1], sibling)
    first.start()
    second.start()
    first.wait_recv()
    far = 2 * (1 - x) + c
    total[0] = (parts[far].astype(F32) + near[0].astype(F32)).astype(BF16)
    third = remote(total.at[0], total.at[1], send.at[2], recv.at[2], across)
    third.start()
    second.wait_recv()
    kept = parts[2 * x + c].astype(F32) + near[1].astype(F32)
    third.wait_recv()
    out[...] = (kept + total[1].astype(F32)).astype(BF16)
    first.wait_send()
    second.wait_send()
    third.wait_send()


def scatter_rows(parts, collective):
    shape = parts.shape[1:]
    return pl.pallas_call(
        scatter_kernel,
        out_shape=jax.ShapeDtypeStruct(shape, parts.dtype),
        in_specs=[VMEM],
        out_specs=VMEM,
        scratch_shapes=[
            pltpu.VMEM((2,) + shape, BF16),
            pltpu.VMEM((2,) + shape, BF16),
            pltpu.SemaphoreType.DMA((3,)),
            pltpu.SemaphoreType.DMA((3,)),
        ],
        compiler_params=pltpu.CompilerParams(
            collective_id=collective, has_side_effects=True, vmem_limit_bytes=VMEM_LIMIT
        ),
        name="scatter_rows",
    )(parts)


SIZE = {"z": 4, "y": 2, "x": 2}
ORDERS = (("x", "y", "z"), ("y", "x", "z"), ("z", "x", "y"), ("z", "y", "x"))


def upper_rows(piece):
    return (piece // 2 + 15) // 16 * 16


def stage_buffers(order, piece, wide):
    free = ["z", "y", "x"]
    shapes = [tuple(SIZE[a] for a in free) + (piece, wide)]
    for axis in order:
        free.remove(axis)
        lead = tuple(SIZE[a] for a in free)
        if axis == "z":
            top = upper_rows(piece)
            shapes += [lead + (top, wide), lead + (piece - top, wide), (2,) + lead + (piece, wide)]
        else:
            shapes.append(lead + (piece, wide))
    return shapes


def reduce_kernel(shapes, turns, slabs, small_in, outs, small_out, work, total, small, landing, send, recv, loads, flip):
    d = lax.axis_index("dp")
    s = lax.axis_index("seq")
    here = {"z": d // 2, "y": lax.rem(d, 2), "x": s // 2}
    c = lax.rem(s, 2)

    def device(z=None, y=None, x=None, core=None):
        z = here["z"] if z is None else z
        y = here["y"] if y is None else y
        x = here["x"] if x is None else x
        core = c if core is None else core
        return (2 * z + y, 2 * x + core)

    ring = lambda step: lax.rem(here["z"] + step, 4)
    sibling = device(core=1 - c)
    peer = {"x": device(x=1 - here["x"]), "y": device(y=1 - here["y"])}
    up, down, opposite = device(z=ring(1)), device(z=ring(3)), device(z=ring(2))
    greet((sibling, peer["x"], peer["y"], up, down, opposite))

    count = iter(range(send.shape[0]))
    pending = []
    wide = work.shape[-1]
    piece = work.shape[-2]

    def push(src, dst, to):
        at = next(count)
        copy = remote(src, dst, send.at[at], recv.at[at], to)
        copy.start()
        pending.append(copy)
        return copy

    def pick(free, where, rows=None):
        index = tuple(slice(None) if a in free else where[a] for a in "zyx")
        return index if rows is None else index + (rows,)

    def each(free, run):
        sizes = [SIZE[a] for a in free]
        many = 1
        for size in sizes:
            many *= size
        if many == 1:
            run({}, ())
            return

        @pl.loop(0, many)
        def _(i):
            where, lead, rest = {}, [], i
            for a, size in reversed(list(zip(free, sizes))):
                where[a] = lax.rem(rest, size)
                rest = rest // size
            run(where, tuple(where[a] for a in free))

    def job(number, layer, order_at):
        order = ORDERS[order_at]
        mine = work.at[number]
        bufs = landing[number]
        rows = pl.ds(order_at * piece, piece)
        near = push(slabs[layer].at[:, :, :, 1 - c, rows], bufs[0], sibling)
        load = pltpu.make_async_copy(slabs[layer].at[:, :, :, c, rows], mine, loads.at[number])
        load.start()
        yield
        load.wait()
        near.wait_recv()
        free = ["z", "y", "x"]

        def join(where, lead):
            at = pick((), where)
            mine[at] = (mine[at].astype(F32) + bufs[0][lead].astype(F32)).astype(BF16)

        each(free, join)
        used = 1
        for position, axis in enumerate(order):
            last = position == 2
            free.remove(axis)
            spot = dict(here)
            if axis == "z":
                first, second, third = bufs[used : used + 3]
                used += 3
                top = first.shape[-2]
                spot["z"] = ring(2)
                head = push(mine.at[pick(free, spot, pl.ds(0, top))], first, up)
                tail = push(mine.at[pick(free, spot, pl.ds(top, piece - top))], second, down)
                yield
                head.wait_recv()
                tail.wait_recv()

                def halves(where, lead):
                    at = pick((), dict(spot, z=ring(1), **where), slice(0, top))
                    mine[at] = (mine[at].astype(F32) + first[lead].astype(F32)).astype(BF16)
                    at = pick((), dict(spot, z=ring(3), **where), slice(top, piece))
                    mine[at] = (mine[at].astype(F32) + second[lead].astype(F32)).astype(BF16)

                each(free, halves)
                head = push(mine.at[pick(free, dict(spot, z=ring(1)))], third.at[0], up)
                tail = push(mine.at[pick(free, dict(spot, z=ring(3)))], third.at[1], down)
                yield
                head.wait_recv()
                tail.wait_recv()

                def gain(lead):
                    return third[(0,) + lead].astype(F32) + third[(1,) + lead].astype(F32)

            else:
                buf = bufs[used]
                used += 1
                spot[axis] = 1 - here[axis]
                only = push(mine.at[pick(free, spot)], buf, peer[axis])
                yield
                only.wait_recv()

                def gain(lead, buf=buf):
                    return buf[lead].astype(F32)

            if last:
                at = pick((), here)
                total[layer, c, rows] = mine[at].astype(F32) + gain(())
            else:

                def add(where, lead):
                    at = pick((), dict(here, **where))
                    mine[at] = (mine[at].astype(F32) + gain(lead)).astype(BF16)

                each(free, add)
        end = push(total.at[layer, c, rows], total.at[layer, c, rows], sibling)
        yield
        end.wait_recv()

    def small_job():
        small[0, 0] = small_in[0][...]
        small[0, 1] = small_in[1][...]
        for step, to in enumerate((sibling, peer["x"], peer["y"])):
            one = push(small.at[2 * step], small.at[2 * step + 1], to)
            yield
            one.wait_recv()
            small[2 * step + 2] = small[2 * step] + small[2 * step + 1]
        around = [push(small.at[6], small.at[7 + i], to) for i, to in enumerate((up, opposite, down))]
        yield
        for one in around:
            one.wait_recv()
        small_out[...] = (small[6] + small[8]) + (small[7] + small[9])

    jobs = {}
    number = 0
    for layer in reversed(range(LAYERS)):
        for order_at in range(4):
            jobs[layer, order_at] = job(number, layer, order_at)
            number += 1
    jobs["small"] = small_job()
    for key in turns:
        next(jobs[key], None)

    out_in, out_out, out_up, out_down = outs
    half = wide
    quarter = half // 2
    sizes, starts = shapes

    for layer in range(LAYERS):
        for which, out in ((0, out_in), (1, out_out), (2, out_up)):
            rows = slice(starts[which], starts[which + 1])
            both = jnp.concatenate([total[layer, 0, rows], total[layer, 1, rows]], axis=0)
            flip[:, 0 : both.shape[0]] = both.T
            out[layer] = flip[pl.ds(pl.multiple_of(quarter * c, 8), quarter), 0 : both.shape[0]]
        part = sizes[1]
        strips = sizes[3] // part // 2
        for e in range(strips):
            rows = pl.ds(pl.multiple_of(starts[3] + part * (strips * c + e), 16), part)
            both = jnp.concatenate([total[layer, 0, rows], total[layer, 1, rows]], axis=0)
            out_down[layer, half * e : half * (e + 1)] = both.T
    for copy in pending:
        copy.wait_send()


def turn_order():
    late, early = 1, 0
    every = [(layer, order) for layer in (late, early) for order in (2, 0, 1, 3)]
    first = [("small")] + every
    second = every + ["small"]
    rest = []
    for layer in (late, early):
        rest += [(layer, 2), (layer, 0), (layer, 1), (layer, 3), "small"]
        rest += [(layer, 2), (layer, 0), (layer, 1), (layer, 3), "small"]
        rest += [(layer, 2), (layer, 0), (layer, 1), (layer, 3)]
    for layer in (late, early):
        for _ in range(4):
            rest += [(layer, 2), (layer, 0), (layer, 1), (layer, 3)]
    return first + second + rest + ["small"] * 3


def reduce_weights(slabs, small, model, hidden, n_seq):
    n_dp = 8
    sizes, starts = slab_rows(model, hidden, n_dp)
    deep, wide = slabs[0].shape[-2:]
    piece = deep // 4
    views = [slab.reshape((4, 2, 2, 2, deep, wide)) for slab in slabs]
    landing = []
    for _ in range(LAYERS):
        for order in ORDERS:
            landing.append([pltpu.VMEM(shape, BF16) for shape in stage_buffers(order, piece, wide)])
    n_copies = LAYERS * 4 * 8 + 6
    rows = model // n_seq
    out_shapes = [
        (LAYERS, rows, 3 * model // n_dp),
        (LAYERS, rows, model // n_dp),
        (LAYERS, rows, hidden // n_dp),
        (LAYERS, hidden // n_seq, model // n_dp),
        (LAYERS,) + small[0].shape,
    ]

    def kernel(slab_0, slab_1, small_0, small_1, o_in, o_out, o_up, o_down, o_small, work, total, small_v, flip, send, recv, loads, *flat):
        flat = list(flat)
        bufs = [[flat.pop(0) for _ in group] for group in landing]
        reduce_kernel(
            (sizes, starts), turn_order(), (slab_0, slab_1), (small_0, small_1),
            (o_in, o_out, o_up, o_down), o_small, work, total, small_v, bufs, send, recv, loads, flip,
        )

    return pl.pallas_call(
        kernel,
        out_shape=[jax.ShapeDtypeStruct(shape, F32) for shape in out_shapes],
        in_specs=[ANY, ANY, VMEM, VMEM],
        out_specs=[VMEM] * 5,
        scratch_shapes=[
            pltpu.VMEM((LAYERS * 4, 4, 2, 2, piece, wide), BF16),
            pltpu.VMEM((LAYERS, 2, deep, wide), F32),
            pltpu.VMEM((10, LAYERS) + small[0].shape, F32),
            pltpu.VMEM((wide, 2 * max(sizes[:3])), F32),
            pltpu.SemaphoreType.DMA((n_copies,)),
            pltpu.SemaphoreType.DMA((n_copies,)),
            pltpu.SemaphoreType.DMA((LAYERS * 4,)),
        ]
        + [shape for group in landing for shape in group],
        compiler_params=pltpu.CompilerParams(
            collective_id=2, has_side_effects=True, vmem_limit_bytes=VMEM_LIMIT
        ),
        name="reduce_weights",
    )(*views, *small)


def reduce_plainly(slabs, small, model, hidden):
    d, s = lax.axis_index("dp"), lax.axis_index("seq")
    n_seq, n_dp = lax.axis_size("seq"), lax.axis_size("dp")
    blocks = slabs[0].shape[0]
    sizes, starts = slab_rows(model, hidden, blocks)
    sums = jnp.stack([lax.psum(slab.astype(F32), ("dp", "seq")) for slab in slabs])
    small_sum = lax.psum(jnp.stack(small), ("dp", "seq"))

    def own(whole):
        rows, cols = whole.shape[1] // n_seq, whole.shape[2] // n_dp
        return lax.dynamic_slice(whole, (0, s * rows, d * cols), (LAYERS, rows, cols))

    outs = []
    for which in range(3):
        part = sums[:, :, :, :, starts[which] : starts[which + 1]]
        outs.append(own(part.transpose(0, 2, 5, 1, 3, 4).reshape(LAYERS, model, -1)))
    part = sums[:, :, :, :, starts[3] :]
    part = part.reshape(part.shape[:4] + (-1, sizes[1], part.shape[-1]))
    outs.append(own(part.transpose(0, 2, 4, 6, 1, 3, 5).reshape(LAYERS, hidden, model)))
    return outs + [small_sum]


def body(
    x_long, x_short, len_long, len_short, w_attn_in, w_attn_out, w_ffn_in, w_ffn_out,
    bias_vec, gain_vec, bias_ffn, cot_long, cot_short,
):
    n_seq = lax.axis_size("seq")
    tl, ts = x_long.shape[1], x_short.shape[1]
    weights = (w_attn_in, w_attn_out, w_ffn_in, w_ffn_out)
    lens = jnp.concatenate([len_long, len_short])
    rows = jnp.concatenate([x_long[0], x_short[0]], axis=0)
    saved = []
    for layer in range(LAYERS):
        h_all = gather_rows(rows, n_seq, 0)
        outs = forward_layer(layer, tl, ts, lens, h_all, rows, weights, bias_vec, gain_vec, bias_ffn)
        saved.append((rows, outs[:-1]))
        rows = outs[-1]
    y_long, y_short = rows[None, :tl], rows[None, tl:]
    grad = jnp.concatenate([cot_long[0], cot_short[0]], axis=0).astype(F32)
    slabs = [None] * LAYERS
    small = [None] * LAYERS
    for layer in reversed(range(LAYERS)):
        rows_in, keep = saved[layer]
        back = backward_layer(layer, tl, ts, lens, grad, keep, weights, gain_vec)
        dkv = scatter_rows(back[5], 1)
        grad, slabs[layer] = weights_layer(layer, 8, rows_in, keep, back, dkv, weights)
        small[layer] = back[6]
    dx_long, dx_short = grad[None, :tl], grad[None, tl:]
    return finish(y_long, y_short, dx_long, dx_short, slabs, small, w_attn_out.shape[1], w_ffn_in.shape[2])


def finish(y_long, y_short, dx_long, dx_short, slabs, small, model, hidden):
    n_seq, n_dp = lax.axis_size("seq"), lax.axis_size("dp")
    if n_dp == 8 and n_seq == 4:
        *sums, tiny = reduce_weights(slabs, small, model, hidden, n_seq)
    else:
        *sums, tiny = reduce_plainly(slabs, small, model, hidden)
    d = lax.axis_index("dp")
    wide = model // n_dp
    vectors = lax.dynamic_slice(tiny, (0, 0, d * wide), (LAYERS, 8, wide))
    bias_up = tiny[:, 8:].reshape(LAYERS, hidden)
    bias_up = lax.dynamic_slice(bias_up, (0, d * (hidden // n_dp)), (LAYERS, hidden // n_dp))
    return (y_long, y_short, dx_long, dx_short, *sums, vectors[:, :6], vectors[:, 6:], bias_up)


def solution(mesh):
    tokens = P("dp", "seq", None)
    matrix = P(None, "seq", "dp")
    vector = P(None, None, "dp")
    return jax.shard_map(
        body,
        mesh=mesh,
        in_specs=(tokens, tokens, P("dp"), P("dp")) + (P(),) * 7 + (tokens, tokens),
        out_specs=(tokens,) * 4 + (matrix,) * 4 + (vector, vector, P(None, "dp")),
        check_vma=False,
    )
```

```python
from functools import partial

import jax
import jax.numpy as jnp
from jax import lax
from jax.experimental import pallas as pl
from jax.experimental.pallas import tpu as pltpu
from jax.sharding import PartitionSpec as P

HD = 64
LAYERS = 2
PAIR = 2 * HD
F32 = jnp.float32
BF16 = jnp.bfloat16
MESH = pl.DeviceIdType.MESH
VMEM_LIMIT = 60 << 20
ANY = pl.BlockSpec(memory_space=pl.ANY)
VMEM = pl.BlockSpec(memory_space=pltpu.VMEM)
SMEM = pl.BlockSpec(memory_space=pltpu.SMEM)


def dot(left, right):
    return jnp.dot(left, right, preferred_element_type=F32)


def dot_t(left, right):
    return lax.dot_general(left, right, (((1,), (1,)), ((), ())), preferred_element_type=F32)


def t_dot(left, right):
    return lax.dot_general(left, right, (((0,), (0,)), ((), ())), preferred_element_type=F32)


def row_mean(values):
    return jnp.mean(values, axis=-1, keepdims=True)


def col_sum(values):
    return jnp.sum(values, axis=0, keepdims=True)


def chunk(i, step, base=0, mult=None):
    return pl.ds(pl.multiple_of(base + i * step, mult or step), step)


def place():
    d, s = lax.axis_index("dp"), lax.axis_index("seq")
    return {"zh": d // 4, "zl": lax.rem(d // 2, 2), "y": lax.rem(d, 2), "x": s // 2, "c": lax.rem(s, 2)}


def peer_devices(at):
    def device(**other):
        p = dict(at, **other)
        return (4 * p["zh"] + 2 * p["zl"] + p["y"], 2 * p["x"] + p["c"])

    return {axis: device(**{axis: 1 - at[axis]}) for axis in ("zh", "zl", "y", "x", "c")}


def greet(peers):
    barrier = pltpu.get_barrier_semaphore()
    for peer in peers:
        pl.semaphore_signal(barrier, inc=1, device_id=peer, device_id_type=MESH)
    pl.semaphore_wait(barrier, len(peers))


def remote(src, dst, send, recv, peer):
    return pltpu.make_async_remote_copy(
        src_ref=src, dst_ref=dst, send_sem=send, recv_sem=recv, device_id=peer, device_id_type=MESH
    )


def low_lanes():
    return lax.broadcasted_iota(jnp.int32, (1, PAIR), 1) < HD


def stacked(rows):
    low = low_lanes()
    masks = (low.astype(F32).astype(BF16), (~low).astype(F32).astype(BF16))
    return jnp.concatenate([rows * mask for mask in masks], axis=0)


def joined(ref, own, lanes):
    return jnp.concatenate([ref[s, own, lanes] for s in range(ref.shape[0])], axis=0)


def softmax_t(keys, query, length):
    place = lax.broadcasted_iota(jnp.int32, (keys.shape[0], 1), 0)
    scores = jnp.where(place < length, dot_t(keys, query), -1e9)
    powers = jnp.exp(scores - jnp.max(scores, axis=0, keepdims=True))
    return powers * (1.0 / jnp.sum(powers, axis=0, keepdims=True))


def attend_pair(query, keys, values, length):
    weights = softmax_t(keys, stacked(query), length).astype(BF16)
    both = t_dot(weights, values)
    count = query.shape[0]
    return jnp.where(low_lanes(), both[:count], both[count:])


def back_pair(query, keys, values, grad, length):
    count = query.shape[0]
    query, grad = stacked(query), stacked(grad)
    probs = softmax_t(keys, query, length)
    grad_probs = dot_t(values, grad)
    inner = col_sum(probs * grad_probs)
    grad_scores = (probs * (grad_probs - inner)).astype(BF16)
    both = t_dot(keys, grad_scores)
    grad_query = jnp.concatenate([both[:HD, :count], both[HD:, count:]], axis=0).T
    return grad_query * HD**-0.5, dot(grad_scores, query), dot(probs.astype(BF16), grad)


def attend(tl, lens, query, keys, values, context):
    rows, width = query.shape
    for p in range(width // PAIR):
        lanes = slice(p * PAIR, (p + 1) * PAIR)
        for which, own in enumerate((slice(0, tl), slice(tl, rows))):
            context[own, lanes] = attend_pair(
                query[own, lanes], joined(keys, own, lanes), joined(values, own, lanes), lens[which]
            ).astype(BF16)


def attend_back(tl, lens, query, keys, values, grad, packed, parts, small, many=2):
    rows, width = query.shape

    @pl.loop(0, width // PAIR // many)
    def _(i):
        for u in range(many):
            lanes = pl.ds(pl.multiple_of((i * many + u) * PAIR, PAIR), PAIR)
            vlanes = pl.ds(pl.multiple_of(width + (i * many + u) * PAIR, PAIR), PAIR)
            sums_q = jnp.zeros((1, PAIR), F32)
            sums_v = jnp.zeros((1, PAIR), F32)
            for which, own in enumerate((slice(0, tl), slice(tl, rows))):
                count = own.stop - own.start
                grad_q, grad_k, grad_v = back_pair(
                    query[own, lanes], joined(keys, own, lanes), joined(values, own, lanes), grad[own, lanes], lens[which]
                )
                grad_q = grad_q.astype(BF16)
                packed[own, lanes] = grad_q
                sums_q += col_sum(grad_q.astype(F32))
                sums_v += col_sum(grad_v)
                grad_k = grad_k.astype(BF16)
                grad_v = grad_v.astype(BF16)
                for s in range(parts.shape[0]):
                    parts[s, own, lanes] = grad_k[count * s : count * (s + 1)]
                    parts[s, own, vlanes] = grad_v[count * s : count * (s + 1)]
            small[0:1, lanes] = sums_q
            small[1:2, lanes] = sums_v


def fill_vec(vec, layer, bias, gain, bias_up):
    width = vec.shape[1]
    vec[0:6, :] = bias[layer].astype(F32)
    vec[6:8, :] = gain[layer].astype(F32)
    for part in range(bias_up.shape[1] // width):
        vec[8 + part : 9 + part, :] = bias_up[layer : layer + 1, part * width : (part + 1) * width].astype(F32)


def project_query(own, w_in, vec, query):
    @pl.loop(0, own.shape[1] // 256)
    def _(i):
        cols = chunk(i, 256)
        out = dot(own[...], w_in[:, cols]) + vec[0:1, cols]
        query[:, cols] = out.astype(BF16) * jnp.asarray(HD**-0.5, BF16)


def project_keys(rows, w_in, vec, keys, values):
    width = rows.shape[1]

    @pl.loop(0, width // 256)
    def _(i):
        cols = chunk(i, 256)
        keys[:, cols] = dot(rows[...], w_in[:, chunk(i, 256, width)]).astype(BF16)
        values[:, cols] = (dot(rows[...], w_in[:, chunk(i, 256, 2 * width)]) + vec[1:2, cols]).astype(BF16)


def normalize(residual, gain_row, shift_row, scaled_o, inverse_o, out):
    centre = residual - row_mean(residual)
    inverse = lax.rsqrt(row_mean(centre * centre) + 1e-12)
    scaled = centre * inverse
    scaled_o[...] = scaled
    inverse_o[...] = jnp.broadcast_to(inverse, inverse_o.shape)
    out[...] = (scaled * gain_row + shift_row).astype(BF16)


def out_norm(own, context, w_out, vec, scaled, inverse, normed):
    residual = own[...].astype(F32) + dot(context[...], w_out[...]) + vec[2:3, :]
    normalize(residual, vec[6:7, :], vec[3:4, :], scaled, inverse, normed)


def ffn_up(normed, w_up, vec, hidden, slope):
    width = normed.shape[1]
    for part in range(w_up.shape[1] // width):

        @pl.loop(0, width // 256)
        def _(i, part=part):
            cols = chunk(i, 256, part * width)
            pre = dot(normed[...], w_up[:, cols]) + vec[8 + part : 9 + part, chunk(i, 256)]
            below, hidden[:, cols] = gelu(pre)
            slope[:, cols] = (below + pre * (jnp.exp(pre * pre * -0.5) * 0.3989422804014327)).astype(BF16)


def gelu(pre):
    below = 0.5 + 0.5 * lax.erf(pre * (2.0**-0.5))
    return below, (pre * below).astype(BF16)


def half_hidden(normed, w_up, vec, x, out):
    width = normed.shape[1]
    for part in range(out.shape[1] // width):
        at = x * (out.shape[1] // width) + part

        @pl.loop(0, width // 256)
        def _(i, part=part, at=at):
            here = pl.ds(pl.multiple_of(at * width + i * 256, 256), 256)
            pre = dot(normed[...], w_up[:, here]) + vec[pl.ds(8 + at, 1), chunk(i, 256)]
            out[:, chunk(i, 256, part * width)] = gelu(pre)[1]


def ffn_down(normed, hidden, w_down, vec, scaled, inverse, out):
    residual = normed[...].astype(F32) + dot(hidden[...], w_down[...]) + vec[4:5, :]
    normalize(residual, vec[7:8, :], vec[5:6, :], scaled, inverse, out)


def norm_back(gradient, scaled, inverse, gain_row):
    inner = gradient * gain_row
    return inverse * (inner - row_mean(inner) - scaled * row_mean(inner * scaled))


def norm_two_back(grad, scaled, inverse, vec, two, feed, small):
    value = grad[...]
    small[5:6, :] = col_sum(value)
    small[7:8, :] = col_sum(value * scaled[...])
    back = norm_back(value, scaled[...], inverse[:, 0:1], vec[7:8, :])
    two[...] = back
    feed[...] = back.astype(BF16)
    small[4:5, :] = col_sum(feed[...].astype(F32))


def ffn_back(feed, w_down, slope, pre, small):
    width = feed.shape[1]
    for part in range(w_down.shape[0] // width):

        @pl.loop(0, width // 256)
        def _(i, part=part):
            cols = chunk(i, 256, part * width)
            back = dot_t(feed[...], w_down[cols, :]) * slope[:, cols].astype(F32)
            pre[:, cols] = back.astype(BF16)
            small[8 + part : 9 + part, chunk(i, 256)] = col_sum(pre[:, cols].astype(F32))


def add_back(total, left, weight):
    @pl.loop(0, total.shape[1] // 256)
    def _(i):
        cols = chunk(i, 256)
        total[:, cols] = total[:, cols] + dot_t(left[...], weight[cols, :])


def norm_one_back(two, scaled, inverse, vec, branch, small):
    value = two[...]
    small[3:4, :] = col_sum(value)
    small[6:7, :] = col_sum(value * scaled[...])
    back = norm_back(value, scaled[...], inverse[:, 0:1], vec[6:7, :])
    two[...] = back
    branch[...] = back.astype(BF16)
    small[2:3, :] = col_sum(branch[...].astype(F32))


def context_back(branch, w_out, grad):
    @pl.loop(0, branch.shape[1] // 256)
    def _(i):
        cols = chunk(i, 256)
        grad[:, cols] = dot_t(branch[...], w_out[cols, :]).astype(BF16)


SAVED = (
    "rows", "query", "keys", "values", "context", "scaled_one", "inverse_one", "normed", "slope", "hidden",
    "scaled_two", "inverse_two",
)
FAR = ("rows_far", "normed_far", "hidden_far")


def saved_shapes(rows, width, hidden, n_seq):
    return {
        "rows": ((rows, width), BF16),
        "query": ((rows, width), BF16),
        "keys": ((n_seq, rows, width), BF16),
        "values": ((n_seq, rows, width), BF16),
        "context": ((rows, width), BF16),
        "scaled_one": ((rows, width), F32),
        "inverse_one": ((rows, 128), F32),
        "normed": ((rows, width), BF16),
        "slope": ((rows, hidden), BF16),
        "hidden": ((rows, hidden), BF16),
        "scaled_two": ((rows, width), F32),
        "inverse_two": ((rows, 128), F32),
        "rows_far": ((rows, width), BF16),
        "normed_far": ((rows, width), BF16),
        "hidden_far": ((rows, hidden // 2), BF16),
    }


def forward_kernel(n_seq, lens, x_long, x_short, *refs):
    refs = list(refs)
    take = lambda count: [refs.pop(0) for _ in range(count)]
    w_hbm = take(4)
    bias, gain, bias_up = take(3)
    y_long, y_short = take(2)
    outs = [dict(zip(SAVED + FAR, take(len(SAVED + FAR)))) for _ in range(LAYERS)]
    w_vmem = [take(4) for _ in range(LAYERS)]
    keep = [dict(zip(SAVED, take(len(SAVED)))) for _ in range(LAYERS)]
    group, last, normed_x, hidden_x, vec, load, store, send, recv = take(9)

    loads = []
    for layer in range(LAYERS):
        for i in range(4):
            loads.append(pltpu.make_async_copy(w_hbm[i].at[layer], w_vmem[layer][i], load.at[layer, i]))
    for copy in loads[:4]:
        copy.start()
    at = place()
    x, c = at["x"], at["c"]
    mine, far = 2 * x + c, 2 * (1 - x) + c
    beside, beyond = 2 * x + 1 - c, 2 * (1 - x) + 1 - c
    peers = peer_devices(at)
    sibling, across = peers["c"], peers["x"]
    tl = x_long.shape[1]
    first = keep[0]["rows"]
    first[0:tl, :] = x_long[0]
    first[tl:, :] = x_short[0]
    greet((sibling, across, peers["y"]))
    rows = first.shape[0]
    halves = (pl.ds(0, rows // 2), pl.ds(rows // 2, rows // 2))
    copies = []
    arrivals = []
    across_normed = []
    stores = []

    def far_hidden(layer):
        across_normed[layer].wait_recv()
        half_hidden(normed_x.at[layer], w_vmem[layer][2], vec.at[layer], x, hidden_x.at[layer])
        stores.append(
            pltpu.make_async_copy(hidden_x.at[layer], outs[layer]["hidden_far"], store.at[layer, len(SAVED) + 1])
        )
        stores[-1].start()

    for layer in range(LAYERS):
        k = keep[layer]
        w_in, w_out, w_up, w_down = w_vmem[layer]
        full = group.at[layer]

        def save(*names, k=k, layer=layer):
            for name in names:
                stores.append(pltpu.make_async_copy(k[name], outs[layer][name], store.at[layer, SAVED.index(name)]))
                stores[-1].start()

        def fly(i, src, dst, to, layer=layer):
            copies.append(remote(src, dst, send.at[layer, i], recv.at[layer, i], to))
            return copies[-1]

        flights = [fly(i, k["rows"].at[part], full.at[mine, part], across) for i, part in enumerate(halves)]
        flights.append(fly(2, k["rows"], full.at[mine], sibling))
        flights += [fly(3 + i, full.at[far, part], full.at[far, part], sibling) for i, part in enumerate(halves)]
        for copy in flights[:3]:
            copy.start()
        if layer == 0:
            for copy in loads[4:]:
                copy.start()
            for i in range(LAYERS):
                fill_vec(vec.at[i], i, bias, gain, bias_up)
        save("rows")
        loads[4 * layer].wait()
        project_query(k["rows"], w_in, vec.at[layer], k["query"])

        def keys_of(source, where, k=k, w_in=w_in, layer=layer):
            project_keys(source, w_in, vec.at[layer], k["keys"].at[where], k["values"].at[where])

        keys_of(k["rows"], mine)
        flights[2].wait_recv()
        keys_of(full.at[beside], beside)
        if layer > 0:
            far_hidden(layer - 1)
        for i in range(2):
            flights[i].wait_recv()
            flights[3 + i].start()
        stores.append(pltpu.make_async_copy(full.at[far], outs[layer]["rows_far"], store.at[layer, len(SAVED)]))
        stores[-1].start()
        keys_of(full.at[far], far)
        flights[3].wait_recv()
        flights[4].wait_recv()
        keys_of(full.at[beyond], beyond)
        save("query", "keys", "values")
        attend(tl, lens, k["query"], k["keys"], k["values"], k["context"])
        save("context")
        loads[4 * layer + 1].wait()
        out_norm(k["rows"], k["context"], w_out, vec.at[layer], k["scaled_one"], k["inverse_one"], k["normed"])
        across_normed.append(fly(6, k["normed"], normed_x.at[layer], across))
        across_normed[-1].start()
        arrivals.append(fly(5, k["normed"], outs[layer]["normed_far"], peers["y"]))
        arrivals[-1].start()
        save("scaled_one", "inverse_one", "normed")
        loads[4 * layer + 2].wait()
        ffn_up(k["normed"], w_up, vec.at[layer], k["hidden"], k["slope"])
        save("hidden", "slope")
        loads[4 * layer + 3].wait()
        after = keep[layer + 1]["rows"] if layer + 1 < LAYERS else last
        ffn_down(k["normed"], k["hidden"], w_down, vec.at[layer], k["scaled_two"], k["inverse_two"], after)
        save("scaled_two", "inverse_two")
    y_long[0] = last[0:tl, :]
    y_short[0] = last[tl:, :]
    far_hidden(LAYERS - 1)
    for copy in arrivals:
        copy.wait_recv()
    for copy in copies:
        copy.wait_send()
    for copy in stores:
        copy.wait()


def forward(lens, x_long, x_short, weights, bias, gain, bias_up, n_seq):
    tl, ts, width = x_long.shape[1], x_short.shape[1], x_long.shape[2]
    rows, hidden = tl + ts, bias_up.shape[1]
    shapes = saved_shapes(rows, width, hidden, n_seq)
    struct = lambda shape, dtype: jax.ShapeDtypeStruct(shape, dtype)
    names = SAVED + FAR
    outs = pl.pallas_call(
        partial(forward_kernel, n_seq),
        out_shape=[struct(x_long.shape, BF16), struct(x_short.shape, BF16)]
        + [struct(*shapes[name]) for name in names] * LAYERS,
        in_specs=[SMEM, VMEM, VMEM] + [ANY] * 4 + [VMEM] * 3,
        out_specs=[VMEM, VMEM] + [ANY] * (len(names) * LAYERS),
        scratch_shapes=[pltpu.VMEM(w.shape[1:], BF16) for w in weights] * LAYERS
        + [pltpu.VMEM(*shapes[name]) for name in SAVED] * LAYERS
        + [
            pltpu.VMEM((LAYERS, n_seq, rows, width), BF16),
            pltpu.VMEM((rows, width), BF16),
            pltpu.VMEM((LAYERS, rows, width), BF16),
            pltpu.VMEM((LAYERS, rows, hidden // 2), BF16),
            pltpu.VMEM((LAYERS, 8 + hidden // width, width), F32),
            pltpu.SemaphoreType.DMA((LAYERS, 4)),
            pltpu.SemaphoreType.DMA((LAYERS, len(SAVED) + 2)),
            pltpu.SemaphoreType.DMA((LAYERS, 7)),
            pltpu.SemaphoreType.DMA((LAYERS, 7)),
        ],
        compiler_params=pltpu.CompilerParams(collective_id=0, has_side_effects=True, vmem_limit_bytes=VMEM_LIMIT),
        name="forward",
    )(lens, x_long, x_short, *weights, bias, gain, bias_up)
    count = len(names)
    return outs[0], outs[1], [dict(zip(names, outs[2 + count * i : 2 + count * (i + 1)])) for i in range(LAYERS)]


DIGITS = ("zh", "zl", "y", "x")
BLOCKS = {"in": DIGITS, "out": DIGITS, "up": ("zh", "zl", "x"), "down": ("zh", "zl", "y")}
JOBS = {
    "down": ("down", None, ("y", "zl", "zh")),
    "out": ("out", None, ("y", "x", "zl", "zh")),
    "up": ("up", None, ("x", "zl", "zh")),
    "in_z": ("in", 0, ("zl", "x", "y", "zh")),
    "in_x": ("in", 1, ("x", "y", "zl", "zh")),
    "in_y": ("in", 2, ("y", "x", "zl", "zh")),
}
LOADED = (
    "scaled_two", "inverse_two", "hidden", "hidden_far", "slope", "scaled_one", "inverse_one", "context", "query",
    "keys", "values", "normed", "normed_far", "rows", "rows_far",
)
ALL = slice(None)


def matrix_rows(width, hidden):
    return {"in": 3 * width // 16, "out": width // 16, "up": hidden // 16, "down": (hidden // width) * (width // 16)}


def job_rows(name, rows):
    matrix, third, _ = JOBS[name]
    count = rows[matrix]
    return (0, count) if third is None else (third * (count // 3), count // 3)


def lead_shape(axes):
    return (2,) * len(axes)


def backward_kernel(width, hidden, tl, names, lens, cot_long, cot_short, *refs):
    refs = list(refs)
    take = lambda count: [refs.pop(0) for _ in range(count)]
    saved = [dict(zip(LOADED, take(len(LOADED)))) for _ in range(LAYERS)]
    w_in, w_out, w_up, w_down = take(4)
    gain = take(1)[0]
    dx_long, dx_short = take(2)
    outs = dict(zip(("in", "out", "up", "down", "small"), take(5)))
    b = dict(zip(names, refs))
    rows_of = matrix_rows(width, hidden)
    half = width // 2

    at = place()
    peers = peer_devices(at)
    c, x = at["c"], at["x"]

    copies = []

    def load(src, dst, sem):
        copy = pltpu.make_async_copy(src, dst, sem)
        copy.start()
        return copy

    parts = hidden // width
    square = lambda i: pl.ds(i * width, width)
    waits = {}

    def load_weights(layer, which):
        pool = b["pool"].at[(layer + 1 + (which == "up")) % 2]
        sems = b["pool_sem"].at[layer, ("down", "up", "rest").index(which)]
        if which == "down":
            tiles = [w_down.at[layer, square(i), :] for i in range(parts)]
        elif which == "up":
            tiles = [w_up.at[layer, :, square(i)] for i in range(parts)]
        else:
            tiles = [w_out.at[layer]] + [w_in.at[layer, :, square(i)] for i in range(3)]
        waits[layer, which] = [load(tile, pool.at[i], sems.at[i]) for i, tile in enumerate(tiles)]
        return pool

    def load_saved(layer, *which):
        for name in which:
            waits[layer, name] = [load(saved[layer][name], b[name], b["saved_sem"].at[layer, LOADED.index(name)])]

    def need(layer, *which):
        for name in which:
            for copy in waits.pop((layer, name), ()):
                copy.wait()

    late, early = LAYERS - 1, 0
    load_saved(late, "scaled_two", "inverse_two")
    pools = {(late, "down"): load_weights(late, "down")}
    load_saved(late, "slope", "hidden", "hidden_far")
    pools[late, "up"] = load_weights(late, "up")
    load_saved(late, *LOADED[5:])
    two, small = b["two"], b["small"]
    two[0:tl, :] = cot_long[0].astype(F32)
    two[tl:, :] = cot_short[0].astype(F32)
    for layer in range(LAYERS):
        b["vec"][layer, 6:8, :] = gain[layer].astype(F32)
    greet([peers[axis] for axis in ("zh", "zl", "y", "x", "c")])

    counter = iter(range(b["send"].shape[0]))
    sent = {}

    def push(src, dst, to):
        i = next(counter)
        copy = remote(src, dst, b["send"].at[i], b["recv"].at[i], peers[to])
        copy.start()
        sent[id(copy)] = copy
        return copy

    def done(copy):
        copy.wait_send()
        del sent[id(copy)]

    def wait_all(flying):
        for copy in flying:
            copy.wait_recv()

    total = b["total"]
    starts = {}
    at_row = 0
    for matrix in ("in", "out", "up", "down"):
        starts[matrix] = at_row
        at_row += rows_of[matrix]

    def job(layer, name):
        matrix, _, order = JOBS[name]
        first, count = job_rows(name, rows_of)
        rows = pl.ds(first, count)
        store = b["grad_" + matrix]
        mine = store.at[1 + layer]
        core = b["core_" + name]
        free = list(BLOCKS[matrix])
        if layer == early:
            pl.semaphore_wait(b["credit"].at[list(JOBS).index(name)], 5)
        near = push(store.at[(0,) + (ALL,) * len(free) + (rows,)], core, "c")
        yield
        near.wait_recv()
        done(near)

        def add(where, landed):
            if len(free) >= 3:
                for i in range(2):
                    index = tuple(where.get(axis, ALL) for axis in BLOCKS[matrix])
                    spot = BLOCKS[matrix].index(free[0])
                    index = index[:spot] + (i,) + index[spot + 1 :]
                    mine[index + (rows,)] = mine[index + (rows,)] + landed[i]
            else:
                index = tuple(where.get(axis, ALL) for axis in BLOCKS[matrix]) + (rows,)
                mine[index] = mine[index] + landed[...]

        add({}, core)
        where = {}
        for step, axis in enumerate(order):
            free.remove(axis)
            landing = b[f"land_{name}_{step}"]
            away = dict(where, **{axis: 1 - at[axis]})
            one = push(mine.at[tuple(away.get(a, ALL) for a in BLOCKS[matrix]) + (rows,)], landing, axis)
            yield
            one.wait_recv()
            done(one)
            where[axis] = at[axis]
            if free:
                add(where, landing)
            else:
                index = tuple(where[a] for a in BLOCKS[matrix]) + (rows,)
                slot = pl.ds(starts[matrix] + first, count)
                total[layer, c, slot] = mine[index].astype(F32) + landing[...].astype(F32)
        end = push(total.at[layer, c, slot], total.at[layer, c, slot], "c")
        if layer == late:
            for to in peers.values():
                pl.semaphore_signal(b["credit"].at[list(JOBS).index(name)], inc=1, device_id=to, device_id_type=MESH)
        yield
        end.wait_recv()
        done(end)

    def small_job():
        sums = b["small_sum"]
        sums[0] = small[...]
        for step, axis in enumerate(("c", "x", "y", "zl", "zh")):
            one = push(sums.at[2 * step], sums.at[2 * step + 1], axis)
            yield
            one.wait_recv()
            done(one)
            sums[2 * step + 2] = sums[2 * step] + sums[2 * step + 1]
        outs["small"][...] = sums[10]

    jobs = {}

    def turn(*keys):
        for key in keys:
            if key not in jobs:
                jobs[key] = small_job() if key == "small" else job(*key)
            next(jobs[key], None)

    def slot(layer, core):
        return (1 - (c - core) * (c - core)) * (1 + layer)

    def digits(block, axes):
        value = {"zh": block // 4, "zl": (block // 2) % 2, "y": block % 2}
        return tuple(value[axis] for axis in axes if axis in value)

    def spread(layer, matrix, out, first_row, block0=0, row0=0, col_half=None):
        piece = rows_of[matrix] if matrix != "down" else rows_of["out"]
        store = b["grad_" + matrix]
        row = 0
        while row < out.shape[0]:
            spot = first_row + row
            count = min(piece - spot % piece, out.shape[0] - row)
            block, core, inside = block0 + spot // (2 * piece), (spot // piece) % 2, row0 + spot % piece
            for side in range(2):
                value = out[row : row + count, half * side : half * (side + 1)].astype(BF16)
                index = (slot(layer, core),) + digits(block, BLOCKS[matrix])
                if matrix == "down":
                    store[index + (pl.ds(inside + side * piece, count),)] = value
                else:
                    store[index + (side, pl.ds(inside, count))] = value
            row += count

    step = 384

    def grad_down(layer):
        for e in range(parts // 2):
            here = chunk(x, width, e * width, 128) if parts == 2 else pl.ds(
                pl.multiple_of(x * (hidden // 2) + e * width, 128), width
            )
            for m in range(width // step):
                cols = slice(m * step, (m + 1) * step)
                out = t_dot(b["feed"][:, cols], b["hidden"][:, here])
                out += t_dot(b["feed_far"][layer, :, cols], b["hidden_far"][:, e * width : (e + 1) * width])
                spread(layer, "down", out, m * step, 0, 2 * e * rows_of["out"])

    def grad_out(layer):
        for m in range(width // step):
            cols = slice(m * step, (m + 1) * step)
            spread(layer, "out", t_dot(b["branch"][:, cols], b["context"][...]), m * step)

    def grad_up(layer):
        for m in range(hidden // 2 // step):
            here = pl.ds(pl.multiple_of((2 * m + at["y"]) * step, 128), step)
            out = t_dot(b["pre"][:, here], b["normed"][...])
            out += t_dot(b["pre_far"][layer, :, m * step : (m + 1) * step], b["normed_far"][...])
            spread(layer, "up", out, 0, 2 * m)

    def grad_in(layer):
        for m in range(3 * width // step):
            if m * step < width:
                out = t_dot(b["packed"][:, m * step : (m + 1) * step], b["rows"][...])
            else:
                cols = slice(m * step - width, (m + 1) * step - width)
                out = t_dot(b["near"][layer, 0, :, cols], b["rows_far"][...])
                out += t_dot(b["near"][layer, 1, :, cols], b["rows"][...])
            spread(layer, "in", out, m * step)

    def backward_layer(layer, during):
        vec, sums = b["vec"].at[layer], small.at[layer]
        feed, pre, branch = b["feed"], b["pre"], b["branch"]
        need(layer, "scaled_two", "inverse_two")
        norm_two_back(two, b["scaled_two"], b["inverse_two"], vec, two, feed, sums)
        feed_sent = push(feed, b["feed_far"].at[layer], "x")
        during(0)
        need(layer, "down", "slope")
        pool = pools[layer, "down"]
        pre_sent = []
        for part in range(parts):

            @pl.loop(0, width // 256)
            def _(i, part=part):
                cols = chunk(i, 256, part * width)
                back = dot_t(feed[...], pool[part, chunk(i, 256), :]) * b["slope"][:, cols].astype(F32)
                pre[:, cols] = back.astype(BF16)
                sums[8 + part : 9 + part, chunk(i, 256)] = col_sum(pre[:, cols].astype(F32))

            other = pl.ds(pl.multiple_of((2 * part + 1 - at["y"]) * step, 128), step)
            pre_sent.append(push(pre.at[:, other], b["pre_far"].at[layer, :, pl.ds(part * step, step)], "y"))
            during(1 + part)
        load_weights(layer, "rest")
        rest = pool
        need(layer, "up")
        pool = pools[layer, "up"]

        @pl.loop(0, width // 256)
        def _(i):
            cols = chunk(i, 256)
            value = two[:, cols]
            for part in range(parts):
                value += dot_t(pre[:, part * width : (part + 1) * width], pool[part, chunk(i, 256), :])
            two[:, cols] = value

        if layer == late:
            pools[early, "down"] = load_weights(early, "down")
        need(layer, "scaled_one", "inverse_one")
        norm_one_back(two, b["scaled_one"], b["inverse_one"], vec, branch, sums)
        need(layer, "rest")
        context_back(branch, rest.at[0], b["grad_context"])
        during(5)
        need(layer, "hidden", "hidden_far")
        feed_sent.wait_recv()
        grad_down(layer)
        turn((layer, "down"))
        need(layer, "context")
        grad_out(layer)
        turn((layer, "out"))
        if layer == late:
            load_saved(early, "scaled_two", "inverse_two", "slope", "hidden", "hidden_far", "scaled_one", "inverse_one", "context")
        during(6)
        need(layer, "query", "keys", "values")
        attend_back(
            tl, lens, b["query"], b["keys"], b["values"], b["grad_context"], b["packed"], b["parts"], sums
        )
        near = b["near"]
        scatter = [
            push(b["parts"].at[2 * (1 - x) + 1 - c], near.at[layer, 0], "c"),
            push(b["parts"].at[2 * x + 1 - c], near.at[layer, 1], "c"),
        ]
        during(7)
        need(layer, "normed", "normed_far")
        wait_all(pre_sent)
        grad_up(layer)
        turn((layer, "up"))
        scatter[0].wait_recv()
        near[layer, 0] = near[layer, 0] + b["parts"][2 * (1 - x) + c]
        far_rows = b["far_send"]
        if layer == early:
            done(far_sent[0])

        @pl.loop(0, width // 256)
        def _(i):
            cols = chunk(i, 256)
            value = dot_t(near[layer, 0, :, 0:width], rest[2, chunk(i, 256), :])
            value += dot_t(near[layer, 0, :, width:], rest[3, chunk(i, 256), :])
            far_rows[:, cols] = value.astype(BF16)

        far = push(far_rows, b["far_recv"].at[layer], "x")
        far_sent.append(far)
        scatter[1].wait_recv()
        near[layer, 1] = near[layer, 1] + b["parts"][2 * x + c]
        for copy in scatter:
            done(copy)
        need(layer, "rows", "rows_far")
        during(8)
        grad_in(layer)
        turn((layer, "in_z"), (layer, "in_x"), (layer, "in_y"))
        during(9)

        @pl.loop(0, width // 256)
        def _(i):
            cols = chunk(i, 256)
            value = two[:, cols] + dot_t(b["packed"][...], rest[1, chunk(i, 256), :])
            value += dot_t(near[layer, 1, :, 0:width], rest[2, chunk(i, 256), :])
            two[:, cols] = value + dot_t(near[layer, 1, :, width:], rest[3, chunk(i, 256), :])

        if layer == late:
            pools[early, "up"] = load_weights(early, "up")
            load_saved(early, "query", "keys", "values", "normed", "normed_far", "rows", "rows_far")
        during(10)
        far.wait_recv()
        two[...] = two[...] + b["far_recv"][layer].astype(F32)
        done(feed_sent)
        for copy in pre_sent:
            done(copy)

    far_sent = []

    def turns(keys):
        for key in keys:
            turn(key if key == "small" else (late if key[0] == "L" else early, key[2:]))

    backward_layer(late, lambda point: turns(POINTS["late"][point]))
    backward_layer(early, lambda point: turns(POINTS["early"][point]))
    dx_long[0] = two[0:tl, :]
    dx_short[0] = two[tl:, :]
    turns(TAIL)
    if any(next(one, jobs) is not jobs for one in jobs.values()):
        raise ValueError("turns left")
    for layer in range(LAYERS):
        finish_layer(layer, c, total, starts, rows_of, b["flip"], outs)
    for copy in list(sent.values()):
        done(copy)


def finish_layer(layer, c, total, starts, rows_of, flip, outs):
    half = total.shape[-1]
    quarter = half // 2
    for matrix in ("in", "out", "up"):
        rows = slice(starts[matrix], starts[matrix] + rows_of[matrix])
        both = jnp.concatenate([total[layer, 0, rows], total[layer, 1, rows]], axis=0)
        flip[:, 0 : both.shape[0]] = both.T
        outs[matrix][layer] = flip[pl.ds(pl.multiple_of(quarter * c, 8), quarter), 0 : both.shape[0]]
    part = rows_of["out"]
    strips = rows_of["down"] // part // 2
    for e in range(strips):
        rows = pl.ds(pl.multiple_of(starts["down"] + part * (strips * c + e), 16), part)
        both = jnp.concatenate([total[layer, 0, rows], total[layer, 1, rows]], axis=0)
        outs["down"][layer, half * e : half * (e + 1)] = both.T


POINTS = {
    "late": (
        (),
        (),
        (),
        (),
        (),
        (),
        (),
        ("L down",),
        (),
        (),
        ("L up", "L in_z", "L out", "L down", "L in_y", "L out", "L in_x",),
    ),
    "early": (
        (),
        ("L down",),
        ("L in_z", "L out",),
        ("L in_x", "L in_y", "L out",),
        ("L up",),
        ("L down", "L out",),
        ("L in_z", "L in_x", "L up", "E down", "L down", "E out", "L in_z", "L in_y",),
        ("L in_x", "L up",),
        ("L in_y", "small", "E down", "E up", "L in_x", "L in_z", "small", "L in_y",),
        ("L in_z", "E in_z", "E down", "E in_y", "E in_z", "E out", "E up", "small", "E in_y",),
        ("E in_x", "E in_z", "small", "E out", "E down", "L in_y", "L in_x", "E in_y", "E in_z", "E up",
            "E out", "E in_x", "L out", "E in_z", "E in_y", "E in_x", "E up", "small", "E up", "E out",
            "E down", "E out", "E down", "E up", "E out", "E in_y", "E down",),
    ),
}
TAIL = ("E in_y", "E up", "E in_x", "E in_x", "L up", "E in_y", "E in_z", "E in_x", "E in_z", "E in_x", "small",)


def backward(lens, cot_long, cot_short, saved, weights, gain, n_seq):
    tl, ts, width = cot_long.shape[1], cot_short.shape[1], cot_long.shape[2]
    rows, hidden = tl + ts, weights[2].shape[2]
    rows_of = matrix_rows(width, hidden)
    half = width // 2
    shapes = saved_shapes(rows, width, hidden, n_seq)
    small = (LAYERS, 8 + hidden // width, width)
    scratch = {name: pltpu.VMEM(*shapes[name]) for name in LOADED}
    scratch.update(
        pool=pltpu.VMEM((2, 4, width, width), BF16),
        two=pltpu.VMEM((rows, width), F32),
        vec=pltpu.VMEM(small, F32),
        small=pltpu.VMEM(small, F32),
        small_sum=pltpu.VMEM((11,) + small, F32),
        feed=pltpu.VMEM((rows, width), BF16),
        feed_far=pltpu.VMEM((LAYERS, rows, width), BF16),
        pre=pltpu.VMEM((rows, hidden), BF16),
        pre_far=pltpu.VMEM((LAYERS, rows, hidden // 2), BF16),
        branch=pltpu.VMEM((rows, width), BF16),
        grad_context=pltpu.VMEM((rows, width), BF16),
        packed=pltpu.VMEM((rows, width), BF16),
        parts=pltpu.VMEM((n_seq, rows, 2 * width), BF16),
        near=pltpu.VMEM((LAYERS, 2, rows, 2 * width), BF16),
        far_send=pltpu.VMEM((rows, width), BF16),
        far_recv=pltpu.VMEM((LAYERS, rows, width), BF16),
        total=pltpu.VMEM((LAYERS, 2, sum(rows_of.values()), half), F32),
        flip=pltpu.VMEM((half, 2 * max(rows_of.values())), F32),
    )
    for matrix, axes in BLOCKS.items():
        scratch["grad_" + matrix] = pltpu.VMEM((1 + LAYERS,) + lead_shape(axes) + (rows_of[matrix], half), BF16)
    copies = 3 + 5
    for name, (matrix, _, order) in JOBS.items():
        count = job_rows(name, rows_of)[1]
        axes = list(BLOCKS[matrix])
        scratch["core_" + name] = pltpu.VMEM(lead_shape(axes) + (count, half), BF16)
        for step, axis in enumerate(order):
            axes.remove(axis)
            scratch[f"land_{name}_{step}"] = pltpu.VMEM(lead_shape(axes) + (count, half), BF16)
        copies += LAYERS * (len(order) + 2)
    copies += LAYERS * (4 + hidden // width)
    scratch.update(
        pool_sem=pltpu.SemaphoreType.DMA((LAYERS, 3, 4)),
        saved_sem=pltpu.SemaphoreType.DMA((LAYERS, len(LOADED))),
        send=pltpu.SemaphoreType.DMA((copies,)),
        recv=pltpu.SemaphoreType.DMA((copies,)),
        credit=pltpu.SemaphoreType.REGULAR((len(JOBS),)),
    )
    struct = lambda shape, dtype=F32: jax.ShapeDtypeStruct(shape, dtype)
    return pl.pallas_call(
        partial(backward_kernel, width, hidden, tl, tuple(scratch)),
        out_shape=[
            struct(cot_long.shape),
            struct(cot_short.shape),
            struct((LAYERS, width // 4, 3 * width // 8)),
            struct((LAYERS, width // 4, width // 8)),
            struct((LAYERS, width // 4, hidden // 8)),
            struct((LAYERS, hidden // 4, width // 8)),
            struct(small),
        ],
        in_specs=[SMEM, VMEM, VMEM] + [ANY] * (len(LOADED) * LAYERS + 4) + [VMEM],
        out_specs=[VMEM] * 7,
        scratch_shapes=list(scratch.values()),
        compiler_params=pltpu.CompilerParams(collective_id=1, has_side_effects=True, vmem_limit_bytes=VMEM_LIMIT),
        name="backward",
    )(lens, cot_long, cot_short, *(saved[i][name] for i in range(LAYERS) for name in LOADED), *weights, gain)


def norm_rows(values, gain_row, shift_row):
    centre = values - jnp.mean(values, axis=-1, keepdims=True)
    spread = jnp.mean(centre * centre, axis=-1, keepdims=True)
    inverse = lax.rsqrt(spread + 1e-12)
    scaled = centre * inverse
    return (scaled * gain_row + shift_row, scaled, inverse)


def plain_norm_back(gradient, scaled, inverse, gain_row):
    inner_sum = gradient * gain_row
    mean_one = jnp.mean(inner_sum, axis=-1, keepdims=True)
    mean_two = jnp.mean(inner_sum * scaled, axis=-1, keepdims=True)
    back = inverse * (inner_sum - mean_one - scaled * mean_two)
    return (back, jnp.sum(gradient * scaled, axis=0), jnp.sum(gradient, axis=0))


def product(left_side, right_side):
    return jnp.dot(left_side, right_side, preferred_element_type=jnp.float32)


def contract_rows(left_side, right_side):
    return lax.dot_general(
        left_side, right_side, (((0,), (0,)), ((), ())), preferred_element_type=jnp.float32
    )


def times_transpose(left_side, right_side):
    return lax.dot_general(
        left_side, right_side, (((1,), (1,)), ((), ())), preferred_element_type=jnp.float32
    )


def head_scores(packed, lengths):
    seq_count, length, _, group_width = packed.shape
    split_heads = packed.reshape(seq_count, length, 3, group_width // HD, HD)
    query_rows = split_heads[:, :, 0]
    key_rows = split_heads[:, :, 1]
    value_rows = split_heads[:, :, 2]
    scores = jnp.einsum(
        "bqhd,bkhd->bhqk", query_rows, key_rows, preferred_element_type=jnp.float32
    ) * HD ** (-0.5)
    places = lax.broadcasted_iota(jnp.int32, (seq_count, length), 1)
    key_valid = (places < lengths[:, None])[:, None, None, :]
    scores = jnp.where(key_valid, scores, -1000000000.0)
    return (scores, query_rows, key_rows, value_rows)


def plain_attend(packed, lengths):
    seq_count, length, _, group_width = packed.shape
    scores, query_rows, key_rows, value_rows = head_scores(packed, lengths)
    log_total = jax.nn.logsumexp(scores, axis=-1, keepdims=True)
    weights = jnp.exp(scores - log_total).astype(jnp.bfloat16)
    context = jnp.einsum("bhqk,bkhd->bqhd", weights, value_rows, preferred_element_type=jnp.float32)
    return (context.astype(jnp.bfloat16).reshape(seq_count, length, group_width), log_total)


def plain_attend_back(packed, lengths, log_total, grad_context):
    seq_count, length, _, group_width = packed.shape
    scores, query_rows, key_rows, value_rows = head_scores(packed, lengths)
    probabilities = jnp.exp(scores - log_total)
    weights = probabilities.astype(jnp.bfloat16)
    grad_heads = grad_context.reshape(seq_count, length, group_width // HD, HD)
    grad_values = jnp.einsum(
        "bhqk,bqhd->bkhd", weights, grad_heads, preferred_element_type=jnp.float32
    )
    grad_probs = jnp.einsum(
        "bqhd,bkhd->bhqk", grad_heads, value_rows, preferred_element_type=jnp.float32
    )
    inner_sum = jnp.sum(probabilities * grad_probs, axis=-1, keepdims=True)
    grad_scores = (probabilities * (grad_probs - inner_sum)).astype(jnp.bfloat16)
    score_scale = HD ** (-0.5)
    grad_query = (
        jnp.einsum("bhqk,bkhd->bqhd", grad_scores, key_rows, preferred_element_type=jnp.float32)
        * score_scale
    )
    grad_keys = (
        jnp.einsum("bhqk,bqhd->bkhd", grad_scores, query_rows, preferred_element_type=jnp.float32)
        * score_scale
    )
    joined = jnp.stack([grad_query, grad_keys, grad_values], axis=2).astype(jnp.bfloat16)
    return joined.reshape(seq_count, length, 3, group_width)


def body(
    x_long,
    x_short,
    len_long,
    len_short,
    w_attn_in,
    w_attn_out,
    w_ffn_in,
    w_ffn_out,
    bias_vec,
    gain_vec,
    bias_ffn,
    cot_long,
    cot_short,
):
    long_shape = x_long.shape
    short_shape = x_short.shape
    count_long = long_shape[0] * long_shape[1]
    model_width = long_shape[2]

    def split_long(token_rows, tail):
        return token_rows[:count_long].reshape((long_shape[0], long_shape[1]) + tail)

    def split_short(token_rows, tail):
        return token_rows[count_long:].reshape((short_shape[0], short_shape[1]) + tail)

    token_rows = jnp.concatenate(
        [x_long.reshape(-1, model_width), x_short.reshape(-1, model_width)], axis=0
    )
    saved = []
    for layer_idx in range(LAYERS):
        biases = bias_vec[layer_idx].astype(jnp.float32)
        gain_rows = gain_vec[layer_idx].astype(jnp.float32)
        packed_bias = jnp.concatenate([biases[0], jnp.zeros_like(biases[0]), biases[1]])
        packed = (product(token_rows, w_attn_in[layer_idx]) + packed_bias).astype(jnp.bfloat16)
        heads_long, heads_short = (
            lax.all_to_all(
                split_long(packed, (3, model_width)), "seq", split_axis=3, concat_axis=1, tiled=True
            ),
            lax.all_to_all(
                split_short(packed, (3, model_width)),
                "seq",
                split_axis=3,
                concat_axis=1,
                tiled=True,
            ),
        )
        context_long, total_long = plain_attend(heads_long, len_long)
        context_short, total_short = plain_attend(heads_short, len_short)
        back_long, back_short = (
            lax.all_to_all(context_long, "seq", split_axis=1, concat_axis=2, tiled=True),
            lax.all_to_all(context_short, "seq", split_axis=1, concat_axis=2, tiled=True),
        )
        context = jnp.concatenate(
            [back_long.reshape(-1, model_width), back_short.reshape(-1, model_width)], axis=0
        )
        branch = product(context, w_attn_out[layer_idx]) + biases[2]
        normed, scaled_one, inverse_one = norm_rows(
            token_rows.astype(jnp.float32) + branch, gain_rows[0], biases[3]
        )
        normed = normed.astype(jnp.bfloat16)
        hidden_pre = product(normed, w_ffn_in[layer_idx]) + bias_ffn[layer_idx].astype(jnp.float32)
        hidden = jax.nn.gelu(hidden_pre, approximate=False).astype(jnp.bfloat16)
        feed_out = product(hidden, w_ffn_out[layer_idx]) + biases[4]
        layer_out, scaled_two, inverse_two = norm_rows(
            normed.astype(jnp.float32) + feed_out, gain_rows[1], biases[5]
        )
        saved.append(
            (
                token_rows,
                heads_long,
                heads_short,
                total_long,
                total_short,
                context,
                scaled_one,
                inverse_one,
                normed,
                hidden_pre,
                hidden,
                scaled_two,
                inverse_two,
            )
        )
        token_rows = layer_out.astype(jnp.bfloat16)
    y_long = token_rows[:count_long].reshape(long_shape)
    y_short = token_rows[count_long:].reshape(short_shape)
    grad_rows = jnp.concatenate(
        [cot_long.reshape(-1, model_width), cot_short.reshape(-1, model_width)], axis=0
    ).astype(jnp.float32)
    layer_grads = [None] * LAYERS
    for layer_idx in reversed(range(LAYERS)):
        (
            rows_in,
            heads_long,
            heads_short,
            total_long,
            total_short,
            context,
            scaled_one,
            inverse_one,
            normed,
            hidden_pre,
            hidden,
            scaled_two,
            inverse_two,
        ) = saved[layer_idx]
        gain_rows = gain_vec[layer_idx].astype(jnp.float32)
        grad_two, grad_gain_two, grad_shift_two = plain_norm_back(
            grad_rows, scaled_two, inverse_two, gain_rows[1]
        )
        grad_feed = grad_two.astype(jnp.bfloat16)
        grad_bias_down = jnp.sum(grad_feed.astype(jnp.float32), axis=0)
        grad_down = contract_rows(hidden, grad_feed)
        grad_hidden = times_transpose(grad_feed, w_ffn_out[layer_idx])
        gelu_value, gelu_back = jax.vjp(partial(jax.nn.gelu, approximate=False), hidden_pre)
        grad_pre = gelu_back(grad_hidden)[0].astype(jnp.bfloat16)
        grad_bias_up = jnp.sum(grad_pre.astype(jnp.float32), axis=0)
        grad_up = contract_rows(normed, grad_pre)
        grad_normed = grad_two + times_transpose(grad_pre, w_ffn_in[layer_idx])
        grad_one, grad_gain_one, grad_shift_one = plain_norm_back(
            grad_normed, scaled_one, inverse_one, gain_rows[0]
        )
        grad_branch = grad_one.astype(jnp.bfloat16)
        grad_bias_out = jnp.sum(grad_branch.astype(jnp.float32), axis=0)
        grad_out = contract_rows(context, grad_branch)
        grad_context = times_transpose(grad_branch, w_attn_out[layer_idx]).astype(jnp.bfloat16)
        grad_heads_long, grad_heads_short = (
            lax.all_to_all(
                split_long(grad_context, (model_width,)),
                "seq",
                split_axis=2,
                concat_axis=1,
                tiled=True,
            ),
            lax.all_to_all(
                split_short(grad_context, (model_width,)),
                "seq",
                split_axis=2,
                concat_axis=1,
                tiled=True,
            ),
        )
        joined_long = plain_attend_back(heads_long, len_long, total_long, grad_heads_long)
        joined_short = plain_attend_back(heads_short, len_short, total_short, grad_heads_short)
        tokens_long, tokens_short = (
            lax.all_to_all(joined_long, "seq", split_axis=1, concat_axis=3, tiled=True),
            lax.all_to_all(joined_short, "seq", split_axis=1, concat_axis=3, tiled=True),
        )
        grad_packed = jnp.concatenate(
            [tokens_long.reshape(-1, 3 * model_width), tokens_short.reshape(-1, 3 * model_width)],
            axis=0,
        )
        packed_sums = jnp.sum(grad_packed.astype(jnp.float32), axis=0)
        grad_in = contract_rows(rows_in, grad_packed)
        grad_rows = grad_one + times_transpose(grad_packed, w_attn_in[layer_idx])
        grad_bias = jnp.stack(
            [
                packed_sums[:model_width],
                packed_sums[2 * model_width :],
                grad_bias_out,
                grad_shift_one,
                grad_bias_down,
                grad_shift_two,
            ]
        )
        grad_gain = jnp.stack([grad_gain_one, grad_gain_two])
        layer_grads[layer_idx] = (
            grad_in,
            grad_out,
            grad_up,
            grad_down,
            grad_bias,
            grad_gain,
            grad_bias_up,
        )
    dx_long = grad_rows[:count_long].reshape(long_shape)
    dx_short = grad_rows[count_long:].reshape(short_shape)
    local_in = jnp.stack([entry[0] for entry in layer_grads])
    local_out = jnp.stack([entry[1] for entry in layer_grads])
    local_up = jnp.stack([entry[2] for entry in layer_grads])
    local_down = jnp.stack([entry[3] for entry in layer_grads])
    local_bias = jnp.stack([entry[4] for entry in layer_grads])
    local_gain = jnp.stack([entry[5] for entry in layer_grads])
    local_ffn = jnp.stack([entry[6] for entry in layer_grads])
    part_in, part_out, part_up, part_down = (local_in, local_out, local_up, local_down)
    sum_in, sum_out, sum_up, sum_down, sum_bias, sum_gain, sum_ffn = (
        lax.psum_scatter(part_in, "dp", scatter_dimension=2, tiled=True),
        lax.psum_scatter(part_out, "dp", scatter_dimension=2, tiled=True),
        lax.psum_scatter(part_up, "dp", scatter_dimension=2, tiled=True),
        lax.psum_scatter(part_down, "dp", scatter_dimension=2, tiled=True),
        lax.psum_scatter(local_bias, "dp", scatter_dimension=2, tiled=True),
        lax.psum_scatter(local_gain, "dp", scatter_dimension=2, tiled=True),
        lax.psum_scatter(local_ffn, "dp", scatter_dimension=1, tiled=True),
    )
    sum_in, sum_out, sum_up, sum_down = (
        lax.psum_scatter(
            sum_in.astype(jnp.bfloat16), "seq", scatter_dimension=1, tiled=True
        ).astype(jnp.float32),
        lax.psum_scatter(
            sum_out.astype(jnp.bfloat16), "seq", scatter_dimension=1, tiled=True
        ).astype(jnp.float32),
        lax.psum_scatter(
            sum_up.astype(jnp.bfloat16), "seq", scatter_dimension=1, tiled=True
        ).astype(jnp.float32),
        lax.psum_scatter(
            sum_down.astype(jnp.bfloat16), "seq", scatter_dimension=1, tiled=True
        ).astype(jnp.float32),
    )
    sum_bias, sum_gain, sum_ffn = lax.psum((sum_bias, sum_gain, sum_ffn), "seq")
    return (
        y_long,
        y_short,
        dx_long,
        dx_short,
        sum_in,
        sum_out,
        sum_up,
        sum_down,
        sum_bias,
        sum_gain,
        sum_ffn,
    )


def fast_body(
    x_long, x_short, len_long, len_short, w_attn_in, w_attn_out, w_ffn_in, w_ffn_out,
    bias_vec, gain_vec, bias_ffn, cot_long, cot_short,
):
    n_seq, n_dp = lax.axis_size("seq"), lax.axis_size("dp")
    weights = (w_attn_in, w_attn_out, w_ffn_in, w_ffn_out)
    lens = jnp.concatenate([len_long, len_short])
    y_long, y_short, saved = forward(lens, x_long, x_short, weights, bias_vec, gain_vec, bias_ffn, n_seq)
    dx_long, dx_short, *sums, tiny = backward(lens, cot_long, cot_short, saved, weights, gain_vec, n_seq)
    model, hidden = w_attn_out.shape[1], w_ffn_in.shape[2]
    d = lax.axis_index("dp")
    wide = model // n_dp
    vectors = lax.dynamic_slice(tiny, (0, 0, d * wide), (LAYERS, 8, wide))
    bias_up = tiny[:, 8:].reshape(LAYERS, hidden)
    bias_up = lax.dynamic_slice(bias_up, (0, d * (hidden // n_dp)), (LAYERS, hidden // n_dp))
    return (y_long, y_short, dx_long, dx_short, *sums, vectors[:, :6], vectors[:, 6:], bias_up)


def solution(mesh):
    tokens = P("dp", "seq", None)
    matrix = P(None, "seq", "dp")
    vector = P(None, None, "dp")
    return jax.shard_map(
        fast_body if mesh.shape["dp"] == 8 and mesh.shape["seq"] == 4 else body,
        mesh=mesh,
        in_specs=(tokens, tokens, P("dp"), P("dp")) + (P(),) * 7 + (tokens, tokens),
        out_specs=(tokens,) * 4 + (matrix,) * 4 + (vector, vector, P(None, "dp")),
        check_vma=False,
    )
```

```python
from functools import partial
from types import SimpleNamespace

import jax
import jax.numpy as jnp
from jax import lax
from jax.experimental import pallas as pl
from jax.experimental.pallas import tpu as pltpu
from jax.sharding import PartitionSpec as P

HD = 64
LAYERS = 2
PAIR = 2 * HD
F32 = jnp.float32
BF16 = jnp.bfloat16
MESH = pl.DeviceIdType.MESH
VMEM_LIMIT = 63 << 20
ANY = pl.BlockSpec(memory_space=pl.ANY)
VMEM = pl.BlockSpec(memory_space=pltpu.VMEM)
SMEM = pl.BlockSpec(memory_space=pltpu.SMEM)


def dot(left, right):
    return jnp.dot(left, right, preferred_element_type=F32)


def dot_t(left, right):
    return lax.dot_general(left, right, (((1,), (1,)), ((), ())), preferred_element_type=F32)


def t_dot(left, right):
    return lax.dot_general(left, right, (((0,), (0,)), ((), ())), preferred_element_type=F32)


def row_mean(values):
    return jnp.mean(values, axis=-1, keepdims=True)


def col_sum(values):
    return jnp.sum(values, axis=0, keepdims=True)


def chunk(i, step, base=0, mult=None):
    return pl.ds(pl.multiple_of(base + i * step, mult or step), step)


ZH, ZL, Y, X, C = range(5)


def place():
    d, s = lax.axis_index("dp"), lax.axis_index("seq")
    return d // 4, lax.rem(d // 2, 2), lax.rem(d, 2), s // 2, lax.rem(s, 2)


def peer_devices(at):
    peers = []
    for digit in range(5):
        zh, zl, y, x, c = (1 - value if i == digit else value for i, value in enumerate(at))
        peers.append((4 * zh + 2 * zl + y, 2 * x + c))
    return peers


def greet(peers):
    barrier = pltpu.get_barrier_semaphore()
    for peer in peers:
        pl.semaphore_signal(barrier, inc=1, device_id=peer, device_id_type=MESH)
    pl.semaphore_wait(barrier, len(peers))


def low_lanes():
    return lax.broadcasted_iota(jnp.int32, (1, PAIR), 1) < HD


def stacked(rows):
    low = low_lanes()
    masks = (low.astype(F32).astype(BF16), (~low).astype(F32).astype(BF16))
    return jnp.concatenate([rows * mask for mask in masks], axis=0)


def joined(ref, own, lanes):
    return jnp.concatenate([ref[s, own, lanes] for s in range(ref.shape[0])], axis=0)


def softmax_t(keys, query, length):
    place = lax.broadcasted_iota(jnp.int32, (keys.shape[0], 1), 0)
    scores = jnp.where(place < length, dot_t(keys, query), -1e9)
    powers = jnp.exp(scores - jnp.max(scores, axis=0, keepdims=True))
    return powers * (1.0 / jnp.sum(powers, axis=0, keepdims=True))


def attend_pair(query, keys, values, length):
    weights = softmax_t(keys, stacked(query), length).astype(BF16)
    both = t_dot(weights, values)
    count = query.shape[0]
    return jnp.where(low_lanes(), both[:count], both[count:])


def back_pair(query, keys, values, grad, length):
    count = query.shape[0]
    query, grad = stacked(query), stacked(grad)
    probs = softmax_t(keys, query, length)
    grad_probs = dot_t(values, grad)
    inner = col_sum(probs * grad_probs)
    grad_scores = (probs * (grad_probs - inner)).astype(BF16)
    both = t_dot(keys, grad_scores)
    grad_query = jnp.concatenate([both[:HD, :count], both[HD:, count:]], axis=0).T
    return grad_query * HD**-0.5, dot(grad_scores, query), dot(probs.astype(BF16), grad)


def attend(tl, lens, query, keys, values, context):
    rows, width = query.shape
    for p in range(width // PAIR):
        lanes = slice(p * PAIR, (p + 1) * PAIR)
        for which, own in enumerate((slice(0, tl), slice(tl, rows))):
            context[own, lanes] = attend_pair(
                query[own, lanes], joined(keys, own, lanes), joined(values, own, lanes), lens[which]
            ).astype(BF16)


def attend_back(tl, lens, query, keys, values, grad, packed, parts, small, many=2):
    rows, width = query.shape

    @pl.loop(0, width // PAIR // many)
    def _(i):
        for u in range(many):
            lanes = pl.ds(pl.multiple_of((i * many + u) * PAIR, PAIR), PAIR)
            vlanes = pl.ds(pl.multiple_of(width + (i * many + u) * PAIR, PAIR), PAIR)
            sums_q = jnp.zeros((1, PAIR), F32)
            sums_v = jnp.zeros((1, PAIR), F32)
            for which, own in enumerate((slice(0, tl), slice(tl, rows))):
                count = own.stop - own.start
                grad_q, grad_k, grad_v = back_pair(
                    query[own, lanes], joined(keys, own, lanes), joined(values, own, lanes), grad[own, lanes], lens[which]
                )
                grad_q = grad_q.astype(BF16)
                packed[own, lanes] = grad_q
                sums_q += col_sum(grad_q.astype(F32))
                sums_v += col_sum(grad_v)
                grad_k = grad_k.astype(BF16)
                grad_v = grad_v.astype(BF16)
                for s in range(parts.shape[0]):
                    parts[s, own, lanes] = grad_k[count * s : count * (s + 1)]
                    parts[s, own, vlanes] = grad_v[count * s : count * (s + 1)]
            small[0:1, lanes] = sums_q
            small[1:2, lanes] = sums_v


def fill_vec(vec, layer, bias, gain, bias_up):
    width = vec.shape[1]
    vec[0:6, :] = bias[:, layer, :].astype(F32)
    vec[6:8, :] = gain[layer].astype(F32)
    for part in range(bias_up.shape[1] // width):
        vec[8 + part : 9 + part, :] = bias_up[layer : layer + 1, part * width : (part + 1) * width].astype(F32)


def project_query(own, tile, vec, query):
    @pl.loop(0, own.shape[1] // 256)
    def _(i):
        cols = chunk(i, 256)
        out = dot(own[...], tile[:, cols]) + vec[0:1, cols]
        query[:, cols] = out.astype(BF16) * jnp.asarray(HD**-0.5, BF16)


def project_keys(rows, key_tile, value_tile, vec, keys, values):
    @pl.loop(0, keys.shape[1] // 256)
    def _(i):
        cols = chunk(i, 256)
        keys[:, cols] = dot(rows[...], key_tile[:, cols]).astype(BF16)
        values[:, cols] = (dot(rows[...], value_tile[:, cols]) + vec[1:2, cols]).astype(BF16)


def normalize(residual, gain_row, shift_row, scaled_o, inverse_o, out):
    centre = residual - row_mean(residual)
    inverse = lax.rsqrt(row_mean(centre * centre) + 1e-12)
    scaled = centre * inverse
    scaled_o[...] = scaled
    inverse_o[...] = jnp.broadcast_to(inverse, inverse_o.shape)
    out[...] = (scaled * gain_row + shift_row).astype(BF16)


def out_norm(own, context, w_out, vec, scaled, inverse, normed):
    residual = own[...].astype(F32) + dot(context[...], w_out[...]) + vec[2:3, :]
    normalize(residual, vec[6:7, :], vec[3:4, :], scaled, inverse, normed)


def gelu(pre):
    below = 0.5 + 0.5 * lax.erf(pre * (2.0**-0.5))
    return below, (pre * below).astype(BF16)


def ffn_up(normed, tiles, vec, hidden, slope):
    width = normed.shape[1]
    for part in range(hidden.shape[1] // width):

        @pl.loop(0, width // 256)
        def _(i, part=part):
            cols = chunk(i, 256, part * width)
            pre = dot(normed[...], tiles[part, :, chunk(i, 256)]) + vec[8 + part : 9 + part, chunk(i, 256)]
            below, hidden[:, cols] = gelu(pre)
            slope[:, cols] = (below + pre * (jnp.exp(pre * pre * -0.5) * 0.3989422804014327)).astype(BF16)


def half_hidden(normed, tiles, vec, x, out):
    width = normed.shape[1]
    for part in range(out.shape[1] // width):
        at = x * (out.shape[1] // width) + part

        @pl.loop(0, width // 256)
        def _(i, part=part, at=at):
            pre = dot(normed[...], tiles[at, :, chunk(i, 256)]) + vec[pl.ds(8 + at, 1), chunk(i, 256)]
            out[:, chunk(i, 256, part * width)] = gelu(pre)[1]


def ffn_down(normed, hidden, tiles, vec, scaled, inverse, out):
    width = normed.shape[1]
    residual = normed[...].astype(F32) + vec[4:5, :]
    for part in range(hidden.shape[1] // width):
        residual += dot(hidden[:, part * width : (part + 1) * width], tiles[part])
    normalize(residual, vec[7:8, :], vec[5:6, :], scaled, inverse, out)


def norm_back(gradient, scaled, inverse, gain_row):
    inner = gradient * gain_row
    return inverse * (inner - row_mean(inner) - scaled * row_mean(inner * scaled))


def norm_two_back(grad, scaled, inverse, vec, two, feed, small):
    value = grad[...]
    small[5:6, :] = col_sum(value)
    small[7:8, :] = col_sum(value * scaled[...])
    back = norm_back(value, scaled[...], inverse[:, 0:1], vec[7:8, :])
    two[...] = back
    feed[...] = back.astype(BF16)
    small[4:5, :] = col_sum(feed[...].astype(F32))


def norm_one_back(two, scaled, inverse, vec, branch, small):
    value = two[...]
    small[3:4, :] = col_sum(value)
    small[6:7, :] = col_sum(value * scaled[...])
    back = norm_back(value, scaled[...], inverse[:, 0:1], vec[6:7, :])
    two[...] = back
    branch[...] = back.astype(BF16)
    small[2:3, :] = col_sum(branch[...].astype(F32))


def context_back(branch, w_out, grad):
    @pl.loop(0, branch.shape[1] // 256)
    def _(i):
        cols = chunk(i, 256)
        grad[:, cols] = dot_t(branch[...], w_out[cols, :]).astype(BF16)


IN, OUT, UP, DOWN = range(4)
BLOCKS = ((ZH, ZL, Y, X), (ZH, ZL, Y, X), (ZH, ZL, X), (ZH, ZL, Y))
JOBS = (
    (DOWN, None, (Y, ZL, ZH)),
    (OUT, None, (Y, X, ZL, ZH)),
    (UP, None, (X, ZL, ZH)),
    (IN, 0, (ZL, X, Y, ZH)),
    (IN, 1, (X, Y, ZL, ZH)),
    (IN, 2, (Y, X, ZL, ZH)),
)
ALL = slice(None)
LATE, EARLY = LAYERS - 1, 0

LATE_POINTS = (
    (),
    (),
    (),
    (),
    (),
    (),
    (),
    (0,),
    (4, 0,),
    (3, 4, 2, 3, 5, 2, 1,),
    (4, 5,),
)
EARLY_POINTS = (
    (1,),
    (0,),
    (3,),
    (),
    (4,),
    (),
    (0, 2,),
    (5, 4, 20, 3, 1, 0, 20,),
    (5, 10, 1, 5, 20, 3, 2, 4, 10,),
    (1, 5, 3, 20, 13, 14, 13,),
    (2, 14, 12, 1, 2, 10, 15, 12, 20, 14, 0, 15, 10, 11, 13, 11, 14, 15, 12, 10, 14, 11, 15, 3,),
)
TAIL = (12, 13, 11, 15, 13, 20, 4, 11, 14, 13, 12, 1, 15, 10, 11, 5, 15, 13, 14, 12, 11,)


def matrix_rows(width, hidden):
    sizes = (3 * width // 16, width // 16, hidden // 16, (hidden // width) * (width // 16))
    return sizes, tuple(sum(sizes[:i]) for i in range(4))


def job_rows(number, sizes):
    matrix, third, _ = JOBS[number]
    count = sizes[matrix]
    return (0, count) if third is None else (third * (count // 3), count // 3)


class Copies:
    def __init__(self, send, recv, peers):
        self.send, self.recv, self.peers = send, recv, peers
        self.count = 0
        self.open = {}

    def make(self, src, dst, to):
        copy = pltpu.make_async_remote_copy(
            src_ref=src,
            dst_ref=dst,
            send_sem=self.send.at[self.count],
            recv_sem=self.recv.at[self.count],
            device_id=self.peers[to],
            device_id_type=MESH,
        )
        self.count += 1
        return copy

    def push(self, src, dst, to):
        copy = self.make(src, dst, to)
        copy.start()
        self.open[id(copy)] = copy
        return copy

    def left(self, *copies):
        for copy in copies or tuple(self.open.values()):
            copy.wait_send()
            del self.open[id(copy)]


def encoder_kernel(tree, counts, *refs):
    r = SimpleNamespace(**jax.tree.unflatten(tree, refs))
    b = SimpleNamespace(**r.scratch)
    w_in, w_out, w_up, w_down = r.weights
    tl = r.x_long.shape[1]
    n_seq, rows, width = b.keys.shape
    hidden = b.hidden.shape[1]
    parts, half = hidden // width, width // 2
    sizes, starts = matrix_rows(width, hidden)
    lens = (r.len_long[0], r.len_short[0])
    at = place()
    x, c = at[X], at[C]
    links = Copies(b.send, b.recv, peer_devices(at))
    push, left = links.push, links.left

    waits = {}

    def start_copy(src, dst, sem):
        copy = pltpu.make_async_copy(src, dst, sem)
        copy.start()
        return copy

    square = lambda i: pl.ds(i * width, width)
    pool_count = iter(range(b.pool_sem.shape[0]))
    DOWN_W, UP_W, REST_W = range(3)

    def load_weights(layer, which, pool):
        if which == DOWN_W:
            tiles = [w_down.at[layer, square(i), :] for i in range(parts)]
        elif which == UP_W:
            tiles = [w_up.at[layer, :, square(i)] for i in range(parts)]
        else:
            tiles = [w_in.at[layer, :, square(i)] for i in range(3)] + [w_out.at[layer]]
        sems = b.pool_sem.at[next(pool_count)]
        waits[pool] = [start_copy(tile, b.pool.at[pool, i], sems.at[i]) for i, tile in enumerate(tiles)]

    def tiles_of(pool):
        for copy in waits.pop(pool, ()):
            copy.wait()
        return b.pool.at[pool]

    kept = {name: (getattr(b, name), ref, i) for i, (name, ref) in enumerate(r.kept.items())}
    storing, loading = {}, {}

    def store(**names):
        for name in names:
            src, dst, i = kept[name]
            storing[name] = start_copy(src, dst, b.store_sem.at[i])

    def stored(**names):
        for name in names:
            storing.pop(name).wait()

    def reload(**names):
        for name in names:
            dst, src, i = kept[name]
            loading[name] = start_copy(src, dst, b.load_sem.at[i])

    def need(**names):
        for name in names:
            if name in loading:
                loading.pop(name).wait()

    load_weights(0, REST_W, 0)
    load_weights(0, UP_W, 1)
    b.rows[0:tl, :] = r.x_long[0]
    b.rows[tl:, :] = r.x_short[0]
    greet(links.peers)

    mine, far = 2 * x + c, 2 * (1 - x) + c
    beside, beyond = 2 * x + 1 - c, 2 * (1 - x) + 1 - c
    halves = (pl.ds(0, rows // 2), pl.ds(rows // 2, rows // 2))
    normed_x_flights = []
    normed_y_flights = []
    gathers = []

    for layer in range(LAYERS):
        vec = b.vec.at[layer]
        lanes = pl.ds(layer * width, width)
        group = b.parts
        flights = [push(b.rows.at[part], group.at[mine, part, lanes], X) for part in halves]
        flights.append(push(b.rows, group.at[mine, :, lanes], C))
        if layer == 0:
            for i in range(LAYERS):
                fill_vec(b.vec.at[i], i, r.bias, r.gain, r.bias_up)
            store(rows=1)
        else:
            normed_x_flights.append(push(b.normed, b.normed_x.at[0], X))
            stored(query=1, keys=1, values=1)
        rest = tiles_of(layer)
        project_query(b.rows, rest.at[0], vec, b.query)

        def keys_of(source, where, rest=rest, vec=vec):
            project_keys(source, rest.at[1], rest.at[2], vec, b.keys.at[where], b.values.at[where])

        keys_of(b.rows, mine)
        flights[2].wait_recv()
        keys_of(group.at[beside, :, lanes], beside)
        passed = []
        for i, part in enumerate(halves):
            flights[i].wait_recv()
            passed.append(push(group.at[far, part, lanes], group.at[far, part, lanes], C))
        if layer == 0:
            far_copy = start_copy(group.at[far, :, lanes], r.kept["rows_far"], b.far_sem.at[0])
        else:
            far_copy = start_copy(group.at[far, :, lanes], b.rows_far, b.far_sem.at[1])
        keys_of(group.at[far, :, lanes], far)
        gathers += passed + (flights if layer else [])
        for copy in passed:
            copy.wait_recv()
        keys_of(group.at[beyond, :, lanes], beyond)
        if layer == 0:
            store(query=1, keys=1, values=1)
        else:
            stored(context=1)
        attend(tl, lens, b.query, b.keys, b.values, b.context)
        if layer == 0:
            store(context=1)
        else:
            stored(scaled_one=1, inverse_one=1, normed=1)
            left(*normed_x_flights, *normed_y_flights)
        out_norm(b.rows, b.context, rest.at[3], vec, b.scaled_one, b.inverse_one, b.normed)
        load_weights(layer, DOWN_W, layer)
        if layer == 0:
            normed_y_flights.append(push(b.normed, r.kept["normed_far"], Y))
            store(scaled_one=1, inverse_one=1, normed=1)
        else:
            normed_x_flights.append(push(b.normed, b.normed_x.at[1], X))
            normed_y_flights.append(push(b.normed, b.normed_far, Y))
            stored(hidden=1, slope=1)
        ffn_up(b.normed, tiles_of(1 - layer), vec, b.hidden, b.slope)
        if layer == 0:
            load_weights(1, REST_W, 1)
            store(hidden=1, slope=1)
            stored(rows=1)
            left(*flights)
        else:
            stored(scaled_two=1, inverse_two=1)
        far_copy.wait()
        after = b.rows if layer == 0 else r.y_rows
        ffn_down(b.normed, b.hidden, tiles_of(layer), vec, b.scaled_two, b.inverse_two, after)
        if layer == 0:
            load_weights(1, UP_W, 0)
            store(scaled_two=1, inverse_two=1)
    left(*gathers)

    two, small = b.two, b.small
    two[0:tl, :] = r.cot_long[0].astype(F32)
    two[tl:, :] = r.cot_short[0].astype(F32)

    step = 384

    def slot(layer, core):
        return (1 - (c - core) * (c - core)) * (1 + layer)

    def spread(layer, matrix, out, first_row, block0=0, row0=0):
        piece = sizes[OUT if matrix == DOWN else matrix]
        row = 0
        while row < out.shape[0]:
            spot = first_row + row
            count = min(piece - spot % piece, out.shape[0] - row)
            block, core, inside = block0 + spot // (2 * piece), (spot // piece) % 2, row0 + spot % piece
            digits = (block // 4, (block // 2) % 2, block % 2)
            index = (slot(layer, core),) + tuple(digits[axis] for axis in BLOCKS[matrix] if axis != X)
            for side in range(2):
                value = out[row : row + count, half * side : half * (side + 1)].astype(BF16)
                if matrix == DOWN:
                    b.grads[matrix][index + (pl.ds(inside + side * piece, count),)] = value
                else:
                    b.grads[matrix][index + (side, pl.ds(inside, count))] = value
            row += count

    sent = [SimpleNamespace(pre=[]) for _ in range(LAYERS)]
    normed_x_flights = [(normed_x_flights[i], i) for i in range(LAYERS)]

    def far_hidden(layer, pool):
        normed_x_flights[layer][0].wait_recv()
        half_hidden(b.normed_x.at[layer], tiles_of(pool), b.vec.at[layer], x, b.hidden_far)

    def grad_down(layer):
        sent[layer].feed.wait_recv()
        need(hidden=1)
        if layer == EARLY:
            far_hidden(layer, 1)
        for e in range(parts // 2):
            here = pl.ds(pl.multiple_of(x * (hidden // 2) + e * width, 128), width)
            for m in range(width // step):
                cols = slice(m * step, (m + 1) * step)
                out = t_dot(b.feed[:, cols], b.hidden[:, here])
                out += t_dot(b.feed_far[layer, :, cols], b.hidden_far[:, e * width : (e + 1) * width])
                spread(layer, DOWN, out, m * step, 0, 2 * e * sizes[OUT])
        if layer == LATE:
            reload(hidden=1)

    def grad_out(layer):
        need(context=1)
        for m in range(width // step):
            cols = slice(m * step, (m + 1) * step)
            spread(layer, OUT, t_dot(b.branch[:, cols], b.context[...]), m * step)
        if layer == LATE:
            reload(context=1)

    def grad_up(layer):
        for copy in sent[layer].pre:
            copy.wait_recv()
        need(normed=1, normed_far=1)
        if layer == LATE:
            normed_y_flights[LATE].wait_recv()
        for m in range(hidden // 2 // step):
            here = pl.ds(pl.multiple_of((2 * m + at[Y]) * step, 128), step)
            out = t_dot(b.pre[:, here], b.normed[...])
            out += t_dot(b.pre_far[layer, :, m * step : (m + 1) * step], b.normed_far[...])
            spread(layer, UP, out, 0, 2 * m)
        if layer == LATE:
            normed_y_flights[EARLY].wait_recv()
            left(normed_y_flights[LATE])
            left(normed_x_flights[LATE][0])
            reload(normed=1, normed_far=1)

    def grad_in(layer):
        need(rows=1, rows_far=1)
        for m in range(3 * width // step):
            if m * step < width:
                out = t_dot(b.packed[:, m * step : (m + 1) * step], b.rows[...])
            else:
                cols = slice(m * step - width, (m + 1) * step - width)
                out = t_dot(b.near[layer, 0, :, cols], b.rows_far[...])
                out += t_dot(b.near[layer, 1, :, cols], b.rows[...])
            spread(layer, IN, out, m * step)
        if layer == LATE:
            reload(rows=1, rows_far=1)

    grad_fns = {IN: grad_in, OUT: grad_out, UP: grad_up, DOWN: grad_down}
    made = set()

    total = r.total

    def job(layer, number):
        matrix, _, order = JOBS[number]
        axes = BLOCKS[matrix]
        first, count = job_rows(number, sizes)
        part = pl.ds(first, count)
        mine_ref = b.grads[matrix].at[1 + layer]
        free = list(axes)
        if (layer, matrix) not in made:
            made.add((layer, matrix))
            grad_fns[matrix](layer)
        if layer == EARLY:
            pl.semaphore_wait(b.credit.at[number], 5)
        near = push(b.grads[matrix].at[(0,) + (ALL,) * len(free) + (part,)], b.core[number], C)
        yield
        near.wait_recv()
        left(near)

        def add(where, landed):
            index = tuple(where.get(axis, ALL) for axis in axes)
            if len(free) >= 3:
                spot = axes.index(free[0])
                for i in range(2):
                    one = index[:spot] + (i,) + index[spot + 1 :] + (part,)
                    mine_ref[one] = mine_ref[one] + landed[i]
            else:
                mine_ref[index + (part,)] = mine_ref[index + (part,)] + landed[...]

        add({}, b.core[number])
        where = {}
        for step_at, axis in enumerate(order):
            free.remove(axis)
            landing = b.land[number][step_at]
            away = {**where, axis: 1 - at[axis]}
            one = push(mine_ref.at[tuple(away.get(a, ALL) for a in axes) + (part,)], landing, axis)
            yield
            one.wait_recv()
            left(one)
            where[axis] = at[axis]
            if free:
                add(where, landing)
            else:
                index = tuple(where[a] for a in axes) + (part,)
                spot = pl.ds(starts[matrix] + first, count)
                total[layer, c, spot] = mine_ref[index].astype(F32) + landing[...].astype(F32)
        end = push(total.at[layer, c, spot], total.at[layer, c, spot], C)
        if layer == LATE:
            for to in links.peers:
                pl.semaphore_signal(b.credit.at[number], inc=1, device_id=to, device_id_type=MESH)
        yield
        end.wait_recv()
        left(end)

    def small_job():
        b.small_sum[0] = small[...]
        for step_at, axis in enumerate((C, X, Y, ZL, ZH)):
            one = push(b.small_sum.at[2 * step_at], b.small_sum.at[2 * step_at + 1], axis)
            yield
            one.wait_recv()
            left(one)
            b.small_sum[2 * step_at + 2] = b.small_sum[2 * step_at] + b.small_sum[2 * step_at + 1]
        r.small_out[...] = b.small_sum[10]

    jobs = {}

    def turns(keys):
        for key in keys:
            if key not in jobs:
                jobs[key] = small_job() if key == 20 else job(EARLY, key - 10) if key >= 10 else job(LATE, key)
            next(jobs[key], None)

    for layer in (LATE, EARLY):
        during = lambda point, lists=(LATE_POINTS if layer == LATE else EARLY_POINTS): turns(lists[point])
        vec, sums = b.vec.at[layer], small.at[layer]
        down_pool = 1 if layer == LATE else 0
        need(scaled_two=1, inverse_two=1)
        norm_two_back(two, b.scaled_two, b.inverse_two, vec, two, b.feed, sums)
        if layer == LATE:
            reload(scaled_two=1, inverse_two=1)
        sent[layer].feed = push(b.feed, b.feed_far.at[layer], X)
        during(0)
        need(slope=1)
        tiles = tiles_of(down_pool)
        for part in range(parts):

            @pl.loop(0, width // 256)
            def _(i, part=part, tiles=tiles, sums=sums):
                cols = chunk(i, 256, part * width)
                back = dot_t(b.feed[...], tiles[part, chunk(i, 256), :]) * b.slope[:, cols].astype(F32)
                b.pre[:, cols] = back.astype(BF16)
                sums[8 + part : 9 + part, chunk(i, 256)] = col_sum(b.pre[:, cols].astype(F32))

            other = pl.ds(pl.multiple_of((2 * part + 1 - at[Y]) * step, 128), step)
            sent[layer].pre.append(push(b.pre.at[:, other], b.pre_far.at[layer, :, pl.ds(part * step, step)], Y))
            during(1 + part)
        load_weights(layer, REST_W, down_pool)
        if layer == LATE:
            reload(slope=1)
            far_hidden(layer, 0)
        tiles = tiles_of(1 - down_pool)

        @pl.loop(0, width // 256)
        def _(i, tiles=tiles):
            cols = chunk(i, 256)
            value = two[:, cols]
            for part in range(parts):
                value += dot_t(b.pre[:, part * width : (part + 1) * width], tiles[part, chunk(i, 256), :])
            two[:, cols] = value

        if layer == LATE:
            load_weights(EARLY, DOWN_W, 0)
        need(scaled_one=1, inverse_one=1)
        norm_one_back(two, b.scaled_one, b.inverse_one, vec, b.branch, sums)
        if layer == LATE:
            reload(scaled_one=1, inverse_one=1)
        rest = tiles_of(down_pool)
        context_back(b.branch, rest.at[3], b.grad_context)
        during(5)
        during(6)
        need(query=1, keys=1, values=1)
        attend_back(tl, lens, b.query, b.keys, b.values, b.grad_context, b.packed, b.parts, sums)
        if layer == LATE:
            reload(query=1, keys=1, values=1)
        near = b.near
        scatter = [push(b.parts.at[beyond], near.at[layer, 0], C), push(b.parts.at[beside], near.at[layer, 1], C)]
        during(7)
        scatter[0].wait_recv()
        near[layer, 0] = near[layer, 0] + b.parts[far]
        if layer == EARLY:
            left(sent[LATE].far)

        @pl.loop(0, width // 256)
        def _(i, layer=layer, rest=rest):
            cols = chunk(i, 256)
            value = dot_t(near[layer, 0, :, 0:width], rest[1, chunk(i, 256), :])
            value += dot_t(near[layer, 0, :, width:], rest[2, chunk(i, 256), :])
            b.far_send[:, cols] = value.astype(BF16)

        sent[layer].far = push(b.far_send, b.far_recv.at[layer], X)
        scatter[1].wait_recv()
        near[layer, 1] = near[layer, 1] + b.parts[mine]
        left(*scatter)
        during(8)

        @pl.loop(0, width // 256)
        def _(i, layer=layer, rest=rest):
            cols = chunk(i, 256)
            value = two[:, cols] + dot_t(b.packed[...], rest[0, chunk(i, 256), :])
            value += dot_t(near[layer, 1, :, 0:width], rest[1, chunk(i, 256), :])
            two[:, cols] = value + dot_t(near[layer, 1, :, width:], rest[2, chunk(i, 256), :])

        if layer == LATE:
            load_weights(EARLY, UP_W, 1)
        during(9)
        during(10)
        sent[layer].far.wait_recv()
        out = two if layer == LATE else r.dx_rows
        out[...] = two[...] + b.far_recv[layer].astype(F32)
        if layer == LATE:
            left(sent[layer].feed, *sent[layer].pre)

    turns(TAIL)
    for one in jobs.values():
        assert next(one, jobs) is jobs
    assert len(jobs) == 2 * len(JOBS) + 1
    left()


def finish_kernel(total_h, small_h, y_h, dx_h, *outs):
    y_long, y_short, dx_long, dx_short, out_in, out_out, out_up, out_down, out_bias, out_gain, out_bias_up = outs[:11]
    total, small, y_rows, dx_rows, flip, sems = outs[11:]
    copies = [
        pltpu.make_async_copy(src, dst, sems.at[i])
        for i, (src, dst) in enumerate(((y_h, y_rows), (dx_h, dx_rows), (small_h, small), (total_h, total)))
    ]
    for copy in copies:
        copy.start()
    for copy in copies:
        copy.wait()
    d, c = lax.axis_index("dp"), lax.rem(lax.axis_index("seq"), 2)
    half, width = total.shape[-1], y_rows.shape[1]
    tl = y_long.shape[1]
    sizes, starts = matrix_rows(width, (small.shape[1] - 8) * width)
    y_long[0], y_short[0] = y_rows[0:tl, :], y_rows[tl:, :]
    dx_long[0], dx_short[0] = dx_rows[0:tl, :], dx_rows[tl:, :]
    quarter = half // 2
    for layer in range(LAYERS):
        for matrix, out in ((IN, out_in), (OUT, out_out), (UP, out_up)):
            part = slice(starts[matrix], starts[matrix] + sizes[matrix])
            both = jnp.concatenate([total[layer, 0, part], total[layer, 1, part]], axis=0)
            flip[:, 0 : both.shape[0]] = both.T
            out[layer] = flip[pl.ds(pl.multiple_of(quarter * c, 8), quarter), 0 : both.shape[0]]
        piece = sizes[OUT]
        strips = width // half
        for core in range(2):
            for e in range(strips):
                part = pl.ds(pl.multiple_of(starts[DOWN] + piece * (strips * c + e), 8), piece)
                out_down[layer, piece * core : piece * (core + 1), half * e : half * (e + 1)] = total[layer, core, part]
        wide = out_bias.shape[2]
        turned = pltpu.roll(small[layer, 0:8, :], lax.rem(width - wide * d, width), 1)
        for i in range(6):
            out_bias[i, layer : layer + 1, :] = turned[i : i + 1, 0:wide]
        out_gain[layer] = turned[6:8, 0:wide]
        wide = out_bias_up.shape[1]
        each = width // wide
        here = pl.ds(pl.multiple_of(wide * lax.rem(d, each), 128), wide)
        out_bias_up[layer : layer + 1, :] = small[layer, pl.ds(8 + d // each, 1), here]


def run_kernels(len_long, len_short, x_long, x_short, cot_long, cot_short, weights, bias, gain, bias_up):
    n_seq, n_dp = lax.axis_size("seq"), lax.axis_size("dp")
    tl, ts, width = x_long.shape[1], x_short.shape[1], x_long.shape[2]
    rows, hidden = tl + ts, bias_up.shape[1]
    sizes, _ = matrix_rows(width, hidden)
    half = width // 2
    sums = (LAYERS, 8 + hidden // width, width)
    two_d, tall = (rows, width), (rows, hidden)
    bf = lambda *shape: pltpu.VMEM(shape, BF16)
    f32 = lambda *shape: pltpu.VMEM(shape, F32)
    group = (n_seq,) + two_d
    kept = dict(
        rows=(two_d, BF16), query=(two_d, BF16), keys=(group, BF16), values=(group, BF16), context=(two_d, BF16),
        scaled_one=(two_d, F32), inverse_one=((rows, 128), F32), normed=(two_d, BF16), slope=(tall, BF16),
        hidden=(tall, BF16), scaled_two=(two_d, F32), inverse_two=((rows, 128), F32), rows_far=(two_d, BF16),
        normed_far=(two_d, BF16),
    )
    core, land = [], []
    copies = LAYERS * 7 + 5 + LAYERS * (4 + hidden // width)
    for number, (matrix, _, order) in enumerate(JOBS):
        count = job_rows(number, sizes)[1]
        free = len(BLOCKS[matrix])
        core.append(bf(*(2,) * free, count, half))
        land.append([bf(*(2,) * (free - 1 - i), count, half) for i in range(len(order))])
        copies += LAYERS * (len(order) + 2)
    scratch = dict(
        pool=bf(2, 4, width, width),
        hidden_far=bf(rows, hidden // 2),
        normed_x=bf(LAYERS, *two_d),
        two=f32(*two_d),
        vec=f32(*sums),
        small=f32(*sums),
        small_sum=f32(11, *sums),
        feed=bf(*two_d),
        feed_far=bf(LAYERS, *two_d),
        pre=bf(*tall),
        pre_far=bf(LAYERS, rows, hidden // 2),
        branch=bf(*two_d),
        grad_context=bf(*two_d),
        packed=bf(*two_d),
        parts=bf(n_seq, rows, 2 * width),
        near=bf(LAYERS, 2, rows, 2 * width),
        far_send=bf(*two_d),
        far_recv=bf(LAYERS, *two_d),
        grads=[bf(1 + LAYERS, *(2,) * len(BLOCKS[m]), sizes[m], half) for m in range(4)],
        core=core,
        land=land,
        pool_sem=pltpu.SemaphoreType.DMA((10, 4)),
        store_sem=pltpu.SemaphoreType.DMA((len(kept),)),
        load_sem=pltpu.SemaphoreType.DMA((len(kept),)),
        far_sem=pltpu.SemaphoreType.DMA((2,)),
        send=pltpu.SemaphoreType.DMA((copies,)),
        recv=pltpu.SemaphoreType.DMA((copies,)),
        credit=pltpu.SemaphoreType.REGULAR((len(JOBS),)),
        **{name: pltpu.VMEM(*shape) for name, shape in kept.items()},
    )
    struct = lambda shape, dtype=F32: jax.ShapeDtypeStruct(shape, dtype)
    ins = dict(
        len_long=len_long, len_short=len_short, x_long=x_long, x_short=x_short, cot_long=cot_long,
        cot_short=cot_short, weights=list(weights), bias=bias, gain=gain, bias_up=bias_up,
    )
    in_specs = dict.fromkeys(ins, VMEM)
    in_specs.update(len_long=SMEM, len_short=SMEM, weights=[ANY] * 4)
    outs = dict(
        y_rows=struct(two_d, BF16),
        dx_rows=struct(two_d),
        total=struct((LAYERS, 2, sum(sizes), half)),
        small_out=struct(sums),
        kept={name: struct(*shape) for name, shape in kept.items()},
    )
    out_specs = dict.fromkeys(outs, VMEM)
    out_specs.update(kept={name: ANY for name in kept})
    trees = [jax.tree.flatten(part) for part in (ins, outs, scratch)]
    index = iter(range(sum(len(leaves) for leaves, _ in trees)))
    numbered = [jax.tree.unflatten(tree, [next(index) for _ in leaves]) for leaves, tree in trees]
    names = {**numbered[0], **numbered[1], **dict(scratch=numbered[2])}
    places, tree = jax.tree.flatten(names)

    def kernel(*refs):
        encoder_kernel(tree, None, *(refs[i] for i in places))

    flat_out = pl.pallas_call(
        kernel,
        out_shape=trees[1][0],
        in_specs=jax.tree.leaves(in_specs),
        out_specs=jax.tree.leaves(out_specs),
        scratch_shapes=trees[2][0],
        compiler_params=pltpu.CompilerParams(collective_id=0, has_side_effects=True, vmem_limit_bytes=VMEM_LIMIT),
        name="encoder",
    )(*trees[0][0])
    made = jax.tree.unflatten(trees[1][1], flat_out)
    finals = [
        struct(x_long.shape, BF16),
        struct(x_short.shape, BF16),
        struct(x_long.shape),
        struct(x_short.shape),
        struct((LAYERS, width // n_seq, 3 * width // n_dp)),
        struct((LAYERS, width // n_seq, width // n_dp)),
        struct((LAYERS, width // n_seq, hidden // n_dp)),
        struct((LAYERS, width // n_dp, hidden // n_seq)),
        struct((6, LAYERS, width // n_dp)),
        struct((LAYERS, 2, width // n_dp)),
        struct((LAYERS, hidden // n_dp)),
    ]
    return pl.pallas_call(
        finish_kernel,
        out_shape=finals,
        in_specs=[ANY] * 4,
        out_specs=[VMEM] * len(finals),
        scratch_shapes=[
            f32(LAYERS, 2, sum(sizes), half),
            f32(*sums),
            bf(*two_d),
            f32(*two_d),
            f32(half, 2 * max(sizes)),
            pltpu.SemaphoreType.DMA((4,)),
        ],
        compiler_params=pltpu.CompilerParams(vmem_limit_bytes=VMEM_LIMIT),
        name="finish",
    )(made["total"], made["small_out"], made["y_rows"], made["dx_rows"])


def norm_rows(values, gain_row, shift_row):
    centre = values - jnp.mean(values, axis=-1, keepdims=True)
    spread = jnp.mean(centre * centre, axis=-1, keepdims=True)
    inverse = lax.rsqrt(spread + 1e-12)
    scaled = centre * inverse
    return (scaled * gain_row + shift_row, scaled, inverse)


def plain_norm_back(gradient, scaled, inverse, gain_row):
    inner_sum = gradient * gain_row
    mean_one = jnp.mean(inner_sum, axis=-1, keepdims=True)
    mean_two = jnp.mean(inner_sum * scaled, axis=-1, keepdims=True)
    back = inverse * (inner_sum - mean_one - scaled * mean_two)
    return (back, jnp.sum(gradient * scaled, axis=0), jnp.sum(gradient, axis=0))


def product(left_side, right_side):
    return jnp.dot(left_side, right_side, preferred_element_type=jnp.float32)


def contract_rows(left_side, right_side):
    return lax.dot_general(
        left_side, right_side, (((0,), (0,)), ((), ())), preferred_element_type=jnp.float32
    )


def times_transpose(left_side, right_side):
    return lax.dot_general(
        left_side, right_side, (((1,), (1,)), ((), ())), preferred_element_type=jnp.float32
    )


def head_scores(packed, lengths):
    seq_count, length, _, group_width = packed.shape
    split_heads = packed.reshape(seq_count, length, 3, group_width // HD, HD)
    query_rows = split_heads[:, :, 0]
    key_rows = split_heads[:, :, 1]
    value_rows = split_heads[:, :, 2]
    scores = jnp.einsum(
        "bqhd,bkhd->bhqk", query_rows, key_rows, preferred_element_type=jnp.float32
    ) * HD ** (-0.5)
    places = lax.broadcasted_iota(jnp.int32, (seq_count, length), 1)
    key_valid = (places < lengths[:, None])[:, None, None, :]
    scores = jnp.where(key_valid, scores, -1000000000.0)
    return (scores, query_rows, key_rows, value_rows)


def plain_attend(packed, lengths):
    seq_count, length, _, group_width = packed.shape
    scores, query_rows, key_rows, value_rows = head_scores(packed, lengths)
    log_total = jax.nn.logsumexp(scores, axis=-1, keepdims=True)
    weights = jnp.exp(scores - log_total).astype(jnp.bfloat16)
    context = jnp.einsum("bhqk,bkhd->bqhd", weights, value_rows, preferred_element_type=jnp.float32)
    return (context.astype(jnp.bfloat16).reshape(seq_count, length, group_width), log_total)


def plain_attend_back(packed, lengths, log_total, grad_context):
    seq_count, length, _, group_width = packed.shape
    scores, query_rows, key_rows, value_rows = head_scores(packed, lengths)
    probabilities = jnp.exp(scores - log_total)
    weights = probabilities.astype(jnp.bfloat16)
    grad_heads = grad_context.reshape(seq_count, length, group_width // HD, HD)
    grad_values = jnp.einsum(
        "bhqk,bqhd->bkhd", weights, grad_heads, preferred_element_type=jnp.float32
    )
    grad_probs = jnp.einsum(
        "bqhd,bkhd->bhqk", grad_heads, value_rows, preferred_element_type=jnp.float32
    )
    inner_sum = jnp.sum(probabilities * grad_probs, axis=-1, keepdims=True)
    grad_scores = (probabilities * (grad_probs - inner_sum)).astype(jnp.bfloat16)
    score_scale = HD ** (-0.5)
    grad_query = (
        jnp.einsum("bhqk,bkhd->bqhd", grad_scores, key_rows, preferred_element_type=jnp.float32)
        * score_scale
    )
    grad_keys = (
        jnp.einsum("bhqk,bqhd->bkhd", grad_scores, query_rows, preferred_element_type=jnp.float32)
        * score_scale
    )
    joined = jnp.stack([grad_query, grad_keys, grad_values], axis=2).astype(jnp.bfloat16)
    return joined.reshape(seq_count, length, 3, group_width)


def body(
    x_long,
    x_short,
    len_long,
    len_short,
    w_attn_in,
    w_attn_out,
    w_ffn_in,
    w_ffn_out,
    bias_vec,
    gain_vec,
    bias_ffn,
    cot_long,
    cot_short,
):
    long_shape = x_long.shape
    short_shape = x_short.shape
    count_long = long_shape[0] * long_shape[1]
    model_width = long_shape[2]

    def split_long(token_rows, tail):
        return token_rows[:count_long].reshape((long_shape[0], long_shape[1]) + tail)

    def split_short(token_rows, tail):
        return token_rows[count_long:].reshape((short_shape[0], short_shape[1]) + tail)

    token_rows = jnp.concatenate(
        [x_long.reshape(-1, model_width), x_short.reshape(-1, model_width)], axis=0
    )
    saved = []
    for layer_idx in range(LAYERS):
        biases = bias_vec[layer_idx].astype(jnp.float32)
        gain_rows = gain_vec[layer_idx].astype(jnp.float32)
        packed_bias = jnp.concatenate([biases[0], jnp.zeros_like(biases[0]), biases[1]])
        packed = (product(token_rows, w_attn_in[layer_idx]) + packed_bias).astype(jnp.bfloat16)
        heads_long, heads_short = (
            lax.all_to_all(
                split_long(packed, (3, model_width)), "seq", split_axis=3, concat_axis=1, tiled=True
            ),
            lax.all_to_all(
                split_short(packed, (3, model_width)),
                "seq",
                split_axis=3,
                concat_axis=1,
                tiled=True,
            ),
        )
        context_long, total_long = plain_attend(heads_long, len_long)
        context_short, total_short = plain_attend(heads_short, len_short)
        back_long, back_short = (
            lax.all_to_all(context_long, "seq", split_axis=1, concat_axis=2, tiled=True),
            lax.all_to_all(context_short, "seq", split_axis=1, concat_axis=2, tiled=True),
        )
        context = jnp.concatenate(
            [back_long.reshape(-1, model_width), back_short.reshape(-1, model_width)], axis=0
        )
        branch = product(context, w_attn_out[layer_idx]) + biases[2]
        normed, scaled_one, inverse_one = norm_rows(
            token_rows.astype(jnp.float32) + branch, gain_rows[0], biases[3]
        )
        normed = normed.astype(jnp.bfloat16)
        hidden_pre = product(normed, w_ffn_in[layer_idx]) + bias_ffn[layer_idx].astype(jnp.float32)
        hidden = jax.nn.gelu(hidden_pre, approximate=False).astype(jnp.bfloat16)
        feed_out = product(hidden, w_ffn_out[layer_idx]) + biases[4]
        layer_out, scaled_two, inverse_two = norm_rows(
            normed.astype(jnp.float32) + feed_out, gain_rows[1], biases[5]
        )
        saved.append(
            (
                token_rows,
                heads_long,
                heads_short,
                total_long,
                total_short,
                context,
                scaled_one,
                inverse_one,
                normed,
                hidden_pre,
                hidden,
                scaled_two,
                inverse_two,
            )
        )
        token_rows = layer_out.astype(jnp.bfloat16)
    y_long = token_rows[:count_long].reshape(long_shape)
    y_short = token_rows[count_long:].reshape(short_shape)
    grad_rows = jnp.concatenate(
        [cot_long.reshape(-1, model_width), cot_short.reshape(-1, model_width)], axis=0
    ).astype(jnp.float32)
    layer_grads = [None] * LAYERS
    for layer_idx in reversed(range(LAYERS)):
        (
            rows_in,
            heads_long,
            heads_short,
            total_long,
            total_short,
            context,
            scaled_one,
            inverse_one,
            normed,
            hidden_pre,
            hidden,
            scaled_two,
            inverse_two,
        ) = saved[layer_idx]
        gain_rows = gain_vec[layer_idx].astype(jnp.float32)
        grad_two, grad_gain_two, grad_shift_two = plain_norm_back(
            grad_rows, scaled_two, inverse_two, gain_rows[1]
        )
        grad_feed = grad_two.astype(jnp.bfloat16)
        grad_bias_down = jnp.sum(grad_feed.astype(jnp.float32), axis=0)
        grad_down = contract_rows(hidden, grad_feed)
        grad_hidden = times_transpose(grad_feed, w_ffn_out[layer_idx])
        gelu_value, gelu_back = jax.vjp(partial(jax.nn.gelu, approximate=False), hidden_pre)
        grad_pre = gelu_back(grad_hidden)[0].astype(jnp.bfloat16)
        grad_bias_up = jnp.sum(grad_pre.astype(jnp.float32), axis=0)
        grad_up = contract_rows(normed, grad_pre)
        grad_normed = grad_two + times_transpose(grad_pre, w_ffn_in[layer_idx])
        grad_one, grad_gain_one, grad_shift_one = plain_norm_back(
            grad_normed, scaled_one, inverse_one, gain_rows[0]
        )
        grad_branch = grad_one.astype(jnp.bfloat16)
        grad_bias_out = jnp.sum(grad_branch.astype(jnp.float32), axis=0)
        grad_out = contract_rows(context, grad_branch)
        grad_context = times_transpose(grad_branch, w_attn_out[layer_idx]).astype(jnp.bfloat16)
        grad_heads_long, grad_heads_short = (
            lax.all_to_all(
                split_long(grad_context, (model_width,)),
                "seq",
                split_axis=2,
                concat_axis=1,
                tiled=True,
            ),
            lax.all_to_all(
                split_short(grad_context, (model_width,)),
                "seq",
                split_axis=2,
                concat_axis=1,
                tiled=True,
            ),
        )
        joined_long = plain_attend_back(heads_long, len_long, total_long, grad_heads_long)
        joined_short = plain_attend_back(heads_short, len_short, total_short, grad_heads_short)
        tokens_long, tokens_short = (
            lax.all_to_all(joined_long, "seq", split_axis=1, concat_axis=3, tiled=True),
            lax.all_to_all(joined_short, "seq", split_axis=1, concat_axis=3, tiled=True),
        )
        grad_packed = jnp.concatenate(
            [tokens_long.reshape(-1, 3 * model_width), tokens_short.reshape(-1, 3 * model_width)],
            axis=0,
        )
        packed_sums = jnp.sum(grad_packed.astype(jnp.float32), axis=0)
        grad_in = contract_rows(rows_in, grad_packed)
        grad_rows = grad_one + times_transpose(grad_packed, w_attn_in[layer_idx])
        grad_bias = jnp.stack(
            [
                packed_sums[:model_width],
                packed_sums[2 * model_width :],
                grad_bias_out,
                grad_shift_one,
                grad_bias_down,
                grad_shift_two,
            ]
        )
        grad_gain = jnp.stack([grad_gain_one, grad_gain_two])
        layer_grads[layer_idx] = (
            grad_in,
            grad_out,
            grad_up,
            grad_down,
            grad_bias,
            grad_gain,
            grad_bias_up,
        )
    dx_long = grad_rows[:count_long].reshape(long_shape)
    dx_short = grad_rows[count_long:].reshape(short_shape)
    local_in = jnp.stack([entry[0] for entry in layer_grads])
    local_out = jnp.stack([entry[1] for entry in layer_grads])
    local_up = jnp.stack([entry[2] for entry in layer_grads])
    local_down = jnp.stack([entry[3] for entry in layer_grads])
    local_bias = jnp.stack([entry[4] for entry in layer_grads])
    local_gain = jnp.stack([entry[5] for entry in layer_grads])
    local_ffn = jnp.stack([entry[6] for entry in layer_grads])
    part_in, part_out, part_up, part_down = (local_in, local_out, local_up, local_down)
    sum_in, sum_out, sum_up, sum_down, sum_bias, sum_gain, sum_ffn = (
        lax.psum_scatter(part_in, "dp", scatter_dimension=2, tiled=True),
        lax.psum_scatter(part_out, "dp", scatter_dimension=2, tiled=True),
        lax.psum_scatter(part_up, "dp", scatter_dimension=2, tiled=True),
        lax.psum_scatter(part_down, "dp", scatter_dimension=2, tiled=True),
        lax.psum_scatter(local_bias, "dp", scatter_dimension=2, tiled=True),
        lax.psum_scatter(local_gain, "dp", scatter_dimension=2, tiled=True),
        lax.psum_scatter(local_ffn, "dp", scatter_dimension=1, tiled=True),
    )
    sum_in, sum_out, sum_up, sum_down = (
        lax.psum_scatter(
            sum_in.astype(jnp.bfloat16), "seq", scatter_dimension=1, tiled=True
        ).astype(jnp.float32),
        lax.psum_scatter(
            sum_out.astype(jnp.bfloat16), "seq", scatter_dimension=1, tiled=True
        ).astype(jnp.float32),
        lax.psum_scatter(
            sum_up.astype(jnp.bfloat16), "seq", scatter_dimension=1, tiled=True
        ).astype(jnp.float32),
        lax.psum_scatter(
            sum_down.astype(jnp.bfloat16), "seq", scatter_dimension=1, tiled=True
        ).astype(jnp.float32),
    )
    sum_bias, sum_gain, sum_ffn = lax.psum((sum_bias, sum_gain, sum_ffn), "seq")
    return (
        y_long,
        y_short,
        dx_long,
        dx_short,
        sum_in,
        sum_out,
        sum_up,
        sum_down,
        sum_bias,
        sum_gain,
        sum_ffn,
    )


def fast_body(
    x_long, x_short, len_long, len_short, w_attn_in, w_attn_out, w_ffn_in, w_ffn_out,
    bias_vec, gain_vec, bias_ffn, cot_long, cot_short,
):
    weights = (w_attn_in, w_attn_out, w_ffn_in, w_ffn_out)
    outs = list(
        run_kernels(
            len_long, len_short, x_long, x_short, cot_long, cot_short, weights,
            bias_vec.transpose(1, 0, 2), gain_vec, bias_ffn,
        )
    )
    outs[7] = outs[7].transpose(0, 2, 1)
    outs[8] = outs[8].transpose(1, 0, 2)
    return tuple(outs)


def solution(mesh):
    tokens = P("dp", "seq", None)
    matrix = P(None, "seq", "dp")
    vector = P(None, None, "dp")
    return jax.shard_map(
        fast_body if mesh.shape["dp"] == 8 and mesh.shape["seq"] == 4 else body,
        mesh=mesh,
        in_specs=(tokens, tokens, P("dp"), P("dp")) + (P(),) * 7 + (tokens, tokens),
        out_specs=(tokens,) * 4 + (matrix,) * 4 + (vector, vector, P(None, "dp")),
        check_vma=False,
    )
```

```python
from functools import partial
from types import SimpleNamespace

import jax
import jax.numpy as jnp
from jax import lax
from jax.experimental import pallas as pl
from jax.experimental.pallas import tpu as pltpu
from jax.sharding import PartitionSpec as P

HD = 64
LAYERS = 2
PAIR = 2 * HD
F32 = jnp.float32
BF16 = jnp.bfloat16
MESH = pl.DeviceIdType.MESH
VMEM_LIMIT = 63 << 20
ANY = pl.BlockSpec(memory_space=pl.ANY)
VMEM = pl.BlockSpec(memory_space=pltpu.VMEM)
SMEM = pl.BlockSpec(memory_space=pltpu.SMEM)


def dot(left, right):
    return jnp.dot(left, right, preferred_element_type=F32)


def dot_t(left, right):
    return lax.dot_general(left, right, (((1,), (1,)), ((), ())), preferred_element_type=F32)


def t_dot(left, right):
    return lax.dot_general(left, right, (((0,), (0,)), ((), ())), preferred_element_type=F32)


def row_mean(values):
    return jnp.mean(values, axis=-1, keepdims=True)


def col_sum(values):
    return jnp.sum(values, axis=0, keepdims=True)


def chunk(i, step, base=0, mult=None):
    return pl.ds(pl.multiple_of(base + i * step, mult or step), step)


ZH, ZL, Y, X, C = range(5)


def place():
    d, s = lax.axis_index("dp"), lax.axis_index("seq")
    return d // 4, lax.rem(d // 2, 2), lax.rem(d, 2), s // 2, lax.rem(s, 2)


def peer_devices(at):
    peers = []
    for digit in range(5):
        zh, zl, y, x, c = (1 - value if i == digit else value for i, value in enumerate(at))
        peers.append((4 * zh + 2 * zl + y, 2 * x + c))
    return peers


def greet(peers):
    barrier = pltpu.get_barrier_semaphore()
    for peer in peers:
        pl.semaphore_signal(barrier, inc=1, device_id=peer, device_id_type=MESH)
    pl.semaphore_wait(barrier, len(peers))


def low_lanes():
    return lax.broadcasted_iota(jnp.int32, (1, PAIR), 1) < HD


def stacked(rows):
    low = low_lanes()
    masks = (low.astype(F32).astype(BF16), (~low).astype(F32).astype(BF16))
    return jnp.concatenate([rows * mask for mask in masks], axis=0)


def joined(ref, own, lanes):
    return jnp.concatenate([ref[s, own, lanes] for s in range(ref.shape[0])], axis=0)


def softmax_t(keys, query, length):
    place = lax.broadcasted_iota(jnp.int32, (keys.shape[0], 1), 0)
    scores = jnp.where(place < length, dot_t(keys, query), -1e9)
    powers = jnp.exp(scores - jnp.max(scores, axis=0, keepdims=True))
    return powers * (1.0 / jnp.sum(powers, axis=0, keepdims=True))


def attend_pair(query, keys, values, length):
    weights = softmax_t(keys, stacked(query), length).astype(BF16)
    both = t_dot(weights, values)
    count = query.shape[0]
    return jnp.where(low_lanes(), both[:count], both[count:])


def back_pair(query, keys, values, grad, length):
    count = query.shape[0]
    query, grad = stacked(query), stacked(grad)
    probs = softmax_t(keys, query, length)
    grad_probs = dot_t(values, grad)
    inner = col_sum(probs * grad_probs)
    grad_scores = (probs * (grad_probs - inner)).astype(BF16)
    both = t_dot(keys, grad_scores)
    grad_query = jnp.concatenate([both[:HD, :count], both[HD:, count:]], axis=0).T
    return grad_query * HD**-0.5, dot(grad_scores, query), dot(probs.astype(BF16), grad)


def attend(tl, lens, query, keys, values, context):
    rows, width = query.shape
    for p in range(width // PAIR):
        lanes = slice(p * PAIR, (p + 1) * PAIR)
        for which, own in enumerate((slice(0, tl), slice(tl, rows))):
            context[own, lanes] = attend_pair(
                query[own, lanes], joined(keys, own, lanes), joined(values, own, lanes), lens[which]
            ).astype(BF16)


def attend_back(tl, lens, query, keys, values, grad, packed, parts, small, many=2):
    rows, width = query.shape

    @pl.loop(0, width // PAIR // many)
    def _(i):
        for u in range(many):
            lanes = pl.ds(pl.multiple_of((i * many + u) * PAIR, PAIR), PAIR)
            vlanes = pl.ds(pl.multiple_of(width + (i * many + u) * PAIR, PAIR), PAIR)
            sums_q = jnp.zeros((1, PAIR), F32)
            sums_v = jnp.zeros((1, PAIR), F32)
            for which, own in enumerate((slice(0, tl), slice(tl, rows))):
                count = own.stop - own.start
                grad_q, grad_k, grad_v = back_pair(
                    query[own, lanes], joined(keys, own, lanes), joined(values, own, lanes), grad[own, lanes], lens[which]
                )
                grad_q = grad_q.astype(BF16)
                packed[own, lanes] = grad_q
                sums_q += col_sum(grad_q.astype(F32))
                sums_v += col_sum(grad_v)
                grad_k = grad_k.astype(BF16)
                grad_v = grad_v.astype(BF16)
                for s in range(parts.shape[0]):
                    parts[s, own, lanes] = grad_k[count * s : count * (s + 1)]
                    parts[s, own, vlanes] = grad_v[count * s : count * (s + 1)]
            small[0:1, lanes] = sums_q
            small[1:2, lanes] = sums_v


def fill_vec(vec, layer, bias, gain, bias_up):
    width = vec.shape[1]
    vec[0:6, :] = bias[:, layer, :].astype(F32)
    vec[6:8, :] = gain[layer].astype(F32)
    for part in range(bias_up.shape[1] // width):
        vec[8 + part : 9 + part, :] = bias_up[layer : layer + 1, part * width : (part + 1) * width].astype(F32)


def project_query(own, tile, vec, query):
    @pl.loop(0, own.shape[1] // 256)
    def _(i):
        cols = chunk(i, 256)
        out = dot(own[...], tile[:, cols]) + vec[0:1, cols]
        query[:, cols] = out.astype(BF16) * jnp.asarray(HD**-0.5, BF16)


def project_keys(rows, key_tile, value_tile, vec, keys, values):
    @pl.loop(0, keys.shape[1] // 256)
    def _(i):
        cols = chunk(i, 256)
        keys[:, cols] = dot(rows[...], key_tile[:, cols]).astype(BF16)
        values[:, cols] = (dot(rows[...], value_tile[:, cols]) + vec[1:2, cols]).astype(BF16)


def normalize(residual, gain_row, shift_row, scaled_o, inverse_o, out):
    centre = residual - row_mean(residual)
    inverse = lax.rsqrt(row_mean(centre * centre) + 1e-12)
    scaled = centre * inverse
    scaled_o[...] = scaled
    inverse_o[...] = jnp.broadcast_to(inverse, inverse_o.shape)
    out[...] = (scaled * gain_row + shift_row).astype(BF16)


def out_norm(own, context, w_out, vec, scaled, inverse, normed):
    residual = own[...].astype(F32) + dot(context[...], w_out[...]) + vec[2:3, :]
    normalize(residual, vec[6:7, :], vec[3:4, :], scaled, inverse, normed)


def gelu(pre):
    below = 0.5 + 0.5 * lax.erf(pre * (2.0**-0.5))
    return below, (pre * below).astype(BF16)


def ffn_up(normed, tiles, vec, hidden, slope):
    width = normed.shape[1]
    for part in range(hidden.shape[1] // width):

        @pl.loop(0, width // 256)
        def _(i, part=part):
            cols = chunk(i, 256, part * width)
            pre = dot(normed[...], tiles[part, :, chunk(i, 256)]) + vec[8 + part : 9 + part, chunk(i, 256)]
            below, hidden[:, cols] = gelu(pre)
            slope[:, cols] = (below + pre * (jnp.exp(pre * pre * -0.5) * 0.3989422804014327)).astype(BF16)


def half_hidden(normed, tiles, vec, x, out):
    width = normed.shape[1]
    for part in range(out.shape[1] // width):
        at = x * (out.shape[1] // width) + part

        @pl.loop(0, width // 256)
        def _(i, part=part, at=at):
            pre = dot(normed[...], tiles[at, :, chunk(i, 256)]) + vec[pl.ds(8 + at, 1), chunk(i, 256)]
            out[:, chunk(i, 256, part * width)] = gelu(pre)[1]


def ffn_down(normed, hidden, tiles, vec, scaled, inverse, out):
    width = normed.shape[1]
    residual = normed[...].astype(F32) + vec[4:5, :]
    for part in range(hidden.shape[1] // width):
        residual += dot(hidden[:, part * width : (part + 1) * width], tiles[part])
    normalize(residual, vec[7:8, :], vec[5:6, :], scaled, inverse, out)


def norm_back(gradient, scaled, inverse, gain_row):
    inner = gradient * gain_row
    return inverse * (inner - row_mean(inner) - scaled * row_mean(inner * scaled))


def norm_two_back(grad, scaled, inverse, vec, two, feed, small):
    value = grad[...]
    small[5:6, :] = col_sum(value)
    small[7:8, :] = col_sum(value * scaled[...])
    back = norm_back(value, scaled[...], inverse[:, 0:1], vec[7:8, :])
    two[...] = back
    feed[...] = back.astype(BF16)
    small[4:5, :] = col_sum(feed[...].astype(F32))


def norm_one_back(two, scaled, inverse, vec, branch, small):
    value = two[...]
    small[3:4, :] = col_sum(value)
    small[6:7, :] = col_sum(value * scaled[...])
    back = norm_back(value, scaled[...], inverse[:, 0:1], vec[6:7, :])
    two[...] = back
    branch[...] = back.astype(BF16)
    small[2:3, :] = col_sum(branch[...].astype(F32))


def context_back(branch, w_out, grad):
    @pl.loop(0, branch.shape[1] // 256)
    def _(i):
        cols = chunk(i, 256)
        grad[:, cols] = dot_t(branch[...], w_out[cols, :]).astype(BF16)


IN, OUT, UP, DOWN = range(4)
BLOCKS = ((ZH, ZL, Y, X), (ZH, ZL, Y, X), (ZH, ZL, X), (ZH, ZL, Y))
JOBS = ((DOWN, 0, 2), (OUT, 0, 1), (UP, 0, 2), (IN, 0, 3), (IN, 1, 3), (IN, 2, 3), (DOWN, 1, 2), (UP, 1, 2))
ALL = slice(None)
LATE, EARLY = LAYERS - 1, 0

ORDERS = (
    ((Y, ZH, ZL), (ZL, X, Y, ZH), (X, ZH, ZL), (Y, X, ZH, ZL), (Y, X, ZL, ZH), (X, Y, ZL, ZH), (ZL, Y, ZH), (X, ZL, ZH)),
    ((Y, ZL, ZH), (X, Y, ZL, ZH), (X, ZL, ZH), (Y, ZL, X, ZH), (X, ZH, ZL, Y), (Y, ZL, ZH, X), (ZL, Y, ZH), (ZL, X, ZH)),
)
LATE_POINTS = (
    (),
    (),
    (),
    (),
    (),
    (),
    (),
    (0, 6,),
    (3, 4, 0, 6, 7, 4,),
    (),
    (7, 2, 5, 3, 2, 6, 1,),
)
EARLY_POINTS = (
    (5, 0,),
    (),
    (4,),
    (),
    (),
    (),
    (3, 7, 2, 6, 0, 1,),
    (5, 2, 3, 7, 4, 20, 20,),
    (0,),
    (1, 5, 6, 16, 20, 4, 10, 7, 6, 2, 3, 1, 17, 20, 7, 2, 5, 12,),
    (10, 1, 3, 16, 17, 4, 5, 13, 12, 20, 1, 11, 13, 14, 15, 11, 4,),
)
TAIL = (17, 3, 16, 14, 15, 10, 20, 13, 12, 0, 11, 17, 15, 13, 14, 15, 16, 11, 14, 15, 11, 10, 13, 17, 5, 14, 17, 12,
        15, 13, 11, 16, 10, 16, 14, 11, 12, 14, 10, 15, 12, 1, 13,)


def matrix_rows(width, hidden):
    sizes = (3 * width // 16, width // 16, hidden // 16, (hidden // width) * (width // 16))
    return sizes, tuple(sum(sizes[:i]) for i in range(4))


def job_rows(number, sizes):
    matrix, part, parts = JOBS[number]
    count = sizes[matrix] // parts
    return part * count, count


class Copies:
    def __init__(self, send, recv, peers):
        self.send, self.recv, self.peers = send, recv, peers
        self.count = 0
        self.open = {}

    def make(self, src, dst, to):
        copy = pltpu.make_async_remote_copy(
            src_ref=src,
            dst_ref=dst,
            send_sem=self.send.at[self.count],
            recv_sem=self.recv.at[self.count],
            device_id=self.peers[to],
            device_id_type=MESH,
        )
        self.count += 1
        return copy

    def push(self, src, dst, to):
        copy = self.make(src, dst, to)
        copy.start()
        self.open[id(copy)] = copy
        return copy

    def left(self, *copies):
        for copy in copies or tuple(self.open.values()):
            copy.wait_send()
            del self.open[id(copy)]


def encoder_kernel(tree, counts, *refs):
    r = SimpleNamespace(**jax.tree.unflatten(tree, refs))
    b = SimpleNamespace(**r.scratch)
    w_in, w_out, w_up, w_down = r.weights
    tl = r.x_long.shape[1]
    n_seq, rows, width = b.keys.shape
    hidden = b.hidden.shape[1]
    parts, half = hidden // width, width // 2
    sizes, starts = matrix_rows(width, hidden)
    lens = (r.len_long[0], r.len_short[0])
    at = place()
    x, c = at[X], at[C]
    links = Copies(b.send, b.recv, peer_devices(at))
    push, left = links.push, links.left

    waits = {}

    def start_copy(src, dst, sem):
        copy = pltpu.make_async_copy(src, dst, sem)
        copy.start()
        return copy

    square = lambda i: pl.ds(i * width, width)
    pool_count = iter(range(b.pool_sem.shape[0]))
    DOWN_W, UP_W, REST_W = range(3)

    def load_weights(layer, which, pool):
        if which == DOWN_W:
            tiles = [w_down.at[layer, square(i), :] for i in range(parts)]
        elif which == UP_W:
            tiles = [w_up.at[layer, :, square(i)] for i in range(parts)]
        else:
            tiles = [w_in.at[layer, :, square(i)] for i in range(3)] + [w_out.at[layer]]
        sems = b.pool_sem.at[next(pool_count)]
        waits[pool] = [start_copy(tile, b.pool.at[pool, i], sems.at[i]) for i, tile in enumerate(tiles)]

    def tiles_of(pool):
        for copy in waits.pop(pool, ()):
            copy.wait()
        return b.pool.at[pool]

    kept = {name: (getattr(b, name), ref, i) for i, (name, ref) in enumerate(r.kept.items())}
    storing, loading = {}, {}

    def store(**names):
        for name in names:
            src, dst, i = kept[name]
            storing[name] = start_copy(src, dst, b.store_sem.at[i])

    def stored(**names):
        for name in names:
            storing.pop(name).wait()

    def reload(**names):
        for name in names:
            dst, src, i = kept[name]
            loading[name] = start_copy(src, dst, b.load_sem.at[i])

    def need(**names):
        for name in names:
            if name in loading:
                loading.pop(name).wait()

    load_weights(0, REST_W, 0)
    load_weights(0, UP_W, 1)
    b.rows[0:tl, :] = r.x_long[0]
    b.rows[tl:, :] = r.x_short[0]
    greet(links.peers)

    mine, far = 2 * x + c, 2 * (1 - x) + c
    beside, beyond = 2 * x + 1 - c, 2 * (1 - x) + 1 - c
    halves = (pl.ds(0, rows // 2), pl.ds(rows // 2, rows // 2))
    normed_x_flights = []
    normed_y_flights = []
    gathers = []

    for layer in range(LAYERS):
        vec = b.vec.at[layer]
        lanes = pl.ds(layer * width, width)
        group = b.parts
        flights = [push(b.rows.at[part], group.at[mine, part, lanes], X) for part in halves]
        flights.append(push(b.rows, group.at[mine, :, lanes], C))
        if layer == 0:
            for i in range(LAYERS):
                fill_vec(b.vec.at[i], i, r.bias, r.gain, r.bias_up)
            store(rows=1)
        else:
            normed_x_flights.append(push(b.normed, b.normed_x.at[0], X))
            stored(query=1, keys=1, values=1)
        rest = tiles_of(layer)
        project_query(b.rows, rest.at[0], vec, b.query)

        def keys_of(source, where, rest=rest, vec=vec):
            project_keys(source, rest.at[1], rest.at[2], vec, b.keys.at[where], b.values.at[where])

        keys_of(b.rows, mine)
        flights[2].wait_recv()
        keys_of(group.at[beside, :, lanes], beside)
        passed = []
        for i, part in enumerate(halves):
            flights[i].wait_recv()
            passed.append(push(group.at[far, part, lanes], group.at[far, part, lanes], C))
        if layer == 0:
            far_copy = start_copy(group.at[far, :, lanes], r.kept["rows_far"], b.far_sem.at[0])
        else:
            far_copy = start_copy(group.at[far, :, lanes], b.rows_far, b.far_sem.at[1])
        keys_of(group.at[far, :, lanes], far)
        gathers += passed + (flights if layer else [])
        for copy in passed:
            copy.wait_recv()
        keys_of(group.at[beyond, :, lanes], beyond)
        if layer == 0:
            store(query=1, keys=1, values=1)
        else:
            stored(context=1)
        attend(tl, lens, b.query, b.keys, b.values, b.context)
        if layer == 0:
            store(context=1)
        else:
            stored(scaled_one=1, inverse_one=1, normed=1)
            left(*normed_x_flights, *normed_y_flights)
        out_norm(b.rows, b.context, rest.at[3], vec, b.scaled_one, b.inverse_one, b.normed)
        load_weights(layer, DOWN_W, layer)
        if layer == 0:
            normed_y_flights.append(push(b.normed, r.kept["normed_far"], Y))
            store(scaled_one=1, inverse_one=1, normed=1)
        else:
            normed_x_flights.append(push(b.normed, b.normed_x.at[1], X))
            normed_y_flights.append(push(b.normed, b.normed_far, Y))
            stored(hidden=1, slope=1)
        ffn_up(b.normed, tiles_of(1 - layer), vec, b.hidden, b.slope)
        if layer == 0:
            load_weights(1, REST_W, 1)
            store(hidden=1, slope=1)
            stored(rows=1)
            left(*flights)
        else:
            stored(scaled_two=1, inverse_two=1)
        far_copy.wait()
        after = b.rows if layer == 0 else r.y_rows
        ffn_down(b.normed, b.hidden, tiles_of(layer), vec, b.scaled_two, b.inverse_two, after)
        if layer == 0:
            load_weights(1, UP_W, 0)
            store(scaled_two=1, inverse_two=1)
    left(*gathers)

    two, small = b.two, b.small
    two[0:tl, :] = r.cot_long[0].astype(F32)
    two[tl:, :] = r.cot_short[0].astype(F32)

    step = 384

    def slot(layer, core):
        return (1 - (c - core) * (c - core)) * (1 + layer)

    def spread(layer, matrix, out, first_row, block0=0, row0=0):
        piece = sizes[OUT if matrix == DOWN else matrix]
        row = 0
        while row < out.shape[0]:
            spot = first_row + row
            count = min(piece - spot % piece, out.shape[0] - row)
            block, core, inside = block0 + spot // (2 * piece), (spot // piece) % 2, row0 + spot % piece
            digits = (block // 4, (block // 2) % 2, block % 2)
            index = (slot(layer, core),) + tuple(digits[axis] for axis in BLOCKS[matrix] if axis != X)
            for side in range(2):
                value = out[row : row + count, half * side : half * (side + 1)].astype(BF16)
                if matrix == DOWN:
                    b.grads[matrix][index + (pl.ds(inside + side * piece, count),)] = value
                else:
                    b.grads[matrix][index + (side, pl.ds(inside, count))] = value
            row += count

    sent = [SimpleNamespace(pre=[]) for _ in range(LAYERS)]
    normed_x_flights = [(normed_x_flights[i], i) for i in range(LAYERS)]

    def far_hidden(layer, pool):
        normed_x_flights[layer][0].wait_recv()
        half_hidden(b.normed_x.at[layer], tiles_of(pool), b.vec.at[layer], x, b.hidden_far)

    def grad_down(layer):
        sent[layer].feed.wait_recv()
        need(hidden=1)
        if layer == EARLY:
            far_hidden(layer, 1)
        for e in range(parts // 2):
            here = pl.ds(pl.multiple_of(x * (hidden // 2) + e * width, 128), width)
            for m in range(width // step):
                cols = slice(m * step, (m + 1) * step)
                out = t_dot(b.feed[:, cols], b.hidden[:, here])
                out += t_dot(b.feed_far[layer, :, cols], b.hidden_far[:, e * width : (e + 1) * width])
                spread(layer, DOWN, out, m * step, 0, 2 * e * sizes[OUT])
        if layer == LATE:
            reload(hidden=1)

    def grad_out(layer):
        need(context=1)
        for m in range(width // step):
            cols = slice(m * step, (m + 1) * step)
            spread(layer, OUT, t_dot(b.branch[:, cols], b.context[...]), m * step)
        if layer == LATE:
            reload(context=1)

    def grad_up(layer):
        for copy in sent[layer].pre:
            copy.wait_recv()
        need(normed=1, normed_far=1)
        if layer == LATE:
            normed_y_flights[LATE].wait_recv()
        for m in range(hidden // 2 // step):
            here = pl.ds(pl.multiple_of((2 * m + at[Y]) * step, 128), step)
            out = t_dot(b.pre[:, here], b.normed[...])
            out += t_dot(b.pre_far[layer, :, m * step : (m + 1) * step], b.normed_far[...])
            spread(layer, UP, out, 0, 2 * m)
        if layer == LATE:
            normed_y_flights[EARLY].wait_recv()
            left(normed_y_flights[LATE])
            left(normed_x_flights[LATE][0])
            reload(normed=1, normed_far=1)

    def grad_in(layer):
        need(rows=1, rows_far=1)
        for m in range(3 * width // step):
            if m * step < width:
                out = t_dot(b.packed[:, m * step : (m + 1) * step], b.rows[...])
            else:
                cols = slice(m * step - width, (m + 1) * step - width)
                out = t_dot(b.near[layer, 0, :, cols], b.rows_far[...])
                out += t_dot(b.near[layer, 1, :, cols], b.rows[...])
            spread(layer, IN, out, m * step)
        if layer == LATE:
            reload(rows=1, rows_far=1)

    grad_fns = {IN: grad_in, OUT: grad_out, UP: grad_up, DOWN: grad_down}
    made = set()

    total = r.total

    def job(layer, number):
        matrix, order = JOBS[number][0], ORDERS[layer][number]
        axes = BLOCKS[matrix]
        first, count = job_rows(number, sizes)
        part = pl.ds(first, count)
        mine_ref = b.grads[matrix].at[1 + layer]
        free = list(axes)
        if (layer, matrix) not in made:
            made.add((layer, matrix))
            grad_fns[matrix](layer)
        if layer == EARLY:
            pl.semaphore_wait(b.credit.at[number], 5)
        near = push(b.grads[matrix].at[(0,) + (ALL,) * len(free) + (part,)], b.core[number], C)
        yield
        near.wait_recv()
        left(near)

        def add(where, landed):
            index = tuple(where.get(axis, ALL) for axis in axes)
            if len(free) >= 3:
                spot = axes.index(free[0])
                for i in range(2):
                    one = index[:spot] + (i,) + index[spot + 1 :] + (part,)
                    mine_ref[one] = mine_ref[one] + landed[i]
            else:
                mine_ref[index + (part,)] = mine_ref[index + (part,)] + landed[...]

        add({}, b.core[number])
        where = {}
        for step_at, axis in enumerate(order):
            free.remove(axis)
            landing = b.land[number][step_at]
            away = {**where, axis: 1 - at[axis]}
            one = push(mine_ref.at[tuple(away.get(a, ALL) for a in axes) + (part,)], landing, axis)
            yield
            one.wait_recv()
            left(one)
            where[axis] = at[axis]
            if free:
                add(where, landing)
            else:
                index = tuple(where[a] for a in axes) + (part,)
                spot = pl.ds(starts[matrix] + first, count)
                total[layer, c, spot] = mine_ref[index].astype(F32) + landing[...].astype(F32)
        end = push(total.at[layer, c, spot], total.at[layer, c, spot], C)
        if layer == LATE:
            for to in links.peers:
                pl.semaphore_signal(b.credit.at[number], inc=1, device_id=to, device_id_type=MESH)
        yield
        end.wait_recv()
        left(end)

    def small_job():
        b.small_sum[0] = small[...]
        for step_at, axis in enumerate((C, X, Y, ZL, ZH)):
            one = push(b.small_sum.at[2 * step_at], b.small_sum.at[2 * step_at + 1], axis)
            yield
            one.wait_recv()
            left(one)
            b.small_sum[2 * step_at + 2] = b.small_sum[2 * step_at] + b.small_sum[2 * step_at + 1]
        r.small_out[...] = b.small_sum[10]

    jobs = {}

    def turns(keys):
        for key in keys:
            if key not in jobs:
                jobs[key] = small_job() if key == 20 else job(EARLY, key - 10) if key >= 10 else job(LATE, key)
            next(jobs[key], None)

    for layer in (LATE, EARLY):
        during = lambda point, lists=(LATE_POINTS if layer == LATE else EARLY_POINTS): turns(lists[point])
        vec, sums = b.vec.at[layer], small.at[layer]
        down_pool = 1 if layer == LATE else 0
        need(scaled_two=1, inverse_two=1)
        norm_two_back(two, b.scaled_two, b.inverse_two, vec, two, b.feed, sums)
        if layer == LATE:
            reload(scaled_two=1, inverse_two=1)
        sent[layer].feed = push(b.feed, b.feed_far.at[layer], X)
        during(0)
        need(slope=1)
        tiles = tiles_of(down_pool)
        for part in range(parts):

            @pl.loop(0, width // 256)
            def _(i, part=part, tiles=tiles, sums=sums):
                cols = chunk(i, 256, part * width)
                back = dot_t(b.feed[...], tiles[part, chunk(i, 256), :]) * b.slope[:, cols].astype(F32)
                b.pre[:, cols] = back.astype(BF16)
                sums[8 + part : 9 + part, chunk(i, 256)] = col_sum(b.pre[:, cols].astype(F32))

            other = pl.ds(pl.multiple_of((2 * part + 1 - at[Y]) * step, 128), step)
            sent[layer].pre.append(push(b.pre.at[:, other], b.pre_far.at[layer, :, pl.ds(part * step, step)], Y))
            during(1 + part)
        load_weights(layer, REST_W, down_pool)
        if layer == LATE:
            reload(slope=1)
            far_hidden(layer, 0)
        tiles = tiles_of(1 - down_pool)

        @pl.loop(0, width // 256)
        def _(i, tiles=tiles):
            cols = chunk(i, 256)
            value = two[:, cols]
            for part in range(parts):
                value += dot_t(b.pre[:, part * width : (part + 1) * width], tiles[part, chunk(i, 256), :])
            two[:, cols] = value

        if layer == LATE:
            load_weights(EARLY, DOWN_W, 0)
        need(scaled_one=1, inverse_one=1)
        norm_one_back(two, b.scaled_one, b.inverse_one, vec, b.branch, sums)
        if layer == LATE:
            reload(scaled_one=1, inverse_one=1)
        rest = tiles_of(down_pool)
        context_back(b.branch, rest.at[3], b.grad_context)
        during(5)
        during(6)
        need(query=1, keys=1, values=1)
        attend_back(tl, lens, b.query, b.keys, b.values, b.grad_context, b.packed, b.parts, sums)
        if layer == LATE:
            reload(query=1, keys=1, values=1)
        near = b.near
        scatter = [push(b.parts.at[beyond], near.at[layer, 0], C), push(b.parts.at[beside], near.at[layer, 1], C)]
        during(7)
        scatter[0].wait_recv()
        near[layer, 0] = near[layer, 0] + b.parts[far]
        if layer == EARLY:
            left(sent[LATE].far)

        @pl.loop(0, width // 256)
        def _(i, layer=layer, rest=rest):
            cols = chunk(i, 256)
            value = dot_t(near[layer, 0, :, 0:width], rest[1, chunk(i, 256), :])
            value += dot_t(near[layer, 0, :, width:], rest[2, chunk(i, 256), :])
            b.far_send[:, cols] = value.astype(BF16)

        sent[layer].far = push(b.far_send, b.far_recv.at[layer], X)
        scatter[1].wait_recv()
        near[layer, 1] = near[layer, 1] + b.parts[mine]
        left(*scatter)
        during(8)

        @pl.loop(0, width // 256)
        def _(i, layer=layer, rest=rest):
            cols = chunk(i, 256)
            value = two[:, cols] + dot_t(b.packed[...], rest[0, chunk(i, 256), :])
            value += dot_t(near[layer, 1, :, 0:width], rest[1, chunk(i, 256), :])
            two[:, cols] = value + dot_t(near[layer, 1, :, width:], rest[2, chunk(i, 256), :])

        if layer == LATE:
            load_weights(EARLY, UP_W, 1)
        during(9)
        during(10)
        sent[layer].far.wait_recv()
        out = two if layer == LATE else r.dx_rows
        out[...] = two[...] + b.far_recv[layer].astype(F32)
        if layer == LATE:
            left(sent[layer].feed, *sent[layer].pre)

    turns(TAIL)
    for one in jobs.values():
        assert next(one, jobs) is jobs
    assert len(jobs) == 2 * len(JOBS) + 1
    left()


def finish_kernel(total_h, small_h, y_h, dx_h, *outs):
    y_long, y_short, dx_long, dx_short, out_in, out_out, out_up, out_down, out_bias, out_gain, out_bias_up = outs[:11]
    total, small, y_rows, dx_rows, flip, sems = outs[11:]
    copies = [
        pltpu.make_async_copy(src, dst, sems.at[i])
        for i, (src, dst) in enumerate(((y_h, y_rows), (dx_h, dx_rows), (small_h, small), (total_h, total)))
    ]
    for copy in copies:
        copy.start()
    for copy in copies:
        copy.wait()
    d, c = lax.axis_index("dp"), lax.rem(lax.axis_index("seq"), 2)
    half, width = total.shape[-1], y_rows.shape[1]
    tl = y_long.shape[1]
    sizes, starts = matrix_rows(width, (small.shape[1] - 8) * width)
    y_long[0], y_short[0] = y_rows[0:tl, :], y_rows[tl:, :]
    dx_long[0], dx_short[0] = dx_rows[0:tl, :], dx_rows[tl:, :]
    quarter = half // 2
    for layer in range(LAYERS):
        for matrix, out in ((IN, out_in), (OUT, out_out), (UP, out_up)):
            part = slice(starts[matrix], starts[matrix] + sizes[matrix])
            both = jnp.concatenate([total[layer, 0, part], total[layer, 1, part]], axis=0)
            flip[:, 0 : both.shape[0]] = both.T
            out[layer] = flip[pl.ds(pl.multiple_of(quarter * c, 8), quarter), 0 : both.shape[0]]
        piece = sizes[OUT]
        strips = width // half
        for core in range(2):
            for e in range(strips):
                part = pl.ds(pl.multiple_of(starts[DOWN] + piece * (strips * c + e), 8), piece)
                out_down[layer, piece * core : piece * (core + 1), half * e : half * (e + 1)] = total[layer, core, part]
        wide = out_bias.shape[2]
        turned = pltpu.roll(small[layer, 0:8, :], lax.rem(width - wide * d, width), 1)
        for i in range(6):
            out_bias[i, layer : layer + 1, :] = turned[i : i + 1, 0:wide]
        out_gain[layer] = turned[6:8, 0:wide]
        wide = out_bias_up.shape[1]
        each = width // wide
        here = pl.ds(pl.multiple_of(wide * lax.rem(d, each), 128), wide)
        out_bias_up[layer : layer + 1, :] = small[layer, pl.ds(8 + d // each, 1), here]


def run_kernels(len_long, len_short, x_long, x_short, cot_long, cot_short, weights, bias, gain, bias_up):
    n_seq, n_dp = lax.axis_size("seq"), lax.axis_size("dp")
    tl, ts, width = x_long.shape[1], x_short.shape[1], x_long.shape[2]
    rows, hidden = tl + ts, bias_up.shape[1]
    sizes, _ = matrix_rows(width, hidden)
    half = width // 2
    sums = (LAYERS, 8 + hidden // width, width)
    two_d, tall = (rows, width), (rows, hidden)
    bf = lambda *shape: pltpu.VMEM(shape, BF16)
    f32 = lambda *shape: pltpu.VMEM(shape, F32)
    group = (n_seq,) + two_d
    kept = dict(
        rows=(two_d, BF16), query=(two_d, BF16), keys=(group, BF16), values=(group, BF16), context=(two_d, BF16),
        scaled_one=(two_d, F32), inverse_one=((rows, 128), F32), normed=(two_d, BF16), slope=(tall, BF16),
        hidden=(tall, BF16), scaled_two=(two_d, F32), inverse_two=((rows, 128), F32), rows_far=(two_d, BF16),
        normed_far=(two_d, BF16),
    )
    core, land = [], []
    copies = LAYERS * 7 + 5 + LAYERS * (4 + hidden // width)
    for number, (matrix, _, _) in enumerate(JOBS):
        count = job_rows(number, sizes)[1]
        free = len(BLOCKS[matrix])
        core.append(bf(*(2,) * free, count, half))
        land.append([bf(*(2,) * (free - 1 - i), count, half) for i in range(free)])
        copies += LAYERS * (free + 2)
    scratch = dict(
        pool=bf(2, 4, width, width),
        hidden_far=bf(rows, hidden // 2),
        normed_x=bf(LAYERS, *two_d),
        two=f32(*two_d),
        vec=f32(*sums),
        small=f32(*sums),
        small_sum=f32(11, *sums),
        feed=bf(*two_d),
        feed_far=bf(LAYERS, *two_d),
        pre=bf(*tall),
        pre_far=bf(LAYERS, rows, hidden // 2),
        branch=bf(*two_d),
        grad_context=bf(*two_d),
        packed=bf(*two_d),
        parts=bf(n_seq, rows, 2 * width),
        near=bf(LAYERS, 2, rows, 2 * width),
        far_send=bf(*two_d),
        far_recv=bf(LAYERS, *two_d),
        grads=[bf(1 + LAYERS, *(2,) * len(BLOCKS[m]), sizes[m], half) for m in range(4)],
        core=core,
        land=land,
        pool_sem=pltpu.SemaphoreType.DMA((10, 4)),
        store_sem=pltpu.SemaphoreType.DMA((len(kept),)),
        load_sem=pltpu.SemaphoreType.DMA((len(kept),)),
        far_sem=pltpu.SemaphoreType.DMA((2,)),
        send=pltpu.SemaphoreType.DMA((copies,)),
        recv=pltpu.SemaphoreType.DMA((copies,)),
        credit=pltpu.SemaphoreType.REGULAR((len(JOBS),)),
        **{name: pltpu.VMEM(*shape) for name, shape in kept.items()},
    )
    struct = lambda shape, dtype=F32: jax.ShapeDtypeStruct(shape, dtype)
    ins = dict(
        len_long=len_long, len_short=len_short, x_long=x_long, x_short=x_short, cot_long=cot_long,
        cot_short=cot_short, weights=list(weights), bias=bias, gain=gain, bias_up=bias_up,
    )
    in_specs = dict.fromkeys(ins, VMEM)
    in_specs.update(len_long=SMEM, len_short=SMEM, weights=[ANY] * 4)
    outs = dict(
        y_rows=struct(two_d, BF16),
        dx_rows=struct(two_d),
        total=struct((LAYERS, 2, sum(sizes), half)),
        small_out=struct(sums),
        kept={name: struct(*shape) for name, shape in kept.items()},
    )
    out_specs = dict.fromkeys(outs, VMEM)
    out_specs.update(kept={name: ANY for name in kept})
    trees = [jax.tree.flatten(part) for part in (ins, outs, scratch)]
    index = iter(range(sum(len(leaves) for leaves, _ in trees)))
    numbered = [jax.tree.unflatten(tree, [next(index) for _ in leaves]) for leaves, tree in trees]
    names = {**numbered[0], **numbered[1], **dict(scratch=numbered[2])}
    places, tree = jax.tree.flatten(names)

    def kernel(*refs):
        encoder_kernel(tree, None, *(refs[i] for i in places))

    flat_out = pl.pallas_call(
        kernel,
        out_shape=trees[1][0],
        in_specs=jax.tree.leaves(in_specs),
        out_specs=jax.tree.leaves(out_specs),
        scratch_shapes=trees[2][0],
        compiler_params=pltpu.CompilerParams(collective_id=0, has_side_effects=True, vmem_limit_bytes=VMEM_LIMIT),
        name="encoder",
    )(*trees[0][0])
    made = jax.tree.unflatten(trees[1][1], flat_out)
    finals = [
        struct(x_long.shape, BF16),
        struct(x_short.shape, BF16),
        struct(x_long.shape),
        struct(x_short.shape),
        struct((LAYERS, width // n_seq, 3 * width // n_dp)),
        struct((LAYERS, width // n_seq, width // n_dp)),
        struct((LAYERS, width // n_seq, hidden // n_dp)),
        struct((LAYERS, width // n_dp, hidden // n_seq)),
        struct((6, LAYERS, width // n_dp)),
        struct((LAYERS, 2, width // n_dp)),
        struct((LAYERS, hidden // n_dp)),
    ]
    return pl.pallas_call(
        finish_kernel,
        out_shape=finals,
        in_specs=[ANY] * 4,
        out_specs=[VMEM] * len(finals),
        scratch_shapes=[
            f32(LAYERS, 2, sum(sizes), half),
            f32(*sums),
            bf(*two_d),
            f32(*two_d),
            f32(half, 2 * max(sizes)),
            pltpu.SemaphoreType.DMA((4,)),
        ],
        compiler_params=pltpu.CompilerParams(vmem_limit_bytes=VMEM_LIMIT),
        name="finish",
    )(made["total"], made["small_out"], made["y_rows"], made["dx_rows"])


def norm_rows(values, gain_row, shift_row):
    centre = values - jnp.mean(values, axis=-1, keepdims=True)
    spread = jnp.mean(centre * centre, axis=-1, keepdims=True)
    inverse = lax.rsqrt(spread + 1e-12)
    scaled = centre * inverse
    return (scaled * gain_row + shift_row, scaled, inverse)


def plain_norm_back(gradient, scaled, inverse, gain_row):
    inner_sum = gradient * gain_row
    mean_one = jnp.mean(inner_sum, axis=-1, keepdims=True)
    mean_two = jnp.mean(inner_sum * scaled, axis=-1, keepdims=True)
    back = inverse * (inner_sum - mean_one - scaled * mean_two)
    return (back, jnp.sum(gradient * scaled, axis=0), jnp.sum(gradient, axis=0))


def product(left_side, right_side):
    return jnp.dot(left_side, right_side, preferred_element_type=jnp.float32)


def contract_rows(left_side, right_side):
    return lax.dot_general(
        left_side, right_side, (((0,), (0,)), ((), ())), preferred_element_type=jnp.float32
    )


def times_transpose(left_side, right_side):
    return lax.dot_general(
        left_side, right_side, (((1,), (1,)), ((), ())), preferred_element_type=jnp.float32
    )


def head_scores(packed, lengths):
    seq_count, length, _, group_width = packed.shape
    split_heads = packed.reshape(seq_count, length, 3, group_width // HD, HD)
    query_rows = split_heads[:, :, 0]
    key_rows = split_heads[:, :, 1]
    value_rows = split_heads[:, :, 2]
    scores = jnp.einsum(
        "bqhd,bkhd->bhqk", query_rows, key_rows, preferred_element_type=jnp.float32
    ) * HD ** (-0.5)
    places = lax.broadcasted_iota(jnp.int32, (seq_count, length), 1)
    key_valid = (places < lengths[:, None])[:, None, None, :]
    scores = jnp.where(key_valid, scores, -1000000000.0)
    return (scores, query_rows, key_rows, value_rows)


def plain_attend(packed, lengths):
    seq_count, length, _, group_width = packed.shape
    scores, query_rows, key_rows, value_rows = head_scores(packed, lengths)
    log_total = jax.nn.logsumexp(scores, axis=-1, keepdims=True)
    weights = jnp.exp(scores - log_total).astype(jnp.bfloat16)
    context = jnp.einsum("bhqk,bkhd->bqhd", weights, value_rows, preferred_element_type=jnp.float32)
    return (context.astype(jnp.bfloat16).reshape(seq_count, length, group_width), log_total)


def plain_attend_back(packed, lengths, log_total, grad_context):
    seq_count, length, _, group_width = packed.shape
    scores, query_rows, key_rows, value_rows = head_scores(packed, lengths)
    probabilities = jnp.exp(scores - log_total)
    weights = probabilities.astype(jnp.bfloat16)
    grad_heads = grad_context.reshape(seq_count, length, group_width // HD, HD)
    grad_values = jnp.einsum(
        "bhqk,bqhd->bkhd", weights, grad_heads, preferred_element_type=jnp.float32
    )
    grad_probs = jnp.einsum(
        "bqhd,bkhd->bhqk", grad_heads, value_rows, preferred_element_type=jnp.float32
    )
    inner_sum = jnp.sum(probabilities * grad_probs, axis=-1, keepdims=True)
    grad_scores = (probabilities * (grad_probs - inner_sum)).astype(jnp.bfloat16)
    score_scale = HD ** (-0.5)
    grad_query = (
        jnp.einsum("bhqk,bkhd->bqhd", grad_scores, key_rows, preferred_element_type=jnp.float32)
        * score_scale
    )
    grad_keys = (
        jnp.einsum("bhqk,bqhd->bkhd", grad_scores, query_rows, preferred_element_type=jnp.float32)
        * score_scale
    )
    joined = jnp.stack([grad_query, grad_keys, grad_values], axis=2).astype(jnp.bfloat16)
    return joined.reshape(seq_count, length, 3, group_width)


def body(
    x_long,
    x_short,
    len_long,
    len_short,
    w_attn_in,
    w_attn_out,
    w_ffn_in,
    w_ffn_out,
    bias_vec,
    gain_vec,
    bias_ffn,
    cot_long,
    cot_short,
):
    long_shape = x_long.shape
    short_shape = x_short.shape
    count_long = long_shape[0] * long_shape[1]
    model_width = long_shape[2]

    def split_long(token_rows, tail):
        return token_rows[:count_long].reshape((long_shape[0], long_shape[1]) + tail)

    def split_short(token_rows, tail):
        return token_rows[count_long:].reshape((short_shape[0], short_shape[1]) + tail)

    token_rows = jnp.concatenate(
        [x_long.reshape(-1, model_width), x_short.reshape(-1, model_width)], axis=0
    )
    saved = []
    for layer_idx in range(LAYERS):
        biases = bias_vec[layer_idx].astype(jnp.float32)
        gain_rows = gain_vec[layer_idx].astype(jnp.float32)
        packed_bias = jnp.concatenate([biases[0], jnp.zeros_like(biases[0]), biases[1]])
        packed = (product(token_rows, w_attn_in[layer_idx]) + packed_bias).astype(jnp.bfloat16)
        heads_long, heads_short = (
            lax.all_to_all(
                split_long(packed, (3, model_width)), "seq", split_axis=3, concat_axis=1, tiled=True
            ),
            lax.all_to_all(
                split_short(packed, (3, model_width)),
                "seq",
                split_axis=3,
                concat_axis=1,
                tiled=True,
            ),
        )
        context_long, total_long = plain_attend(heads_long, len_long)
        context_short, total_short = plain_attend(heads_short, len_short)
        back_long, back_short = (
            lax.all_to_all(context_long, "seq", split_axis=1, concat_axis=2, tiled=True),
            lax.all_to_all(context_short, "seq", split_axis=1, concat_axis=2, tiled=True),
        )
        context = jnp.concatenate(
            [back_long.reshape(-1, model_width), back_short.reshape(-1, model_width)], axis=0
        )
        branch = product(context, w_attn_out[layer_idx]) + biases[2]
        normed, scaled_one, inverse_one = norm_rows(
            token_rows.astype(jnp.float32) + branch, gain_rows[0], biases[3]
        )
        normed = normed.astype(jnp.bfloat16)
        hidden_pre = product(normed, w_ffn_in[layer_idx]) + bias_ffn[layer_idx].astype(jnp.float32)
        hidden = jax.nn.gelu(hidden_pre, approximate=False).astype(jnp.bfloat16)
        feed_out = product(hidden, w_ffn_out[layer_idx]) + biases[4]
        layer_out, scaled_two, inverse_two = norm_rows(
            normed.astype(jnp.float32) + feed_out, gain_rows[1], biases[5]
        )
        saved.append(
            (
                token_rows,
                heads_long,
                heads_short,
                total_long,
                total_short,
                context,
                scaled_one,
                inverse_one,
                normed,
                hidden_pre,
                hidden,
                scaled_two,
                inverse_two,
            )
        )
        token_rows = layer_out.astype(jnp.bfloat16)
    y_long = token_rows[:count_long].reshape(long_shape)
    y_short = token_rows[count_long:].reshape(short_shape)
    grad_rows = jnp.concatenate(
        [cot_long.reshape(-1, model_width), cot_short.reshape(-1, model_width)], axis=0
    ).astype(jnp.float32)
    layer_grads = [None] * LAYERS
    for layer_idx in reversed(range(LAYERS)):
        (
            rows_in,
            heads_long,
            heads_short,
            total_long,
            total_short,
            context,
            scaled_one,
            inverse_one,
            normed,
            hidden_pre,
            hidden,
            scaled_two,
            inverse_two,
        ) = saved[layer_idx]
        gain_rows = gain_vec[layer_idx].astype(jnp.float32)
        grad_two, grad_gain_two, grad_shift_two = plain_norm_back(
            grad_rows, scaled_two, inverse_two, gain_rows[1]
        )
        grad_feed = grad_two.astype(jnp.bfloat16)
        grad_bias_down = jnp.sum(grad_feed.astype(jnp.float32), axis=0)
        grad_down = contract_rows(hidden, grad_feed)
        grad_hidden = times_transpose(grad_feed, w_ffn_out[layer_idx])
        gelu_value, gelu_back = jax.vjp(partial(jax.nn.gelu, approximate=False), hidden_pre)
        grad_pre = gelu_back(grad_hidden)[0].astype(jnp.bfloat16)
        grad_bias_up = jnp.sum(grad_pre.astype(jnp.float32), axis=0)
        grad_up = contract_rows(normed, grad_pre)
        grad_normed = grad_two + times_transpose(grad_pre, w_ffn_in[layer_idx])
        grad_one, grad_gain_one, grad_shift_one = plain_norm_back(
            grad_normed, scaled_one, inverse_one, gain_rows[0]
        )
        grad_branch = grad_one.astype(jnp.bfloat16)
        grad_bias_out = jnp.sum(grad_branch.astype(jnp.float32), axis=0)
        grad_out = contract_rows(context, grad_branch)
        grad_context = times_transpose(grad_branch, w_attn_out[layer_idx]).astype(jnp.bfloat16)
        grad_heads_long, grad_heads_short = (
            lax.all_to_all(
                split_long(grad_context, (model_width,)),
                "seq",
                split_axis=2,
                concat_axis=1,
                tiled=True,
            ),
            lax.all_to_all(
                split_short(grad_context, (model_width,)),
                "seq",
                split_axis=2,
                concat_axis=1,
                tiled=True,
            ),
        )
        joined_long = plain_attend_back(heads_long, len_long, total_long, grad_heads_long)
        joined_short = plain_attend_back(heads_short, len_short, total_short, grad_heads_short)
        tokens_long, tokens_short = (
            lax.all_to_all(joined_long, "seq", split_axis=1, concat_axis=3, tiled=True),
            lax.all_to_all(joined_short, "seq", split_axis=1, concat_axis=3, tiled=True),
        )
        grad_packed = jnp.concatenate(
            [tokens_long.reshape(-1, 3 * model_width), tokens_short.reshape(-1, 3 * model_width)],
            axis=0,
        )
        packed_sums = jnp.sum(grad_packed.astype(jnp.float32), axis=0)
        grad_in = contract_rows(rows_in, grad_packed)
        grad_rows = grad_one + times_transpose(grad_packed, w_attn_in[layer_idx])
        grad_bias = jnp.stack(
            [
                packed_sums[:model_width],
                packed_sums[2 * model_width :],
                grad_bias_out,
                grad_shift_one,
                grad_bias_down,
                grad_shift_two,
            ]
        )
        grad_gain = jnp.stack([grad_gain_one, grad_gain_two])
        layer_grads[layer_idx] = (
            grad_in,
            grad_out,
            grad_up,
            grad_down,
            grad_bias,
            grad_gain,
            grad_bias_up,
        )
    dx_long = grad_rows[:count_long].reshape(long_shape)
    dx_short = grad_rows[count_long:].reshape(short_shape)
    local_in = jnp.stack([entry[0] for entry in layer_grads])
    local_out = jnp.stack([entry[1] for entry in layer_grads])
    local_up = jnp.stack([entry[2] for entry in layer_grads])
    local_down = jnp.stack([entry[3] for entry in layer_grads])
    local_bias = jnp.stack([entry[4] for entry in layer_grads])
    local_gain = jnp.stack([entry[5] for entry in layer_grads])
    local_ffn = jnp.stack([entry[6] for entry in layer_grads])
    part_in, part_out, part_up, part_down = (local_in, local_out, local_up, local_down)
    sum_in, sum_out, sum_up, sum_down, sum_bias, sum_gain, sum_ffn = (
        lax.psum_scatter(part_in, "dp", scatter_dimension=2, tiled=True),
        lax.psum_scatter(part_out, "dp", scatter_dimension=2, tiled=True),
        lax.psum_scatter(part_up, "dp", scatter_dimension=2, tiled=True),
        lax.psum_scatter(part_down, "dp", scatter_dimension=2, tiled=True),
        lax.psum_scatter(local_bias, "dp", scatter_dimension=2, tiled=True),
        lax.psum_scatter(local_gain, "dp", scatter_dimension=2, tiled=True),
        lax.psum_scatter(local_ffn, "dp", scatter_dimension=1, tiled=True),
    )
    sum_in, sum_out, sum_up, sum_down = (
        lax.psum_scatter(
            sum_in.astype(jnp.bfloat16), "seq", scatter_dimension=1, tiled=True
        ).astype(jnp.float32),
        lax.psum_scatter(
            sum_out.astype(jnp.bfloat16), "seq", scatter_dimension=1, tiled=True
        ).astype(jnp.float32),
        lax.psum_scatter(
            sum_up.astype(jnp.bfloat16), "seq", scatter_dimension=1, tiled=True
        ).astype(jnp.float32),
        lax.psum_scatter(
            sum_down.astype(jnp.bfloat16), "seq", scatter_dimension=1, tiled=True
        ).astype(jnp.float32),
    )
    sum_bias, sum_gain, sum_ffn = lax.psum((sum_bias, sum_gain, sum_ffn), "seq")
    return (
        y_long,
        y_short,
        dx_long,
        dx_short,
        sum_in,
        sum_out,
        sum_up,
        sum_down,
        sum_bias,
        sum_gain,
        sum_ffn,
    )


def fast_body(
    x_long, x_short, len_long, len_short, w_attn_in, w_attn_out, w_ffn_in, w_ffn_out,
    bias_vec, gain_vec, bias_ffn, cot_long, cot_short,
):
    weights = (w_attn_in, w_attn_out, w_ffn_in, w_ffn_out)
    outs = list(
        run_kernels(
            len_long, len_short, x_long, x_short, cot_long, cot_short, weights,
            bias_vec.transpose(1, 0, 2), gain_vec, bias_ffn,
        )
    )
    outs[7] = outs[7].transpose(0, 2, 1)
    outs[8] = outs[8].transpose(1, 0, 2)
    return tuple(outs)


def solution(mesh):
    tokens = P("dp", "seq", None)
    matrix = P(None, "seq", "dp")
    vector = P(None, None, "dp")
    return jax.shard_map(
        fast_body if mesh.shape["dp"] == 8 and mesh.shape["seq"] == 4 else body,
        mesh=mesh,
        in_specs=(tokens, tokens, P("dp"), P("dp")) + (P(),) * 7 + (tokens, tokens),
        out_specs=(tokens,) * 4 + (matrix,) * 4 + (vector, vector, P(None, "dp")),
        check_vma=False,
    )
```

```python
from functools import partial
from types import SimpleNamespace

import jax
import jax.numpy as jnp
from jax import lax
from jax.experimental import pallas as pl
from jax.experimental.pallas import tpu as pltpu
from jax.sharding import PartitionSpec as P

HD = 64
LAYERS = 2
PAIR = 2 * HD
F32 = jnp.float32
BF16 = jnp.bfloat16
MESH = pl.DeviceIdType.MESH
VMEM_LIMIT = 63 << 20
ANY = pl.BlockSpec(memory_space=pl.ANY)
VMEM = pl.BlockSpec(memory_space=pltpu.VMEM)
SMEM = pl.BlockSpec(memory_space=pltpu.SMEM)


def dot(left, right):
    return jnp.dot(left, right, preferred_element_type=F32)


def dot_t(left, right):
    return lax.dot_general(left, right, (((1,), (1,)), ((), ())), preferred_element_type=F32)


def t_dot(left, right):
    return lax.dot_general(left, right, (((0,), (0,)), ((), ())), preferred_element_type=F32)


def row_mean(values):
    return jnp.mean(values, axis=-1, keepdims=True)


def col_sum(values):
    return jnp.sum(values, axis=0, keepdims=True)


def chunk(i, step, base=0, mult=None):
    return pl.ds(pl.multiple_of(base + i * step, mult or step), step)


ZH, ZL, Y, X, C = range(5)


def place():
    d, s = lax.axis_index("dp"), lax.axis_index("seq")
    return d // 4, lax.rem(d // 2, 2), lax.rem(d, 2), s // 2, lax.rem(s, 2)


def peer_devices(at):
    peers = []
    for digit in range(5):
        zh, zl, y, x, c = (1 - value if i == digit else value for i, value in enumerate(at))
        peers.append((4 * zh + 2 * zl + y, 2 * x + c))
    return peers


def greet(peers):
    barrier = pltpu.get_barrier_semaphore()
    for peer in peers:
        pl.semaphore_signal(barrier, inc=1, device_id=peer, device_id_type=MESH)
    pl.semaphore_wait(barrier, len(peers))


def low_lanes():
    return lax.broadcasted_iota(jnp.int32, (1, PAIR), 1) < HD


def stacked(rows):
    low = low_lanes()
    masks = (low.astype(F32).astype(BF16), (~low).astype(F32).astype(BF16))
    return jnp.concatenate([rows * mask for mask in masks], axis=0)


def joined(ref, own, lanes):
    return jnp.concatenate([ref[s, own, lanes] for s in range(ref.shape[0])], axis=0)


def softmax_t(keys, query, length):
    place = lax.broadcasted_iota(jnp.int32, (keys.shape[0], 1), 0)
    scores = jnp.where(place < length, dot_t(keys, query), -1e9)
    powers = jnp.exp(scores - jnp.max(scores, axis=0, keepdims=True))
    return powers * (1.0 / jnp.sum(powers, axis=0, keepdims=True))


def attend_pair(query, keys, values, length):
    weights = softmax_t(keys, stacked(query), length).astype(BF16)
    both = t_dot(weights, values)
    count = query.shape[0]
    return jnp.where(low_lanes(), both[:count], both[count:])


def back_pair(query, keys, values, grad, length):
    count = query.shape[0]
    query, grad = stacked(query), stacked(grad)
    probs = softmax_t(keys, query, length)
    grad_probs = dot_t(values, grad)
    inner = col_sum(probs * grad_probs)
    grad_scores = (probs * (grad_probs - inner)).astype(BF16)
    both = t_dot(keys, grad_scores)
    grad_query = jnp.concatenate([both[:HD, :count], both[HD:, count:]], axis=0).T
    return grad_query * HD**-0.5, dot(grad_scores, query), dot(probs.astype(BF16), grad)


def attend(tl, lens, query, keys, values, context):
    rows, width = query.shape
    for p in range(width // PAIR):
        lanes = slice(p * PAIR, (p + 1) * PAIR)
        for which, own in enumerate((slice(0, tl), slice(tl, rows))):
            context[own, lanes] = attend_pair(
                query[own, lanes], joined(keys, own, lanes), joined(values, own, lanes), lens[which]
            ).astype(BF16)


def attend_back(tl, lens, query, keys, values, grad, packed, parts, small, many=2):
    rows, width = query.shape

    @pl.loop(0, width // PAIR // many)
    def _(i):
        for u in range(many):
            lanes = pl.ds(pl.multiple_of((i * many + u) * PAIR, PAIR), PAIR)
            vlanes = pl.ds(pl.multiple_of(width + (i * many + u) * PAIR, PAIR), PAIR)
            sums_q = jnp.zeros((1, PAIR), F32)
            sums_v = jnp.zeros((1, PAIR), F32)
            for which, own in enumerate((slice(0, tl), slice(tl, rows))):
                count = own.stop - own.start
                grad_q, grad_k, grad_v = back_pair(
                    query[own, lanes], joined(keys, own, lanes), joined(values, own, lanes), grad[own, lanes], lens[which]
                )
                grad_q = grad_q.astype(BF16)
                packed[own, lanes] = grad_q
                sums_q += col_sum(grad_q.astype(F32))
                sums_v += col_sum(grad_v)
                grad_k = grad_k.astype(BF16)
                grad_v = grad_v.astype(BF16)
                for s in range(parts.shape[0]):
                    parts[s, own, lanes] = grad_k[count * s : count * (s + 1)]
                    parts[s, own, vlanes] = grad_v[count * s : count * (s + 1)]
            small[0:1, lanes] = sums_q
            small[1:2, lanes] = sums_v


def fill_vec(vec, layer, bias, gain, bias_up):
    width = vec.shape[1]
    vec[0:6, :] = bias[:, layer, :].astype(F32)
    vec[6:8, :] = gain[layer].astype(F32)
    for part in range(bias_up.shape[1] // width):
        vec[8 + part : 9 + part, :] = bias_up[layer : layer + 1, part * width : (part + 1) * width].astype(F32)


def project_query(own, tile, vec, query):
    @pl.loop(0, own.shape[1] // 256)
    def _(i):
        cols = chunk(i, 256)
        out = dot(own[...], tile[:, cols]) + vec[0:1, cols]
        query[:, cols] = out.astype(BF16) * jnp.asarray(HD**-0.5, BF16)


def project_keys(rows, key_tile, value_tile, vec, keys, values):
    @pl.loop(0, keys.shape[1] // 256)
    def _(i):
        cols = chunk(i, 256)
        keys[:, cols] = dot(rows[...], key_tile[:, cols]).astype(BF16)
        values[:, cols] = (dot(rows[...], value_tile[:, cols]) + vec[1:2, cols]).astype(BF16)


def normalize(residual, gain_row, shift_row, scaled_o, inverse_o, out):
    centre = residual - row_mean(residual)
    inverse = lax.rsqrt(row_mean(centre * centre) + 1e-12)
    scaled = centre * inverse
    scaled_o[...] = scaled
    inverse_o[...] = jnp.broadcast_to(inverse, inverse_o.shape)
    out[...] = (scaled * gain_row + shift_row).astype(BF16)


def out_norm(own, context, w_out, vec, scaled, inverse, normed):
    residual = own[...].astype(F32) + dot(context[...], w_out[...]) + vec[2:3, :]
    normalize(residual, vec[6:7, :], vec[3:4, :], scaled, inverse, normed)


def gelu(pre):
    below = 0.5 + 0.5 * lax.erf(pre * (2.0**-0.5))
    return below, (pre * below).astype(BF16)


def ffn_up(normed, tiles, vec, hidden, slope):
    width = normed.shape[1]
    for part in range(hidden.shape[1] // width):

        @pl.loop(0, width // 256)
        def _(i, part=part):
            cols = chunk(i, 256, part * width)
            pre = dot(normed[...], tiles[part, :, chunk(i, 256)]) + vec[8 + part : 9 + part, chunk(i, 256)]
            below, hidden[:, cols] = gelu(pre)
            slope[:, cols] = (below + pre * (jnp.exp(pre * pre * -0.5) * 0.3989422804014327)).astype(BF16)


def half_hidden(normed, tiles, vec, x, out):
    width = normed.shape[1]
    for part in range(out.shape[1] // width):
        at = x * (out.shape[1] // width) + part

        @pl.loop(0, width // 256)
        def _(i, part=part, at=at):
            pre = dot(normed[...], tiles[at, :, chunk(i, 256)]) + vec[pl.ds(8 + at, 1), chunk(i, 256)]
            out[:, chunk(i, 256, part * width)] = gelu(pre)[1]


def ffn_down(normed, hidden, tiles, vec, scaled, inverse, out):
    width = normed.shape[1]
    residual = normed[...].astype(F32) + vec[4:5, :]
    for part in range(hidden.shape[1] // width):
        residual += dot(hidden[:, part * width : (part + 1) * width], tiles[part])
    normalize(residual, vec[7:8, :], vec[5:6, :], scaled, inverse, out)


def norm_back(gradient, scaled, inverse, gain_row):
    inner = gradient * gain_row
    return inverse * (inner - row_mean(inner) - scaled * row_mean(inner * scaled))


def norm_two_back(grad, scaled, inverse, vec, two, feed, small):
    value = grad[...]
    small[5:6, :] = col_sum(value)
    small[7:8, :] = col_sum(value * scaled[...])
    back = norm_back(value, scaled[...], inverse[:, 0:1], vec[7:8, :])
    two[...] = back
    feed[...] = back.astype(BF16)
    small[4:5, :] = col_sum(feed[...].astype(F32))


def norm_one_back(two, scaled, inverse, vec, branch, small):
    value = two[...]
    small[3:4, :] = col_sum(value)
    small[6:7, :] = col_sum(value * scaled[...])
    back = norm_back(value, scaled[...], inverse[:, 0:1], vec[6:7, :])
    two[...] = back
    branch[...] = back.astype(BF16)
    small[2:3, :] = col_sum(branch[...].astype(F32))


def context_back(branch, w_out, grad):
    @pl.loop(0, branch.shape[1] // 256)
    def _(i):
        cols = chunk(i, 256)
        grad[:, cols] = dot_t(branch[...], w_out[cols, :]).astype(BF16)


IN, OUT, UP, DOWN = range(4)
BLOCKS = ((ZH, ZL, Y, X), (ZH, ZL, Y, X), (ZH, ZL, X), (ZH, ZL, Y))
JOBS = ((DOWN, 0, 2), (OUT, 0, 1), (UP, 0, 2), (IN, 0, 3), (IN, 1, 3), (IN, 2, 3), (DOWN, 1, 2), (UP, 1, 2))
ALL = slice(None)
LATE, EARLY = LAYERS - 1, 0

ORDERS = (
    ((Y, ZH, ZL), (X, ZL, Y, ZH), (X, ZL, ZH), (Y, X, ZL, ZH), (X, Y, ZH, ZL), (Y, X, ZL, ZH), (Y, ZL, ZH), (ZH, X, ZL)),
    ((ZL, Y, ZH), (ZL, Y, ZH, X), (ZL, X, ZH), (Y, ZL, ZH, X), (X, ZL, Y, ZH), (Y, X, ZH, ZL), (Y, ZH, ZL), (X, ZH, ZL)),
)
LATE_POINTS = (
    (),
    (),
    (),
    (),
    (),
    (),
    (1, 6, 0, 1,),
    (6, 0,),
    (7, 1, 2, 4, 3, 7, 6, 0, 5,),
    (),
    (2, 3, 4,),
)
EARLY_POINTS = (
    (5, 1,),
    (),
    (),
    (),
    (7,),
    (),
    (2, 3, 6, 0,),
    (3, 4, 1, 5, 7, 20, 6,),
    (0, 20, 2, 16, 1, 5, 4,),
    (16, 7, 11, 2, 17, 10, 12, 4, 5, 3, 20, 17, 11, 10, 12, 3, 5,),
    (16, 4, 15, 20, 1, 13, 14, 15, 11, 13, 10, 14, 16, 4, 15, 11, 12, 6, 20, 14, 13, 10,),
)
TAIL = (0, 17, 15, 12, 14, 7, 10, 13, 11, 20, 15, 17, 13, 16, 14, 11, 10, 12, 11, 5, 15, 14, 17, 12, 15, 13, 17, 13,
        3, 14, 2, 16,)


def matrix_rows(width, hidden):
    sizes = (3 * width // 16, width // 16, hidden // 16, (hidden // width) * (width // 16))
    return sizes, tuple(sum(sizes[:i]) for i in range(4))


def job_rows(number, sizes):
    matrix, part, parts = JOBS[number]
    count = sizes[matrix] // parts
    return part * count, count


class Copies:
    def __init__(self, send, recv, peers):
        self.send, self.recv, self.peers = send, recv, peers
        self.count = 0
        self.open = {}

    def make(self, src, dst, to):
        copy = pltpu.make_async_remote_copy(
            src_ref=src,
            dst_ref=dst,
            send_sem=self.send.at[self.count],
            recv_sem=self.recv.at[self.count],
            device_id=self.peers[to],
            device_id_type=MESH,
        )
        self.count += 1
        return copy

    def push(self, src, dst, to):
        copy = self.make(src, dst, to)
        copy.start()
        self.open[id(copy)] = copy
        return copy

    def left(self, *copies):
        for copy in copies or tuple(self.open.values()):
            copy.wait_send()
            del self.open[id(copy)]


def encoder_kernel(tree, counts, *refs):
    r = SimpleNamespace(**jax.tree.unflatten(tree, refs))
    b = SimpleNamespace(**r.scratch)
    w_in, w_out, w_up, w_down = r.weights
    tl = r.x_long.shape[1]
    n_seq, rows, width = b.keys.shape
    hidden = b.hidden.shape[1]
    parts, half = hidden // width, width // 2
    sizes, starts = matrix_rows(width, hidden)
    lens = (r.len_long[0], r.len_short[0])
    at = place()
    x, c = at[X], at[C]
    links = Copies(b.send, b.recv, peer_devices(at))
    push, left = links.push, links.left

    waits = {}

    def start_copy(src, dst, sem):
        copy = pltpu.make_async_copy(src, dst, sem)
        copy.start()
        return copy

    square = lambda i: pl.ds(i * width, width)
    pool_count = iter(range(b.pool_sem.shape[0]))
    DOWN_W, UP_W, REST_W = range(3)

    def load_weights(layer, which, pool):
        if which == DOWN_W:
            tiles = [w_down.at[layer, square(i), :] for i in range(parts)]
        elif which == UP_W:
            tiles = [w_up.at[layer, :, square(i)] for i in range(parts)]
        else:
            tiles = [w_in.at[layer, :, square(i)] for i in range(3)] + [w_out.at[layer]]
        sems = b.pool_sem.at[next(pool_count)]
        waits[pool] = [start_copy(tile, b.pool.at[pool, i], sems.at[i]) for i, tile in enumerate(tiles)]

    def tiles_of(pool):
        for copy in waits.pop(pool, ()):
            copy.wait()
        return b.pool.at[pool]

    kept = {name: (getattr(b, name), ref, i) for i, (name, ref) in enumerate(r.kept.items())}
    storing, loading = {}, {}

    def store(**names):
        for name in names:
            src, dst, i = kept[name]
            storing[name] = start_copy(src, dst, b.store_sem.at[i])

    def stored(**names):
        for name in names:
            storing.pop(name).wait()

    def reload(**names):
        for name in names:
            dst, src, i = kept[name]
            loading[name] = start_copy(src, dst, b.load_sem.at[i])

    def need(**names):
        for name in names:
            if name in loading:
                loading.pop(name).wait()

    load_weights(0, REST_W, 0)
    load_weights(0, UP_W, 1)
    b.rows[0:tl, :] = r.x_long[0]
    b.rows[tl:, :] = r.x_short[0]
    greet(links.peers)

    mine, far = 2 * x + c, 2 * (1 - x) + c
    beside, beyond = 2 * x + 1 - c, 2 * (1 - x) + 1 - c
    halves = (pl.ds(0, rows // 2), pl.ds(rows // 2, rows // 2))
    normed_x_flights = []
    normed_y_flights = []
    gathers = []

    for layer in range(LAYERS):
        vec = b.vec.at[layer]
        lanes = pl.ds(layer * width, width)
        group = b.parts
        flights = [push(b.rows.at[part], group.at[mine, part, lanes], X) for part in halves]
        flights.append(push(b.rows, group.at[mine, :, lanes], C))
        if layer == 0:
            for i in range(LAYERS):
                fill_vec(b.vec.at[i], i, r.bias, r.gain, r.bias_up)
            store(rows=1)
        else:
            normed_x_flights.append(push(b.normed, b.normed_x.at[0], X))
            stored(query=1, keys=1, values=1)
        rest = tiles_of(layer)
        project_query(b.rows, rest.at[0], vec, b.query)

        def keys_of(source, where, rest=rest, vec=vec):
            project_keys(source, rest.at[1], rest.at[2], vec, b.keys.at[where], b.values.at[where])

        keys_of(b.rows, mine)
        flights[2].wait_recv()
        keys_of(group.at[beside, :, lanes], beside)
        passed = []
        for i, part in enumerate(halves):
            flights[i].wait_recv()
            passed.append(push(group.at[far, part, lanes], group.at[far, part, lanes], C))
        if layer == 0:
            far_copy = start_copy(group.at[far, :, lanes], r.kept["rows_far"], b.far_sem.at[0])
        else:
            far_copy = start_copy(group.at[far, :, lanes], b.rows_far, b.far_sem.at[1])
        keys_of(group.at[far, :, lanes], far)
        gathers += passed + (flights if layer else [])
        for copy in passed:
            copy.wait_recv()
        keys_of(group.at[beyond, :, lanes], beyond)
        if layer == 0:
            store(query=1, keys=1, values=1)
        else:
            stored(context=1)
        attend(tl, lens, b.query, b.keys, b.values, b.context)
        if layer == 0:
            store(context=1)
        else:
            stored(scaled_one=1, inverse_one=1, normed=1)
            left(*normed_x_flights, *normed_y_flights)
        out_norm(b.rows, b.context, rest.at[3], vec, b.scaled_one, b.inverse_one, b.normed)
        load_weights(layer, DOWN_W, layer)
        if layer == 0:
            normed_y_flights.append(push(b.normed, r.kept["normed_far"], Y))
            store(scaled_one=1, inverse_one=1, normed=1)
        else:
            normed_x_flights.append(push(b.normed, b.normed_x.at[1], X))
            normed_y_flights.append(push(b.normed, b.normed_far, Y))
            stored(hidden=1, slope=1)
        ffn_up(b.normed, tiles_of(1 - layer), vec, b.hidden, b.slope)
        if layer == 0:
            load_weights(1, REST_W, 1)
            store(hidden=1, slope=1)
            stored(rows=1)
            left(*flights)
        else:
            stored(scaled_two=1, inverse_two=1)
        far_copy.wait()
        after = b.rows if layer == 0 else b.y_rows
        ffn_down(b.normed, b.hidden, tiles_of(layer), vec, b.scaled_two, b.inverse_two, after)
        if layer == 0:
            load_weights(1, UP_W, 0)
            store(scaled_two=1, inverse_two=1)
    left(*gathers)
    out_count = iter(range(b.out_sem.shape[0]))
    writing = []

    def write(src, dst):
        writing.append(start_copy(src, dst, b.out_sem.at[next(out_count)]))

    write(b.y_rows.at[0:tl], r.y_long.at[0])
    write(b.y_rows.at[tl:rows], r.y_short.at[0])

    two, small = b.two, b.small
    two[0:tl, :] = r.cot_long[0].astype(F32)
    two[tl:, :] = r.cot_short[0].astype(F32)

    step = 384

    def slot(layer, core):
        return (1 - (c - core) * (c - core)) * (1 + layer)

    def spread(layer, matrix, out, first_row, block0=0, row0=0):
        piece = sizes[OUT if matrix == DOWN else matrix]
        row = 0
        while row < out.shape[0]:
            spot = first_row + row
            count = min(piece - spot % piece, out.shape[0] - row)
            block, core, inside = block0 + spot // (2 * piece), (spot // piece) % 2, row0 + spot % piece
            digits = (block // 4, (block // 2) % 2, block % 2)
            index = (slot(layer, core),) + tuple(digits[axis] for axis in BLOCKS[matrix] if axis != X)
            for side in range(2):
                value = out[row : row + count, half * side : half * (side + 1)].astype(BF16)
                if matrix == DOWN:
                    b.grads[matrix][index + (pl.ds(inside + side * piece, count),)] = value
                else:
                    b.grads[matrix][index + (side, pl.ds(inside, count))] = value
            row += count

    sent = [SimpleNamespace(pre=[]) for _ in range(LAYERS)]
    normed_x_flights = [(normed_x_flights[i], i) for i in range(LAYERS)]

    def far_hidden(layer, pool):
        normed_x_flights[layer][0].wait_recv()
        half_hidden(b.normed_x.at[layer], tiles_of(pool), b.vec.at[layer], x, b.hidden_far)

    def grad_down(layer):
        sent[layer].feed.wait_recv()
        need(hidden=1)
        if layer == EARLY:
            far_hidden(layer, 1)
        for e in range(parts // 2):
            here = pl.ds(pl.multiple_of(x * (hidden // 2) + e * width, 128), width)
            for m in range(width // step):
                cols = slice(m * step, (m + 1) * step)
                out = t_dot(b.feed[:, cols], b.hidden[:, here])
                out += t_dot(b.feed_far[layer, :, cols], b.hidden_far[:, e * width : (e + 1) * width])
                spread(layer, DOWN, out, m * step, 0, 2 * e * sizes[OUT])
        if layer == LATE:
            reload(hidden=1)

    def grad_out(layer):
        need(context=1)
        for m in range(width // step):
            cols = slice(m * step, (m + 1) * step)
            spread(layer, OUT, t_dot(b.branch[:, cols], b.context[...]), m * step)
        if layer == LATE:
            reload(context=1)

    def grad_up(layer):
        for copy in sent[layer].pre:
            copy.wait_recv()
        need(normed=1, normed_far=1)
        if layer == LATE:
            normed_y_flights[LATE].wait_recv()
        for m in range(hidden // 2 // step):
            here = pl.ds(pl.multiple_of((2 * m + at[Y]) * step, 128), step)
            out = t_dot(b.pre[:, here], b.normed[...])
            out += t_dot(b.pre_far[layer, :, m * step : (m + 1) * step], b.normed_far[...])
            spread(layer, UP, out, 0, 2 * m)
        if layer == LATE:
            normed_y_flights[EARLY].wait_recv()
            left(normed_y_flights[LATE])
            left(normed_x_flights[LATE][0])
            reload(normed=1, normed_far=1)

    def grad_in(layer):
        need(rows=1, rows_far=1)
        for m in range(3 * width // step):
            if m * step < width:
                out = t_dot(b.packed[:, m * step : (m + 1) * step], b.rows[...])
            else:
                cols = slice(m * step - width, (m + 1) * step - width)
                out = t_dot(b.near[layer, 0, :, cols], b.rows_far[...])
                out += t_dot(b.near[layer, 1, :, cols], b.rows[...])
            spread(layer, IN, out, m * step)
        if layer == LATE:
            reload(rows=1, rows_far=1)

    grad_fns = {IN: grad_in, OUT: grad_out, UP: grad_up, DOWN: grad_down}
    made = set()

    total = b.total

    def job(layer, number):
        matrix, order = JOBS[number][0], ORDERS[layer][number]
        axes = BLOCKS[matrix]
        first, count = job_rows(number, sizes)
        part = pl.ds(first, count)
        mine_ref = b.grads[matrix].at[1 + layer]
        free = list(axes)
        if (layer, matrix) not in made:
            made.add((layer, matrix))
            grad_fns[matrix](layer)
        if layer == EARLY:
            pl.semaphore_wait(b.credit.at[number], 5)
        near = push(b.grads[matrix].at[(0,) + (ALL,) * len(free) + (part,)], b.core[number], C)
        yield
        near.wait_recv()
        left(near)

        def add(where, landed):
            index = tuple(where.get(axis, ALL) for axis in axes)
            if len(free) >= 3:
                spot = axes.index(free[0])
                for i in range(2):
                    one = index[:spot] + (i,) + index[spot + 1 :] + (part,)
                    mine_ref[one] = mine_ref[one] + landed[i]
            else:
                mine_ref[index + (part,)] = mine_ref[index + (part,)] + landed[...]

        add({}, b.core[number])
        where = {}
        for step_at, axis in enumerate(order):
            free.remove(axis)
            landing = b.land[number][step_at]
            away = {**where, axis: 1 - at[axis]}
            one = push(mine_ref.at[tuple(away.get(a, ALL) for a in axes) + (part,)], landing, axis)
            yield
            one.wait_recv()
            left(one)
            where[axis] = at[axis]
            if free:
                add(where, landing)
            else:
                index = tuple(where[a] for a in axes) + (part,)
                spot = pl.ds(starts[matrix] + first, count)
                total[layer, c, spot] = mine_ref[index].astype(F32) + landing[...].astype(F32)
        end = push(total.at[layer, c, spot], total.at[layer, c, spot], C)
        if layer == LATE:
            for to in links.peers:
                pl.semaphore_signal(b.credit.at[number], inc=1, device_id=to, device_id_type=MESH)
        yield
        end.wait_recv()
        left(end)

    def small_job():
        b.small_sum[0] = small[...]
        for step_at, axis in enumerate((C, X, Y, ZL, ZH)):
            one = push(b.small_sum.at[2 * step_at], b.small_sum.at[2 * step_at + 1], axis)
            yield
            one.wait_recv()
            left(one)
            b.small_sum[2 * step_at + 2] = b.small_sum[2 * step_at] + b.small_sum[2 * step_at + 1]

    jobs = {}
    turned = {}

    def turns(keys):
        for key in keys:
            turned[key] = turned.get(key, 0) + 1
            if key not in jobs:
                jobs[key] = small_job() if key == 20 else job(EARLY, key - 10) if key >= 10 else job(LATE, key)
            next(jobs[key], None)

    for layer in (LATE, EARLY):
        during = lambda point, lists=(LATE_POINTS if layer == LATE else EARLY_POINTS): turns(lists[point])
        vec, sums = b.vec.at[layer], small.at[layer]
        down_pool = 1 if layer == LATE else 0
        need(scaled_two=1, inverse_two=1)
        norm_two_back(two, b.scaled_two, b.inverse_two, vec, two, b.feed, sums)
        if layer == LATE:
            reload(scaled_two=1, inverse_two=1)
        sent[layer].feed = push(b.feed, b.feed_far.at[layer], X)
        during(0)
        need(slope=1)
        tiles = tiles_of(down_pool)
        for part in range(parts):

            @pl.loop(0, width // 256)
            def _(i, part=part, tiles=tiles, sums=sums):
                cols = chunk(i, 256, part * width)
                back = dot_t(b.feed[...], tiles[part, chunk(i, 256), :]) * b.slope[:, cols].astype(F32)
                b.pre[:, cols] = back.astype(BF16)
                sums[8 + part : 9 + part, chunk(i, 256)] = col_sum(b.pre[:, cols].astype(F32))

            other = pl.ds(pl.multiple_of((2 * part + 1 - at[Y]) * step, 128), step)
            sent[layer].pre.append(push(b.pre.at[:, other], b.pre_far.at[layer, :, pl.ds(part * step, step)], Y))
            during(1 + part)
        load_weights(layer, REST_W, down_pool)
        if layer == LATE:
            reload(slope=1)
            far_hidden(layer, 0)
        tiles = tiles_of(1 - down_pool)

        @pl.loop(0, width // 256)
        def _(i, tiles=tiles):
            cols = chunk(i, 256)
            value = two[:, cols]
            for part in range(parts):
                value += dot_t(b.pre[:, part * width : (part + 1) * width], tiles[part, chunk(i, 256), :])
            two[:, cols] = value

        if layer == LATE:
            load_weights(EARLY, DOWN_W, 0)
        need(scaled_one=1, inverse_one=1)
        norm_one_back(two, b.scaled_one, b.inverse_one, vec, b.branch, sums)
        if layer == LATE:
            reload(scaled_one=1, inverse_one=1)
        rest = tiles_of(down_pool)
        context_back(b.branch, rest.at[3], b.grad_context)
        during(5)
        during(6)
        need(query=1, keys=1, values=1)
        attend_back(tl, lens, b.query, b.keys, b.values, b.grad_context, b.packed, b.parts, sums)
        if layer == LATE:
            reload(query=1, keys=1, values=1)
        near = b.near
        scatter = [push(b.parts.at[beyond], near.at[layer, 0], C), push(b.parts.at[beside], near.at[layer, 1], C)]
        during(7)
        scatter[0].wait_recv()
        near[layer, 0] = near[layer, 0] + b.parts[far]
        if layer == EARLY:
            left(sent[LATE].far)

        @pl.loop(0, width // 256)
        def _(i, layer=layer, rest=rest):
            cols = chunk(i, 256)
            value = dot_t(near[layer, 0, :, 0:width], rest[1, chunk(i, 256), :])
            value += dot_t(near[layer, 0, :, width:], rest[2, chunk(i, 256), :])
            b.far_send[:, cols] = value.astype(BF16)

        sent[layer].far = push(b.far_send, b.far_recv.at[layer], X)
        scatter[1].wait_recv()
        near[layer, 1] = near[layer, 1] + b.parts[mine]
        left(*scatter)
        during(8)

        @pl.loop(0, width // 256)
        def _(i, layer=layer, rest=rest):
            cols = chunk(i, 256)
            value = two[:, cols] + dot_t(b.packed[...], rest[0, chunk(i, 256), :])
            value += dot_t(near[layer, 1, :, 0:width], rest[1, chunk(i, 256), :])
            two[:, cols] = value + dot_t(near[layer, 1, :, width:], rest[2, chunk(i, 256), :])

        if layer == LATE:
            load_weights(EARLY, UP_W, 1)
        during(9)
        during(10)
        sent[layer].far.wait_recv()
        two[...] = two[...] + b.far_recv[layer].astype(F32)
        if layer == LATE:
            left(sent[layer].feed, *sent[layer].pre)

    write(two.at[0:tl], r.dx_long.at[0])
    write(two.at[tl:rows], r.dx_short.at[0])

    d = lax.axis_index("dp")
    quarter = half // 2

    def write_matrix(layer, matrix):
        out, made_out = b.finals[matrix], r.finals[matrix]
        if matrix == DOWN:
            piece, strips = sizes[OUT], width // half
            for core in range(2):
                for e in range(strips):
                    part = pl.ds(pl.multiple_of(starts[DOWN] + piece * (strips * c + e), 8), piece)
                    out[layer, piece * core : piece * (core + 1), half * e : half * (e + 1)] = total[layer, core, part]
        else:
            part = slice(starts[matrix], starts[matrix] + sizes[matrix])
            both = jnp.concatenate([total[layer, 0, part], total[layer, 1, part]], axis=0)
            b.flip[:, 0 : both.shape[0]] = both.T
            out[layer] = b.flip[pl.ds(pl.multiple_of(quarter * c, 8), quarter), 0 : both.shape[0]]
        write(out.at[layer], made_out.at[layer])

    def write_vectors():
        wide, tall = b.bias_out.shape[2], b.bias_up_out.shape[1]
        sums = b.small_sum.at[10]
        each = width // tall
        here = pl.ds(pl.multiple_of(tall * lax.rem(d, each), 128), tall)
        for layer in range(LAYERS):
            turned = pltpu.roll(sums[layer, 0:8, :], lax.rem(width - wide * d, width), 1)
            for i in range(6):
                b.bias_out[i, layer : layer + 1, :] = turned[i : i + 1, 0:wide]
            b.gain_out[layer] = turned[6:8, 0:wide]
            b.bias_up_out[layer : layer + 1, :] = sums[layer, pl.ds(8 + d // each, 1), here]
        write(b.bias_out, r.bias_out)
        write(b.gain_out, r.gain_out)
        write(b.bias_up_out, r.bias_up_out)

    lengths = {base + i: len(ORDERS[base == 0][i]) + 3 for i in range(len(JOBS)) for base in (0, 10)}
    lengths[20] = 6
    open_jobs = {(base == 0, m): [base + i for i, job_of in enumerate(JOBS) if job_of[0] == m] for base in (0, 10) for m in range(4)}
    for key in TAIL:
        turns((key,))
        ready = [who for who, keys in open_jobs.items() if all(turned.get(k, 0) >= lengths[k] for k in keys)]
        for who in ready:
            del open_jobs[who]
            write_matrix(LATE if who[0] else EARLY, who[1])
        if key == 20 and turned[20] == lengths[20]:
            write_vectors()
    assert not open_jobs
    for one in jobs.values():
        assert next(one, jobs) is jobs
    assert len(jobs) == 2 * len(JOBS) + 1
    left()
    for copy in writing:
        copy.wait()


def finish_kernel(count, *refs):
    given, outs, held, (sems,) = refs[:count], refs[count : 2 * count], refs[2 * count : 3 * count], refs[3 * count :]
    loads = [pltpu.make_async_copy(given[i], held[i], sems.at[0, i]) for i in range(count)]
    stores = [pltpu.make_async_copy(held[i], outs[i], sems.at[1, i]) for i in range(count)]
    for load in loads:
        load.start()
    for load, store in zip(loads, stores):
        load.wait()
        store.start()
    for store in stores:
        store.wait()


def run_kernels(len_long, len_short, x_long, x_short, cot_long, cot_short, weights, bias, gain, bias_up):
    n_seq, n_dp = lax.axis_size("seq"), lax.axis_size("dp")
    tl, ts, width = x_long.shape[1], x_short.shape[1], x_long.shape[2]
    rows, hidden = tl + ts, bias_up.shape[1]
    sizes, _ = matrix_rows(width, hidden)
    half = width // 2
    sums = (LAYERS, 8 + hidden // width, width)
    two_d, tall = (rows, width), (rows, hidden)
    bf = lambda *shape: pltpu.VMEM(shape, BF16)
    f32 = lambda *shape: pltpu.VMEM(shape, F32)
    group = (n_seq,) + two_d
    kept = dict(
        rows=(two_d, BF16), query=(two_d, BF16), keys=(group, BF16), values=(group, BF16), context=(two_d, BF16),
        scaled_one=(two_d, F32), inverse_one=((rows, 128), F32), normed=(two_d, BF16), slope=(tall, BF16),
        hidden=(tall, BF16), scaled_two=(two_d, F32), inverse_two=((rows, 128), F32), rows_far=(two_d, BF16),
        normed_far=(two_d, BF16),
    )
    finals = (
        (LAYERS, width // n_seq, 3 * width // n_dp),
        (LAYERS, width // n_seq, width // n_dp),
        (LAYERS, width // n_seq, hidden // n_dp),
        (LAYERS, width // n_dp, hidden // n_seq),
    )
    core, land = [], []
    copies = LAYERS * 7 + 5 + LAYERS * (4 + hidden // width)
    for number, (matrix, _, _) in enumerate(JOBS):
        count = job_rows(number, sizes)[1]
        free = len(BLOCKS[matrix])
        core.append(bf(*(2,) * free, count, half))
        land.append([bf(*(2,) * (free - 1 - i), count, half) for i in range(free)])
        copies += LAYERS * (free + 2)
    scratch = dict(
        pool=bf(2, 4, width, width),
        hidden_far=bf(rows, hidden // 2),
        normed_x=bf(LAYERS, *two_d),
        two=f32(*two_d),
        vec=f32(*sums),
        small=f32(*sums),
        small_sum=f32(11, *sums),
        feed=bf(*two_d),
        feed_far=bf(LAYERS, *two_d),
        pre=bf(*tall),
        pre_far=bf(LAYERS, rows, hidden // 2),
        branch=bf(*two_d),
        grad_context=bf(*two_d),
        packed=bf(*two_d),
        parts=bf(n_seq, rows, 2 * width),
        near=bf(LAYERS, 2, rows, 2 * width),
        far_send=bf(*two_d),
        far_recv=bf(LAYERS, *two_d),
        grads=[bf(1 + LAYERS, *(2,) * len(BLOCKS[m]), sizes[m], half) for m in range(4)],
        core=core,
        land=land,
        pool_sem=pltpu.SemaphoreType.DMA((10, 4)),
        store_sem=pltpu.SemaphoreType.DMA((len(kept),)),
        load_sem=pltpu.SemaphoreType.DMA((len(kept),)),
        far_sem=pltpu.SemaphoreType.DMA((2,)),
        send=pltpu.SemaphoreType.DMA((copies,)),
        recv=pltpu.SemaphoreType.DMA((copies,)),
        credit=pltpu.SemaphoreType.REGULAR((len(JOBS),)),
        y_rows=bf(*two_d),
        total=f32(LAYERS, 2, sum(sizes), half),
        flip=f32(half, 2 * max(sizes)),
        finals=[f32(*shape) for shape in finals],
        bias_out=f32(6, LAYERS, width // n_dp),
        gain_out=f32(LAYERS, 2, width // n_dp),
        bias_up_out=f32(LAYERS, hidden // n_dp),
        out_sem=pltpu.SemaphoreType.DMA((4 + 4 * LAYERS + 3,)),
        **{name: pltpu.VMEM(*shape) for name, shape in kept.items()},
    )
    struct = lambda shape, dtype=F32: jax.ShapeDtypeStruct(shape, dtype)
    ins = dict(
        len_long=len_long, len_short=len_short, x_long=x_long, x_short=x_short, cot_long=cot_long,
        cot_short=cot_short, weights=list(weights), bias=bias, gain=gain, bias_up=bias_up,
    )
    in_specs = dict.fromkeys(ins, VMEM)
    in_specs.update(len_long=SMEM, len_short=SMEM, weights=[ANY] * 4)
    outs = dict(
        y_long=struct(x_long.shape, BF16),
        y_short=struct(x_short.shape, BF16),
        dx_long=struct(x_long.shape),
        dx_short=struct(x_short.shape),
        finals=[struct(shape) for shape in finals],
        bias_out=struct((6, LAYERS, width // n_dp)),
        gain_out=struct((LAYERS, 2, width // n_dp)),
        bias_up_out=struct((LAYERS, hidden // n_dp)),
        kept={name: struct(*shape) for name, shape in kept.items()},
    )
    out_specs = jax.tree.map(lambda _: ANY, outs)
    trees = [jax.tree.flatten(part) for part in (ins, outs, scratch)]
    index = iter(range(sum(len(leaves) for leaves, _ in trees)))
    numbered = [jax.tree.unflatten(tree, [next(index) for _ in leaves]) for leaves, tree in trees]
    names = {**numbered[0], **numbered[1], **dict(scratch=numbered[2])}
    places, tree = jax.tree.flatten(names)

    def kernel(*refs):
        encoder_kernel(tree, None, *(refs[i] for i in places))

    flat_out = pl.pallas_call(
        kernel,
        out_shape=trees[1][0],
        in_specs=jax.tree.leaves(in_specs),
        out_specs=jax.tree.leaves(out_specs),
        scratch_shapes=trees[2][0],
        compiler_params=pltpu.CompilerParams(collective_id=0, has_side_effects=True, vmem_limit_bytes=VMEM_LIMIT),
        name="encoder",
    )(*trees[0][0])
    made = jax.tree.unflatten(trees[1][1], flat_out)
    results = [made[name] for name in ("y_long", "y_short", "dx_long", "dx_short")] + made["finals"]
    results += [made["bias_out"], made["gain_out"], made["bias_up_out"]]
    count = len(results)
    return pl.pallas_call(
        partial(finish_kernel, count),
        out_shape=[struct(one.shape, one.dtype) for one in results],
        in_specs=[ANY] * count,
        out_specs=[ANY] * count,
        scratch_shapes=[pltpu.VMEM(one.shape, one.dtype) for one in results] + [pltpu.SemaphoreType.DMA((2, count))],
        compiler_params=pltpu.CompilerParams(vmem_limit_bytes=VMEM_LIMIT),
        name="finish",
    )(*results)


def norm_rows(values, gain_row, shift_row):
    centre = values - jnp.mean(values, axis=-1, keepdims=True)
    spread = jnp.mean(centre * centre, axis=-1, keepdims=True)
    inverse = lax.rsqrt(spread + 1e-12)
    scaled = centre * inverse
    return (scaled * gain_row + shift_row, scaled, inverse)


def plain_norm_back(gradient, scaled, inverse, gain_row):
    inner_sum = gradient * gain_row
    mean_one = jnp.mean(inner_sum, axis=-1, keepdims=True)
    mean_two = jnp.mean(inner_sum * scaled, axis=-1, keepdims=True)
    back = inverse * (inner_sum - mean_one - scaled * mean_two)
    return (back, jnp.sum(gradient * scaled, axis=0), jnp.sum(gradient, axis=0))


def product(left_side, right_side):
    return jnp.dot(left_side, right_side, preferred_element_type=jnp.float32)


def contract_rows(left_side, right_side):
    return lax.dot_general(
        left_side, right_side, (((0,), (0,)), ((), ())), preferred_element_type=jnp.float32
    )


def times_transpose(left_side, right_side):
    return lax.dot_general(
        left_side, right_side, (((1,), (1,)), ((), ())), preferred_element_type=jnp.float32
    )


def head_scores(packed, lengths):
    seq_count, length, _, group_width = packed.shape
    split_heads = packed.reshape(seq_count, length, 3, group_width // HD, HD)
    query_rows = split_heads[:, :, 0]
    key_rows = split_heads[:, :, 1]
    value_rows = split_heads[:, :, 2]
    scores = jnp.einsum(
        "bqhd,bkhd->bhqk", query_rows, key_rows, preferred_element_type=jnp.float32
    ) * HD ** (-0.5)
    places = lax.broadcasted_iota(jnp.int32, (seq_count, length), 1)
    key_valid = (places < lengths[:, None])[:, None, None, :]
    scores = jnp.where(key_valid, scores, -1000000000.0)
    return (scores, query_rows, key_rows, value_rows)


def plain_attend(packed, lengths):
    seq_count, length, _, group_width = packed.shape
    scores, query_rows, key_rows, value_rows = head_scores(packed, lengths)
    log_total = jax.nn.logsumexp(scores, axis=-1, keepdims=True)
    weights = jnp.exp(scores - log_total).astype(jnp.bfloat16)
    context = jnp.einsum("bhqk,bkhd->bqhd", weights, value_rows, preferred_element_type=jnp.float32)
    return (context.astype(jnp.bfloat16).reshape(seq_count, length, group_width), log_total)


def plain_attend_back(packed, lengths, log_total, grad_context):
    seq_count, length, _, group_width = packed.shape
    scores, query_rows, key_rows, value_rows = head_scores(packed, lengths)
    probabilities = jnp.exp(scores - log_total)
    weights = probabilities.astype(jnp.bfloat16)
    grad_heads = grad_context.reshape(seq_count, length, group_width // HD, HD)
    grad_values = jnp.einsum(
        "bhqk,bqhd->bkhd", weights, grad_heads, preferred_element_type=jnp.float32
    )
    grad_probs = jnp.einsum(
        "bqhd,bkhd->bhqk", grad_heads, value_rows, preferred_element_type=jnp.float32
    )
    inner_sum = jnp.sum(probabilities * grad_probs, axis=-1, keepdims=True)
    grad_scores = (probabilities * (grad_probs - inner_sum)).astype(jnp.bfloat16)
    score_scale = HD ** (-0.5)
    grad_query = (
        jnp.einsum("bhqk,bkhd->bqhd", grad_scores, key_rows, preferred_element_type=jnp.float32)
        * score_scale
    )
    grad_keys = (
        jnp.einsum("bhqk,bqhd->bkhd", grad_scores, query_rows, preferred_element_type=jnp.float32)
        * score_scale
    )
    joined = jnp.stack([grad_query, grad_keys, grad_values], axis=2).astype(jnp.bfloat16)
    return joined.reshape(seq_count, length, 3, group_width)


def body(
    x_long,
    x_short,
    len_long,
    len_short,
    w_attn_in,
    w_attn_out,
    w_ffn_in,
    w_ffn_out,
    bias_vec,
    gain_vec,
    bias_ffn,
    cot_long,
    cot_short,
):
    long_shape = x_long.shape
    short_shape = x_short.shape
    count_long = long_shape[0] * long_shape[1]
    model_width = long_shape[2]

    def split_long(token_rows, tail):
        return token_rows[:count_long].reshape((long_shape[0], long_shape[1]) + tail)

    def split_short(token_rows, tail):
        return token_rows[count_long:].reshape((short_shape[0], short_shape[1]) + tail)

    token_rows = jnp.concatenate(
        [x_long.reshape(-1, model_width), x_short.reshape(-1, model_width)], axis=0
    )
    saved = []
    for layer_idx in range(LAYERS):
        biases = bias_vec[layer_idx].astype(jnp.float32)
        gain_rows = gain_vec[layer_idx].astype(jnp.float32)
        packed_bias = jnp.concatenate([biases[0], jnp.zeros_like(biases[0]), biases[1]])
        packed = (product(token_rows, w_attn_in[layer_idx]) + packed_bias).astype(jnp.bfloat16)
        heads_long, heads_short = (
            lax.all_to_all(
                split_long(packed, (3, model_width)), "seq", split_axis=3, concat_axis=1, tiled=True
            ),
            lax.all_to_all(
                split_short(packed, (3, model_width)),
                "seq",
                split_axis=3,
                concat_axis=1,
                tiled=True,
            ),
        )
        context_long, total_long = plain_attend(heads_long, len_long)
        context_short, total_short = plain_attend(heads_short, len_short)
        back_long, back_short = (
            lax.all_to_all(context_long, "seq", split_axis=1, concat_axis=2, tiled=True),
            lax.all_to_all(context_short, "seq", split_axis=1, concat_axis=2, tiled=True),
        )
        context = jnp.concatenate(
            [back_long.reshape(-1, model_width), back_short.reshape(-1, model_width)], axis=0
        )
        branch = product(context, w_attn_out[layer_idx]) + biases[2]
        normed, scaled_one, inverse_one = norm_rows(
            token_rows.astype(jnp.float32) + branch, gain_rows[0], biases[3]
        )
        normed = normed.astype(jnp.bfloat16)
        hidden_pre = product(normed, w_ffn_in[layer_idx]) + bias_ffn[layer_idx].astype(jnp.float32)
        hidden = jax.nn.gelu(hidden_pre, approximate=False).astype(jnp.bfloat16)
        feed_out = product(hidden, w_ffn_out[layer_idx]) + biases[4]
        layer_out, scaled_two, inverse_two = norm_rows(
            normed.astype(jnp.float32) + feed_out, gain_rows[1], biases[5]
        )
        saved.append(
            (
                token_rows,
                heads_long,
                heads_short,
                total_long,
                total_short,
                context,
                scaled_one,
                inverse_one,
                normed,
                hidden_pre,
                hidden,
                scaled_two,
                inverse_two,
            )
        )
        token_rows = layer_out.astype(jnp.bfloat16)
    y_long = token_rows[:count_long].reshape(long_shape)
    y_short = token_rows[count_long:].reshape(short_shape)
    grad_rows = jnp.concatenate(
        [cot_long.reshape(-1, model_width), cot_short.reshape(-1, model_width)], axis=0
    ).astype(jnp.float32)
    layer_grads = [None] * LAYERS
    for layer_idx in reversed(range(LAYERS)):
        (
            rows_in,
            heads_long,
            heads_short,
            total_long,
            total_short,
            context,
            scaled_one,
            inverse_one,
            normed,
            hidden_pre,
            hidden,
            scaled_two,
            inverse_two,
        ) = saved[layer_idx]
        gain_rows = gain_vec[layer_idx].astype(jnp.float32)
        grad_two, grad_gain_two, grad_shift_two = plain_norm_back(
            grad_rows, scaled_two, inverse_two, gain_rows[1]
        )
        grad_feed = grad_two.astype(jnp.bfloat16)
        grad_bias_down = jnp.sum(grad_feed.astype(jnp.float32), axis=0)
        grad_down = contract_rows(hidden, grad_feed)
        grad_hidden = times_transpose(grad_feed, w_ffn_out[layer_idx])
        gelu_value, gelu_back = jax.vjp(partial(jax.nn.gelu, approximate=False), hidden_pre)
        grad_pre = gelu_back(grad_hidden)[0].astype(jnp.bfloat16)
        grad_bias_up = jnp.sum(grad_pre.astype(jnp.float32), axis=0)
        grad_up = contract_rows(normed, grad_pre)
        grad_normed = grad_two + times_transpose(grad_pre, w_ffn_in[layer_idx])
        grad_one, grad_gain_one, grad_shift_one = plain_norm_back(
            grad_normed, scaled_one, inverse_one, gain_rows[0]
        )
        grad_branch = grad_one.astype(jnp.bfloat16)
        grad_bias_out = jnp.sum(grad_branch.astype(jnp.float32), axis=0)
        grad_out = contract_rows(context, grad_branch)
        grad_context = times_transpose(grad_branch, w_attn_out[layer_idx]).astype(jnp.bfloat16)
        grad_heads_long, grad_heads_short = (
            lax.all_to_all(
                split_long(grad_context, (model_width,)),
                "seq",
                split_axis=2,
                concat_axis=1,
                tiled=True,
            ),
            lax.all_to_all(
                split_short(grad_context, (model_width,)),
                "seq",
                split_axis=2,
                concat_axis=1,
                tiled=True,
            ),
        )
        joined_long = plain_attend_back(heads_long, len_long, total_long, grad_heads_long)
        joined_short = plain_attend_back(heads_short, len_short, total_short, grad_heads_short)
        tokens_long, tokens_short = (
            lax.all_to_all(joined_long, "seq", split_axis=1, concat_axis=3, tiled=True),
            lax.all_to_all(joined_short, "seq", split_axis=1, concat_axis=3, tiled=True),
        )
        grad_packed = jnp.concatenate(
            [tokens_long.reshape(-1, 3 * model_width), tokens_short.reshape(-1, 3 * model_width)],
            axis=0,
        )
        packed_sums = jnp.sum(grad_packed.astype(jnp.float32), axis=0)
        grad_in = contract_rows(rows_in, grad_packed)
        grad_rows = grad_one + times_transpose(grad_packed, w_attn_in[layer_idx])
        grad_bias = jnp.stack(
            [
                packed_sums[:model_width],
                packed_sums[2 * model_width :],
                grad_bias_out,
                grad_shift_one,
                grad_bias_down,
                grad_shift_two,
            ]
        )
        grad_gain = jnp.stack([grad_gain_one, grad_gain_two])
        layer_grads[layer_idx] = (
            grad_in,
            grad_out,
            grad_up,
            grad_down,
            grad_bias,
            grad_gain,
            grad_bias_up,
        )
    dx_long = grad_rows[:count_long].reshape(long_shape)
    dx_short = grad_rows[count_long:].reshape(short_shape)
    local_in = jnp.stack([entry[0] for entry in layer_grads])
    local_out = jnp.stack([entry[1] for entry in layer_grads])
    local_up = jnp.stack([entry[2] for entry in layer_grads])
    local_down = jnp.stack([entry[3] for entry in layer_grads])
    local_bias = jnp.stack([entry[4] for entry in layer_grads])
    local_gain = jnp.stack([entry[5] for entry in layer_grads])
    local_ffn = jnp.stack([entry[6] for entry in layer_grads])
    part_in, part_out, part_up, part_down = (local_in, local_out, local_up, local_down)
    sum_in, sum_out, sum_up, sum_down, sum_bias, sum_gain, sum_ffn = (
        lax.psum_scatter(part_in, "dp", scatter_dimension=2, tiled=True),
        lax.psum_scatter(part_out, "dp", scatter_dimension=2, tiled=True),
        lax.psum_scatter(part_up, "dp", scatter_dimension=2, tiled=True),
        lax.psum_scatter(part_down, "dp", scatter_dimension=2, tiled=True),
        lax.psum_scatter(local_bias, "dp", scatter_dimension=2, tiled=True),
        lax.psum_scatter(local_gain, "dp", scatter_dimension=2, tiled=True),
        lax.psum_scatter(local_ffn, "dp", scatter_dimension=1, tiled=True),
    )
    sum_in, sum_out, sum_up, sum_down = (
        lax.psum_scatter(
            sum_in.astype(jnp.bfloat16), "seq", scatter_dimension=1, tiled=True
        ).astype(jnp.float32),
        lax.psum_scatter(
            sum_out.astype(jnp.bfloat16), "seq", scatter_dimension=1, tiled=True
        ).astype(jnp.float32),
        lax.psum_scatter(
            sum_up.astype(jnp.bfloat16), "seq", scatter_dimension=1, tiled=True
        ).astype(jnp.float32),
        lax.psum_scatter(
            sum_down.astype(jnp.bfloat16), "seq", scatter_dimension=1, tiled=True
        ).astype(jnp.float32),
    )
    sum_bias, sum_gain, sum_ffn = lax.psum((sum_bias, sum_gain, sum_ffn), "seq")
    return (
        y_long,
        y_short,
        dx_long,
        dx_short,
        sum_in,
        sum_out,
        sum_up,
        sum_down,
        sum_bias,
        sum_gain,
        sum_ffn,
    )


def fast_body(
    x_long, x_short, len_long, len_short, w_attn_in, w_attn_out, w_ffn_in, w_ffn_out,
    bias_vec, gain_vec, bias_ffn, cot_long, cot_short,
):
    weights = (w_attn_in, w_attn_out, w_ffn_in, w_ffn_out)
    outs = list(
        run_kernels(
            len_long, len_short, x_long, x_short, cot_long, cot_short, weights,
            bias_vec.transpose(1, 0, 2), gain_vec, bias_ffn,
        )
    )
    outs[7] = outs[7].transpose(0, 2, 1)
    outs[8] = outs[8].transpose(1, 0, 2)
    return tuple(outs)


def solution(mesh):
    tokens = P("dp", "seq", None)
    matrix = P(None, "seq", "dp")
    vector = P(None, None, "dp")
    return jax.shard_map(
        fast_body if mesh.shape["dp"] == 8 and mesh.shape["seq"] == 4 else body,
        mesh=mesh,
        in_specs=(tokens, tokens, P("dp"), P("dp")) + (P(),) * 7 + (tokens, tokens),
        out_specs=(tokens,) * 4 + (matrix,) * 4 + (vector, vector, P(None, "dp")),
        check_vma=False,
    )
```

```python
from functools import partial
from types import SimpleNamespace

import jax
import jax.numpy as jnp
from jax import lax
from jax.experimental import pallas as pl
from jax.experimental.pallas import tpu as pltpu
from jax.sharding import PartitionSpec as P

HD = 64
LAYERS = 2
PAIR = 2 * HD
F32 = jnp.float32
BF16 = jnp.bfloat16
MESH = pl.DeviceIdType.MESH
VMEM_LIMIT = 63 << 20
ANY = pl.BlockSpec(memory_space=pl.ANY)
VMEM = pl.BlockSpec(memory_space=pltpu.VMEM)
SMEM = pl.BlockSpec(memory_space=pltpu.SMEM)


def dot(left, right):
    return jnp.dot(left, right, preferred_element_type=F32)


def dot_t(left, right):
    return lax.dot_general(left, right, (((1,), (1,)), ((), ())), preferred_element_type=F32)


def t_dot(left, right):
    return lax.dot_general(left, right, (((0,), (0,)), ((), ())), preferred_element_type=F32)


def row_mean(values):
    return jnp.mean(values, axis=-1, keepdims=True)


def col_sum(values):
    return jnp.sum(values, axis=0, keepdims=True)


def chunk(i, step, base=0, mult=None):
    return pl.ds(pl.multiple_of(base + i * step, mult or step), step)


ZH, ZL, Y, X, C = range(5)


def place():
    d, s = lax.axis_index("dp"), lax.axis_index("seq")
    return d // 4, lax.rem(d // 2, 2), lax.rem(d, 2), s // 2, lax.rem(s, 2)


def peer_devices(at):
    peers = []
    for digit in range(5):
        zh, zl, y, x, c = (1 - value if i == digit else value for i, value in enumerate(at))
        peers.append((4 * zh + 2 * zl + y, 2 * x + c))
    return peers


def greet(peers):
    barrier = pltpu.get_barrier_semaphore()
    for peer in peers:
        pl.semaphore_signal(barrier, inc=1, device_id=peer, device_id_type=MESH)
    pl.semaphore_wait(barrier, len(peers))


def low_lanes():
    return lax.broadcasted_iota(jnp.int32, (1, PAIR), 1) < HD


def stacked(rows):
    low = low_lanes()
    masks = (low.astype(F32).astype(BF16), (~low).astype(F32).astype(BF16))
    return jnp.concatenate([rows * mask for mask in masks], axis=0)


def joined(ref, own, lanes):
    return jnp.concatenate([ref[s, own, lanes] for s in range(ref.shape[0])], axis=0)


def softmax_t(keys, query, length):
    place = lax.broadcasted_iota(jnp.int32, (keys.shape[0], 1), 0)
    scores = jnp.where(place < length, dot_t(keys, query), -1e9)
    powers = jnp.exp(scores - jnp.max(scores, axis=0, keepdims=True))
    return powers * (1.0 / jnp.sum(powers, axis=0, keepdims=True))


def attend_pair(query, keys, values, length):
    weights = softmax_t(keys, stacked(query), length).astype(BF16)
    both = t_dot(weights, values)
    count = query.shape[0]
    return jnp.where(low_lanes(), both[:count], both[count:])


def back_pair(query, keys, values, grad, length):
    count = query.shape[0]
    query, grad = stacked(query), stacked(grad)
    probs = softmax_t(keys, query, length)
    grad_probs = dot_t(values, grad)
    inner = col_sum(probs * grad_probs)
    grad_scores = (probs * (grad_probs - inner)).astype(BF16)
    both = t_dot(keys, grad_scores)
    grad_query = jnp.concatenate([both[:HD, :count], both[HD:, count:]], axis=0).T
    return grad_query * HD**-0.5, dot(grad_scores, query), dot(probs.astype(BF16), grad)


def attend(tl, lens, query, keys, values, context):
    rows, width = query.shape
    for p in range(width // PAIR):
        lanes = slice(p * PAIR, (p + 1) * PAIR)
        for which, own in enumerate((slice(0, tl), slice(tl, rows))):
            context[own, lanes] = attend_pair(
                query[own, lanes], joined(keys, own, lanes), joined(values, own, lanes), lens[which]
            ).astype(BF16)


def attend_back(tl, lens, query, keys, values, grad, packed, parts, small, many=3):
    rows, width = query.shape

    @pl.loop(0, width // PAIR // many)
    def _(i):
        for u in range(many):
            lanes = pl.ds(pl.multiple_of((i * many + u) * PAIR, PAIR), PAIR)
            vlanes = pl.ds(pl.multiple_of(width + (i * many + u) * PAIR, PAIR), PAIR)
            sums_q = jnp.zeros((1, PAIR), F32)
            sums_v = jnp.zeros((1, PAIR), F32)
            for which, own in enumerate((slice(0, tl), slice(tl, rows))):
                count = own.stop - own.start
                grad_q, grad_k, grad_v = back_pair(
                    query[own, lanes], joined(keys, own, lanes), joined(values, own, lanes), grad[own, lanes], lens[which]
                )
                grad_q = grad_q.astype(BF16)
                packed[own, lanes] = grad_q
                sums_q += col_sum(grad_q.astype(F32))
                sums_v += col_sum(grad_v)
                grad_k = grad_k.astype(BF16)
                grad_v = grad_v.astype(BF16)
                for s in range(parts.shape[0]):
                    parts[s, own, lanes] = grad_k[count * s : count * (s + 1)]
                    parts[s, own, vlanes] = grad_v[count * s : count * (s + 1)]
            small[0:1, lanes] = sums_q
            small[1:2, lanes] = sums_v


def fill_vec(vec, layer, bias, gain, bias_up):
    width = vec.shape[1]
    vec[0:6, :] = bias[:, layer, :].astype(F32)
    vec[6:8, :] = gain[layer].astype(F32)
    for part in range(bias_up.shape[1] // width):
        vec[8 + part : 9 + part, :] = bias_up[layer : layer + 1, part * width : (part + 1) * width].astype(F32)


def project_query(own, tile, vec, query):
    @pl.loop(0, own.shape[1] // 256)
    def _(i):
        cols = chunk(i, 256)
        out = dot(own[...], tile[:, cols]) + vec[0:1, cols]
        query[:, cols] = out.astype(BF16) * jnp.asarray(HD**-0.5, BF16)


def project_keys(rows, key_tile, value_tile, vec, keys, values):
    @pl.loop(0, keys.shape[1] // 256)
    def _(i):
        cols = chunk(i, 256)
        keys[:, cols] = dot(rows[...], key_tile[:, cols]).astype(BF16)
        values[:, cols] = (dot(rows[...], value_tile[:, cols]) + vec[1:2, cols]).astype(BF16)


def normalize(residual, gain_row, shift_row, scaled_o, inverse_o, out):
    centre = residual - row_mean(residual)
    inverse = lax.rsqrt(row_mean(centre * centre) + 1e-12)
    scaled = centre * inverse
    scaled_o[...] = scaled
    inverse_o[...] = jnp.broadcast_to(inverse, inverse_o.shape)
    out[...] = (scaled * gain_row + shift_row).astype(BF16)


def out_norm(own, context, w_out, vec, scaled, inverse, normed):
    residual = own[...].astype(F32) + dot(context[...], w_out[...]) + vec[2:3, :]
    normalize(residual, vec[6:7, :], vec[3:4, :], scaled, inverse, normed)


def gelu(pre):
    below = 0.5 + 0.5 * lax.erf(pre * (2.0**-0.5))
    return below, (pre * below).astype(BF16)


def ffn_up(normed, tiles, vec, hidden, slope):
    width = normed.shape[1]
    for part in range(hidden.shape[1] // width):

        @pl.loop(0, width // 256)
        def _(i, part=part):
            cols = chunk(i, 256, part * width)
            pre = dot(normed[...], tiles[part, :, chunk(i, 256)]) + vec[8 + part : 9 + part, chunk(i, 256)]
            below, hidden[:, cols] = gelu(pre)
            slope[:, cols] = (below + pre * (jnp.exp(pre * pre * -0.5) * 0.3989422804014327)).astype(BF16)


def half_hidden(normed, tiles, vec, x, out):
    width = normed.shape[1]
    for part in range(out.shape[1] // width):
        at = x * (out.shape[1] // width) + part

        @pl.loop(0, width // 256)
        def _(i, part=part, at=at):
            pre = dot(normed[...], tiles[at, :, chunk(i, 256)]) + vec[pl.ds(8 + at, 1), chunk(i, 256)]
            out[:, chunk(i, 256, part * width)] = gelu(pre)[1]


def ffn_down(normed, hidden, tiles, vec, scaled, inverse, out):
    width = normed.shape[1]
    residual = normed[...].astype(F32) + vec[4:5, :]
    for part in range(hidden.shape[1] // width):
        residual += dot(hidden[:, part * width : (part + 1) * width], tiles[part])
    normalize(residual, vec[7:8, :], vec[5:6, :], scaled, inverse, out)


def norm_back(gradient, scaled, inverse, gain_row):
    inner = gradient * gain_row
    return inverse * (inner - row_mean(inner) - scaled * row_mean(inner * scaled))


def norm_two_back(grad, scaled, inverse, vec, two, feed, small):
    value = grad[...]
    small[5:6, :] = col_sum(value)
    small[7:8, :] = col_sum(value * scaled[...])
    back = norm_back(value, scaled[...], inverse[:, 0:1], vec[7:8, :])
    two[...] = back
    feed[...] = back.astype(BF16)
    small[4:5, :] = col_sum(feed[...].astype(F32))


def norm_one_back(two, scaled, inverse, vec, branch, small):
    value = two[...]
    small[3:4, :] = col_sum(value)
    small[6:7, :] = col_sum(value * scaled[...])
    back = norm_back(value, scaled[...], inverse[:, 0:1], vec[6:7, :])
    two[...] = back
    branch[...] = back.astype(BF16)
    small[2:3, :] = col_sum(branch[...].astype(F32))


def context_back(branch, w_out, grad):
    @pl.loop(0, branch.shape[1] // 256)
    def _(i):
        cols = chunk(i, 256)
        grad[:, cols] = dot_t(branch[...], w_out[cols, :]).astype(BF16)


IN, OUT, UP, DOWN = range(4)
BLOCKS = ((ZH, ZL, Y, X), (ZH, ZL, Y, X), (ZH, ZL, X), (ZH, ZL, Y))
JOBS = ((DOWN, 0, 2), (OUT, 0, 1), (UP, 0, 2), (IN, 0, 3), (IN, 1, 3), (IN, 2, 3), (DOWN, 1, 2), (UP, 1, 2))
ALL = slice(None)
LATE, EARLY = LAYERS - 1, 0

ORDERS = (
    ((Y, ZH, ZL), (X, ZL, Y, ZH), (X, ZL, ZH), (Y, X, ZL, ZH), (X, Y, ZH, ZL), (Y, X, ZL, ZH), (Y, ZL, ZH), (ZH, X, ZL)),
    ((ZL, Y, ZH), (ZL, Y, ZH, X), (ZL, X, ZH), (Y, ZL, ZH, X), (X, ZL, Y, ZH), (Y, X, ZH, ZL), (Y, ZH, ZL), (X, ZH, ZL)),
)
LATE_POINTS = (
    (),
    (),
    (),
    (),
    (),
    (),
    (1, 6, 0, 1,),
    (6, 0,),
    (7, 1, 2, 4, 3, 7, 6, 0, 5,),
    (),
    (2, 3, 4,),
)
EARLY_POINTS = (
    (5, 1,),
    (),
    (),
    (),
    (7,),
    (),
    (2, 3, 6, 0,),
    (3, 4, 1, 5, 7, 20, 6,),
    (0, 20, 2, 16, 1, 5, 4,),
    (16, 7, 11, 2, 17, 10, 12, 4, 5, 3, 20, 17, 11, 10, 12, 3, 5,),
    (16, 4, 15, 20, 1, 13, 14, 15, 11, 13, 10, 14, 16, 4, 15, 11, 12, 6, 20, 14, 13, 10,),
)
TAIL = (0, 17, 15, 12, 14, 7, 10, 13, 11, 20, 15, 17, 13, 16, 14, 11, 10, 12, 11, 5, 15, 14, 17, 12, 15, 13, 17, 13,
        3, 14, 2, 16,)


def matrix_rows(width, hidden):
    sizes = (3 * width // 16, width // 16, hidden // 16, (hidden // width) * (width // 16))
    return sizes, tuple(sum(sizes[:i]) for i in range(4))


def job_rows(number, sizes):
    matrix, part, parts = JOBS[number]
    count = sizes[matrix] // parts
    return part * count, count


class Copies:
    def __init__(self, send, recv, peers):
        self.send, self.recv, self.peers = send, recv, peers
        self.count = 0
        self.open = {}

    def make(self, src, dst, to):
        copy = pltpu.make_async_remote_copy(
            src_ref=src,
            dst_ref=dst,
            send_sem=self.send.at[self.count],
            recv_sem=self.recv.at[self.count],
            device_id=self.peers[to],
            device_id_type=MESH,
        )
        self.count += 1
        return copy

    def push(self, src, dst, to):
        copy = self.make(src, dst, to)
        copy.start()
        self.open[id(copy)] = copy
        return copy

    def left(self, *copies):
        for copy in copies or tuple(self.open.values()):
            copy.wait_send()
            del self.open[id(copy)]


def encoder_kernel(tree, counts, *refs):
    r = SimpleNamespace(**jax.tree.unflatten(tree, refs))
    b = SimpleNamespace(**r.scratch)
    w_in, w_out, w_up, w_down = r.weights
    tl = r.x_long.shape[1]
    n_seq, rows, width = b.keys.shape
    hidden = b.hidden.shape[1]
    parts, half = hidden // width, width // 2
    sizes, starts = matrix_rows(width, hidden)
    lens = (r.len_long[0], r.len_short[0])
    at = place()
    x, c = at[X], at[C]
    links = Copies(b.send, b.recv, peer_devices(at))
    push, left = links.push, links.left

    waits = {}

    def start_copy(src, dst, sem):
        copy = pltpu.make_async_copy(src, dst, sem)
        copy.start()
        return copy

    square = lambda i: pl.ds(i * width, width)
    pool_count = iter(range(b.pool_sem.shape[0]))
    DOWN_W, UP_W, REST_W = range(3)

    def load_weights(layer, which, pool):
        if which == DOWN_W:
            tiles = [w_down.at[layer, square(i), :] for i in range(parts)]
        elif which == UP_W:
            tiles = [w_up.at[layer, :, square(i)] for i in range(parts)]
        else:
            tiles = [w_in.at[layer, :, square(i)] for i in range(3)] + [w_out.at[layer]]
        sems = b.pool_sem.at[next(pool_count)]
        waits[pool] = [start_copy(tile, b.pool.at[pool, i], sems.at[i]) for i, tile in enumerate(tiles)]

    def tiles_of(pool):
        for copy in waits.pop(pool, ()):
            copy.wait()
        return b.pool.at[pool]

    kept = {name: (getattr(b, name), ref, i) for i, (name, ref) in enumerate(r.kept.items())}
    storing, loading = {}, {}

    def store(**names):
        for name in names:
            src, dst, i = kept[name]
            storing[name] = start_copy(src, dst, b.store_sem.at[i])

    def stored(**names):
        for name in names:
            storing.pop(name).wait()

    def reload(**names):
        for name in names:
            dst, src, i = kept[name]
            loading[name] = start_copy(src, dst, b.load_sem.at[i])

    def need(**names):
        for name in names:
            if name in loading:
                loading.pop(name).wait()

    load_weights(0, REST_W, 0)
    load_weights(0, UP_W, 1)
    b.rows[0:tl, :] = r.x_long[0]
    b.rows[tl:, :] = r.x_short[0]
    greet(links.peers)

    mine, far = 2 * x + c, 2 * (1 - x) + c
    beside, beyond = 2 * x + 1 - c, 2 * (1 - x) + 1 - c
    halves = (pl.ds(0, rows // 2), pl.ds(rows // 2, rows // 2))
    normed_x_flights = []
    normed_y_flights = []
    gathers = []

    for layer in range(LAYERS):
        vec = b.vec.at[layer]
        lanes = pl.ds(layer * width, width)
        group = b.parts
        flights = [push(b.rows.at[part], group.at[mine, part, lanes], X) for part in halves]
        flights.append(push(b.rows, group.at[mine, :, lanes], C))
        if layer == 0:
            for i in range(LAYERS):
                fill_vec(b.vec.at[i], i, r.bias, r.gain, r.bias_up)
            store(rows=1)
        else:
            normed_x_flights.append(push(b.normed, b.normed_x.at[0], X))
            stored(query=1, keys=1, values=1)
        rest = tiles_of(layer)
        project_query(b.rows, rest.at[0], vec, b.query)

        def keys_of(source, where, rest=rest, vec=vec):
            project_keys(source, rest.at[1], rest.at[2], vec, b.keys.at[where], b.values.at[where])

        keys_of(b.rows, mine)
        flights[2].wait_recv()
        keys_of(group.at[beside, :, lanes], beside)
        passed = []
        for i, part in enumerate(halves):
            flights[i].wait_recv()
            passed.append(push(group.at[far, part, lanes], group.at[far, part, lanes], C))
        if layer == 0:
            far_copy = start_copy(group.at[far, :, lanes], r.kept["rows_far"], b.far_sem.at[0])
        else:
            far_copy = start_copy(group.at[far, :, lanes], b.rows_far, b.far_sem.at[1])
        keys_of(group.at[far, :, lanes], far)
        gathers += passed + (flights if layer else [])
        for copy in passed:
            copy.wait_recv()
        keys_of(group.at[beyond, :, lanes], beyond)
        if layer == 0:
            store(query=1, keys=1, values=1)
        else:
            stored(context=1)
        attend(tl, lens, b.query, b.keys, b.values, b.context)
        if layer == 0:
            store(context=1)
        else:
            stored(scaled_one=1, inverse_one=1, normed=1)
            left(*normed_x_flights, *normed_y_flights)
        out_norm(b.rows, b.context, rest.at[3], vec, b.scaled_one, b.inverse_one, b.normed)
        load_weights(layer, DOWN_W, layer)
        if layer == 0:
            normed_y_flights.append(push(b.normed, r.kept["normed_far"], Y))
            store(scaled_one=1, inverse_one=1, normed=1)
        else:
            normed_x_flights.append(push(b.normed, b.normed_x.at[1], X))
            normed_y_flights.append(push(b.normed, b.normed_far, Y))
            stored(hidden=1, slope=1)
        ffn_up(b.normed, tiles_of(1 - layer), vec, b.hidden, b.slope)
        if layer == 0:
            load_weights(1, REST_W, 1)
            store(hidden=1, slope=1)
            stored(rows=1)
            left(*flights)
        else:
            stored(scaled_two=1, inverse_two=1)
        far_copy.wait()
        after = b.rows if layer == 0 else b.y_rows
        ffn_down(b.normed, b.hidden, tiles_of(layer), vec, b.scaled_two, b.inverse_two, after)
        if layer == 0:
            load_weights(1, UP_W, 0)
            store(scaled_two=1, inverse_two=1)
    left(*gathers)
    out_count = iter(range(b.out_sem.shape[0]))
    writing = []

    def write(src, dst):
        writing.append(start_copy(src, dst, b.out_sem.at[next(out_count)]))

    write(b.y_rows.at[0:tl], r.y_long.at[0])
    write(b.y_rows.at[tl:rows], r.y_short.at[0])

    two, small = b.two, b.small
    two[0:tl, :] = r.cot_long[0].astype(F32)
    two[tl:, :] = r.cot_short[0].astype(F32)

    step = 384

    def slot(layer, core):
        return (1 - (c - core) * (c - core)) * (1 + layer)

    def spread(layer, matrix, out, first_row, block0=0, row0=0):
        piece = sizes[OUT if matrix == DOWN else matrix]
        row = 0
        while row < out.shape[0]:
            spot = first_row + row
            count = min(piece - spot % piece, out.shape[0] - row)
            block, core, inside = block0 + spot // (2 * piece), (spot // piece) % 2, row0 + spot % piece
            digits = (block // 4, (block // 2) % 2, block % 2)
            index = (slot(layer, core),) + tuple(digits[axis] for axis in BLOCKS[matrix] if axis != X)
            for side in range(2):
                value = out[row : row + count, half * side : half * (side + 1)].astype(BF16)
                if matrix == DOWN:
                    b.grads[matrix][index + (pl.ds(inside + side * piece, count),)] = value
                else:
                    b.grads[matrix][index + (side, pl.ds(inside, count))] = value
            row += count

    sent = [SimpleNamespace(pre=[]) for _ in range(LAYERS)]
    normed_x_flights = [(normed_x_flights[i], i) for i in range(LAYERS)]

    def far_hidden(layer, pool):
        normed_x_flights[layer][0].wait_recv()
        half_hidden(b.normed_x.at[layer], tiles_of(pool), b.vec.at[layer], x, b.hidden_far)

    def grad_down(layer):
        sent[layer].feed.wait_recv()
        need(hidden=1)
        if layer == EARLY:
            far_hidden(layer, 1)
        for e in range(parts // 2):
            here = pl.ds(pl.multiple_of(x * (hidden // 2) + e * width, 128), width)
            for m in range(width // step):
                cols = slice(m * step, (m + 1) * step)
                out = t_dot(b.feed[:, cols], b.hidden[:, here])
                out += t_dot(b.feed_far[layer, :, cols], b.hidden_far[:, e * width : (e + 1) * width])
                spread(layer, DOWN, out, m * step, 0, 2 * e * sizes[OUT])
        if layer == LATE:
            reload(hidden=1)

    def grad_out(layer):
        need(context=1)
        for m in range(width // step):
            cols = slice(m * step, (m + 1) * step)
            spread(layer, OUT, t_dot(b.branch[:, cols], b.context[...]), m * step)
        if layer == LATE:
            reload(context=1)

    def grad_up(layer):
        for copy in sent[layer].pre:
            copy.wait_recv()
        need(normed=1, normed_far=1)
        if layer == LATE:
            normed_y_flights[LATE].wait_recv()
        for m in range(hidden // 2 // step):
            here = pl.ds(pl.multiple_of((2 * m + at[Y]) * step, 128), step)
            out = t_dot(b.pre[:, here], b.normed[...])
            out += t_dot(b.pre_far[layer, :, m * step : (m + 1) * step], b.normed_far[...])
            spread(layer, UP, out, 0, 2 * m)
        if layer == LATE:
            normed_y_flights[EARLY].wait_recv()
            left(normed_y_flights[LATE])
            left(normed_x_flights[LATE][0])
            reload(normed=1, normed_far=1)

    def grad_in(layer):
        need(rows=1, rows_far=1)
        for m in range(3 * width // step):
            if m * step < width:
                out = t_dot(b.packed[:, m * step : (m + 1) * step], b.rows[...])
            else:
                cols = slice(m * step - width, (m + 1) * step - width)
                out = t_dot(b.near[layer, 0, :, cols], b.rows_far[...])
                out += t_dot(b.near[layer, 1, :, cols], b.rows[...])
            spread(layer, IN, out, m * step)
        if layer == LATE:
            reload(rows=1, rows_far=1)

    grad_fns = {IN: grad_in, OUT: grad_out, UP: grad_up, DOWN: grad_down}
    made = set()

    total = b.total

    def job(layer, number):
        matrix, order = JOBS[number][0], ORDERS[layer][number]
        axes = BLOCKS[matrix]
        first, count = job_rows(number, sizes)
        part = pl.ds(first, count)
        mine_ref = b.grads[matrix].at[1 + layer]
        free = list(axes)
        if (layer, matrix) not in made:
            made.add((layer, matrix))
            grad_fns[matrix](layer)
        if layer == EARLY:
            pl.semaphore_wait(b.credit.at[number], 5)
        near = push(b.grads[matrix].at[(0,) + (ALL,) * len(free) + (part,)], b.core[number], C)
        yield
        near.wait_recv()
        left(near)

        def add(where, landed):
            index = tuple(where.get(axis, ALL) for axis in axes)
            if len(free) >= 3:
                spot = axes.index(free[0])
                for i in range(2):
                    one = index[:spot] + (i,) + index[spot + 1 :] + (part,)
                    mine_ref[one] = mine_ref[one] + landed[i]
            else:
                mine_ref[index + (part,)] = mine_ref[index + (part,)] + landed[...]

        add({}, b.core[number])
        where = {}
        for step_at, axis in enumerate(order):
            free.remove(axis)
            landing = b.land[number][step_at]
            away = {**where, axis: 1 - at[axis]}
            one = push(mine_ref.at[tuple(away.get(a, ALL) for a in axes) + (part,)], landing, axis)
            yield
            one.wait_recv()
            left(one)
            where[axis] = at[axis]
            if free:
                add(where, landing)
            else:
                index = tuple(where[a] for a in axes) + (part,)
                spot = pl.ds(starts[matrix] + first, count)
                total[layer, c, spot] = mine_ref[index].astype(F32) + landing[...].astype(F32)
        end = push(total.at[layer, c, spot], total.at[layer, c, spot], C)
        if layer == LATE:
            for to in links.peers:
                pl.semaphore_signal(b.credit.at[number], inc=1, device_id=to, device_id_type=MESH)
        yield
        end.wait_recv()
        left(end)

    def small_job():
        b.small_sum[0] = small[...]
        for step_at, axis in enumerate((C, X, Y, ZL, ZH)):
            one = push(b.small_sum.at[2 * step_at], b.small_sum.at[2 * step_at + 1], axis)
            yield
            one.wait_recv()
            left(one)
            b.small_sum[2 * step_at + 2] = b.small_sum[2 * step_at] + b.small_sum[2 * step_at + 1]

    jobs = {}
    turned = {}

    def turns(keys):
        for key in keys:
            turned[key] = turned.get(key, 0) + 1
            if key not in jobs:
                jobs[key] = small_job() if key == 20 else job(EARLY, key - 10) if key >= 10 else job(LATE, key)
            next(jobs[key], None)

    for layer in (LATE, EARLY):
        during = lambda point, lists=(LATE_POINTS if layer == LATE else EARLY_POINTS): turns(lists[point])
        vec, sums = b.vec.at[layer], small.at[layer]
        down_pool = 1 if layer == LATE else 0
        need(scaled_two=1, inverse_two=1)
        norm_two_back(two, b.scaled_two, b.inverse_two, vec, two, b.feed, sums)
        if layer == LATE:
            reload(scaled_two=1, inverse_two=1)
        sent[layer].feed = push(b.feed, b.feed_far.at[layer], X)
        during(0)
        need(slope=1)
        tiles = tiles_of(down_pool)
        for part in range(parts):

            @pl.loop(0, width // 256)
            def _(i, part=part, tiles=tiles, sums=sums):
                cols = chunk(i, 256, part * width)
                back = dot_t(b.feed[...], tiles[part, chunk(i, 256), :]) * b.slope[:, cols].astype(F32)
                b.pre[:, cols] = back.astype(BF16)
                sums[8 + part : 9 + part, chunk(i, 256)] = col_sum(b.pre[:, cols].astype(F32))

            other = pl.ds(pl.multiple_of((2 * part + 1 - at[Y]) * step, 128), step)
            sent[layer].pre.append(push(b.pre.at[:, other], b.pre_far.at[layer, :, pl.ds(part * step, step)], Y))
            during(1 + part)
        load_weights(layer, REST_W, down_pool)
        if layer == LATE:
            reload(slope=1)
            far_hidden(layer, 0)
        tiles = tiles_of(1 - down_pool)

        @pl.loop(0, width // 256)
        def _(i, tiles=tiles):
            cols = chunk(i, 256)
            value = two[:, cols]
            for part in range(parts):
                value += dot_t(b.pre[:, part * width : (part + 1) * width], tiles[part, chunk(i, 256), :])
            two[:, cols] = value

        if layer == LATE:
            load_weights(EARLY, DOWN_W, 0)
        need(scaled_one=1, inverse_one=1)
        norm_one_back(two, b.scaled_one, b.inverse_one, vec, b.branch, sums)
        if layer == LATE:
            reload(scaled_one=1, inverse_one=1)
        rest = tiles_of(down_pool)
        context_back(b.branch, rest.at[3], b.grad_context)
        during(5)
        during(6)
        need(query=1, keys=1, values=1)
        attend_back(tl, lens, b.query, b.keys, b.values, b.grad_context, b.packed, b.parts, sums)
        if layer == LATE:
            reload(query=1, keys=1, values=1)
        near = b.near
        scatter = [push(b.parts.at[beyond], near.at[layer, 0], C), push(b.parts.at[beside], near.at[layer, 1], C)]
        during(7)
        scatter[0].wait_recv()
        near[layer, 0] = near[layer, 0] + b.parts[far]
        if layer == EARLY:
            left(sent[LATE].far)

        @pl.loop(0, width // 256)
        def _(i, layer=layer, rest=rest):
            cols = chunk(i, 256)
            value = dot_t(near[layer, 0, :, 0:width], rest[1, chunk(i, 256), :])
            value += dot_t(near[layer, 0, :, width:], rest[2, chunk(i, 256), :])
            b.far_send[:, cols] = value.astype(BF16)

        sent[layer].far = push(b.far_send, b.far_recv.at[layer], X)
        scatter[1].wait_recv()
        near[layer, 1] = near[layer, 1] + b.parts[mine]
        left(*scatter)
        during(8)

        @pl.loop(0, width // 256)
        def _(i, layer=layer, rest=rest):
            cols = chunk(i, 256)
            value = two[:, cols] + dot_t(b.packed[...], rest[0, chunk(i, 256), :])
            value += dot_t(near[layer, 1, :, 0:width], rest[1, chunk(i, 256), :])
            two[:, cols] = value + dot_t(near[layer, 1, :, width:], rest[2, chunk(i, 256), :])

        if layer == LATE:
            load_weights(EARLY, UP_W, 1)
        during(9)
        during(10)
        sent[layer].far.wait_recv()
        two[...] = two[...] + b.far_recv[layer].astype(F32)
        if layer == LATE:
            left(sent[layer].feed, *sent[layer].pre)

    write(two.at[0:tl], r.dx_long.at[0])
    write(two.at[tl:rows], r.dx_short.at[0])

    d = lax.axis_index("dp")
    quarter = half // 2

    def write_matrix(layer, matrix):
        out, made_out = b.finals[matrix], r.finals[matrix]
        if matrix == DOWN:
            piece, strips = sizes[OUT], width // half
            for core in range(2):
                for e in range(strips):
                    part = pl.ds(pl.multiple_of(starts[DOWN] + piece * (strips * c + e), 8), piece)
                    out[layer, piece * core : piece * (core + 1), half * e : half * (e + 1)] = total[layer, core, part]
        else:
            part = slice(starts[matrix], starts[matrix] + sizes[matrix])
            both = jnp.concatenate([total[layer, 0, part], total[layer, 1, part]], axis=0)
            b.flip[:, 0 : both.shape[0]] = both.T
            out[layer] = b.flip[pl.ds(pl.multiple_of(quarter * c, 8), quarter), 0 : both.shape[0]]
        write(out.at[layer], made_out.at[layer])

    def write_vectors():
        wide, tall = b.bias_out.shape[2], b.bias_up_out.shape[1]
        sums = b.small_sum.at[10]
        each = width // tall
        here = pl.ds(pl.multiple_of(tall * lax.rem(d, each), 128), tall)
        for layer in range(LAYERS):
            turned = pltpu.roll(sums[layer, 0:8, :], lax.rem(width - wide * d, width), 1)
            for i in range(6):
                b.bias_out[i, layer : layer + 1, :] = turned[i : i + 1, 0:wide]
            b.gain_out[layer] = turned[6:8, 0:wide]
            b.bias_up_out[layer : layer + 1, :] = sums[layer, pl.ds(8 + d // each, 1), here]
        write(b.bias_out, r.bias_out)
        write(b.gain_out, r.gain_out)
        write(b.bias_up_out, r.bias_up_out)

    lengths = {base + i: len(ORDERS[base == 0][i]) + 3 for i in range(len(JOBS)) for base in (0, 10)}
    lengths[20] = 6
    open_jobs = {(base == 0, m): [base + i for i, job_of in enumerate(JOBS) if job_of[0] == m] for base in (0, 10) for m in range(4)}
    for key in TAIL:
        turns((key,))
        ready = [who for who, keys in open_jobs.items() if all(turned.get(k, 0) >= lengths[k] for k in keys)]
        for who in ready:
            del open_jobs[who]
            write_matrix(LATE if who[0] else EARLY, who[1])
        if key == 20 and turned[20] == lengths[20]:
            write_vectors()
    assert not open_jobs
    for one in jobs.values():
        assert next(one, jobs) is jobs
    assert len(jobs) == 2 * len(JOBS) + 1
    left()
    for copy in writing:
        copy.wait()


def finish_kernel(count, *refs):
    given, outs, held, (sems,) = refs[:count], refs[count : 2 * count], refs[2 * count : 3 * count], refs[3 * count :]
    loads = [pltpu.make_async_copy(given[i], held[i], sems.at[0, i]) for i in range(count)]
    stores = [pltpu.make_async_copy(held[i], outs[i], sems.at[1, i]) for i in range(count)]
    for load in loads:
        load.start()
    for load, store in zip(loads, stores):
        load.wait()
        store.start()
    for store in stores:
        store.wait()


def run_kernels(len_long, len_short, x_long, x_short, cot_long, cot_short, weights, bias, gain, bias_up):
    n_seq, n_dp = lax.axis_size("seq"), lax.axis_size("dp")
    tl, ts, width = x_long.shape[1], x_short.shape[1], x_long.shape[2]
    rows, hidden = tl + ts, bias_up.shape[1]
    sizes, _ = matrix_rows(width, hidden)
    half = width // 2
    sums = (LAYERS, 8 + hidden // width, width)
    two_d, tall = (rows, width), (rows, hidden)
    bf = lambda *shape: pltpu.VMEM(shape, BF16)
    f32 = lambda *shape: pltpu.VMEM(shape, F32)
    group = (n_seq,) + two_d
    kept = dict(
        rows=(two_d, BF16), query=(two_d, BF16), keys=(group, BF16), values=(group, BF16), context=(two_d, BF16),
        scaled_one=(two_d, F32), inverse_one=((rows, 128), F32), normed=(two_d, BF16), slope=(tall, BF16),
        hidden=(tall, BF16), scaled_two=(two_d, F32), inverse_two=((rows, 128), F32), rows_far=(two_d, BF16),
        normed_far=(two_d, BF16),
    )
    finals = (
        (LAYERS, width // n_seq, 3 * width // n_dp),
        (LAYERS, width // n_seq, width // n_dp),
        (LAYERS, width // n_seq, hidden // n_dp),
        (LAYERS, width // n_dp, hidden // n_seq),
    )
    core, land = [], []
    copies = LAYERS * 7 + 5 + LAYERS * (4 + hidden // width)
    for number, (matrix, _, _) in enumerate(JOBS):
        count = job_rows(number, sizes)[1]
        free = len(BLOCKS[matrix])
        core.append(bf(*(2,) * free, count, half))
        land.append([bf(*(2,) * (free - 1 - i), count, half) for i in range(free)])
        copies += LAYERS * (free + 2)
    scratch = dict(
        pool=bf(2, 4, width, width),
        hidden_far=bf(rows, hidden // 2),
        normed_x=bf(LAYERS, *two_d),
        two=f32(*two_d),
        vec=f32(*sums),
        small=f32(*sums),
        small_sum=f32(11, *sums),
        feed=bf(*two_d),
        feed_far=bf(LAYERS, *two_d),
        pre=bf(*tall),
        pre_far=bf(LAYERS, rows, hidden // 2),
        branch=bf(*two_d),
        grad_context=bf(*two_d),
        packed=bf(*two_d),
        parts=bf(n_seq, rows, 2 * width),
        near=bf(LAYERS, 2, rows, 2 * width),
        far_send=bf(*two_d),
        far_recv=bf(LAYERS, *two_d),
        grads=[bf(1 + LAYERS, *(2,) * len(BLOCKS[m]), sizes[m], half) for m in range(4)],
        core=core,
        land=land,
        pool_sem=pltpu.SemaphoreType.DMA((10, 4)),
        store_sem=pltpu.SemaphoreType.DMA((len(kept),)),
        load_sem=pltpu.SemaphoreType.DMA((len(kept),)),
        far_sem=pltpu.SemaphoreType.DMA((2,)),
        send=pltpu.SemaphoreType.DMA((copies,)),
        recv=pltpu.SemaphoreType.DMA((copies,)),
        credit=pltpu.SemaphoreType.REGULAR((len(JOBS),)),
        y_rows=bf(*two_d),
        total=f32(LAYERS, 2, sum(sizes), half),
        flip=f32(half, 2 * max(sizes)),
        finals=[f32(*shape) for shape in finals],
        bias_out=f32(6, LAYERS, width // n_dp),
        gain_out=f32(LAYERS, 2, width // n_dp),
        bias_up_out=f32(LAYERS, hidden // n_dp),
        out_sem=pltpu.SemaphoreType.DMA((4 + 4 * LAYERS + 3,)),
        **{name: pltpu.VMEM(*shape) for name, shape in kept.items()},
    )
    struct = lambda shape, dtype=F32: jax.ShapeDtypeStruct(shape, dtype)
    ins = dict(
        len_long=len_long, len_short=len_short, x_long=x_long, x_short=x_short, cot_long=cot_long,
        cot_short=cot_short, weights=list(weights), bias=bias, gain=gain, bias_up=bias_up,
    )
    in_specs = dict.fromkeys(ins, VMEM)
    in_specs.update(len_long=SMEM, len_short=SMEM, weights=[ANY] * 4)
    outs = dict(
        y_long=struct(x_long.shape, BF16),
        y_short=struct(x_short.shape, BF16),
        dx_long=struct(x_long.shape),
        dx_short=struct(x_short.shape),
        finals=[struct(shape) for shape in finals],
        bias_out=struct((6, LAYERS, width // n_dp)),
        gain_out=struct((LAYERS, 2, width // n_dp)),
        bias_up_out=struct((LAYERS, hidden // n_dp)),
        kept={name: struct(*shape) for name, shape in kept.items()},
    )
    out_specs = jax.tree.map(lambda _: ANY, outs)
    trees = [jax.tree.flatten(part) for part in (ins, outs, scratch)]
    index = iter(range(sum(len(leaves) for leaves, _ in trees)))
    numbered = [jax.tree.unflatten(tree, [next(index) for _ in leaves]) for leaves, tree in trees]
    names = {**numbered[0], **numbered[1], **dict(scratch=numbered[2])}
    places, tree = jax.tree.flatten(names)

    def kernel(*refs):
        encoder_kernel(tree, None, *(refs[i] for i in places))

    flat_out = pl.pallas_call(
        kernel,
        out_shape=trees[1][0],
        in_specs=jax.tree.leaves(in_specs),
        out_specs=jax.tree.leaves(out_specs),
        scratch_shapes=trees[2][0],
        compiler_params=pltpu.CompilerParams(collective_id=0, has_side_effects=True, vmem_limit_bytes=VMEM_LIMIT),
        name="encoder",
    )(*trees[0][0])
    made = jax.tree.unflatten(trees[1][1], flat_out)
    results = [made[name] for name in ("y_long", "y_short", "dx_long", "dx_short")] + made["finals"]
    results += [made["bias_out"], made["gain_out"], made["bias_up_out"]]
    count = len(results)
    return pl.pallas_call(
        partial(finish_kernel, count),
        out_shape=[struct(one.shape, one.dtype) for one in results],
        in_specs=[ANY] * count,
        out_specs=[ANY] * count,
        scratch_shapes=[pltpu.VMEM(one.shape, one.dtype) for one in results] + [pltpu.SemaphoreType.DMA((2, count))],
        compiler_params=pltpu.CompilerParams(vmem_limit_bytes=VMEM_LIMIT),
        name="finish",
    )(*results)


def norm_rows(values, gain_row, shift_row):
    centre = values - jnp.mean(values, axis=-1, keepdims=True)
    spread = jnp.mean(centre * centre, axis=-1, keepdims=True)
    inverse = lax.rsqrt(spread + 1e-12)
    scaled = centre * inverse
    return (scaled * gain_row + shift_row, scaled, inverse)


def plain_norm_back(gradient, scaled, inverse, gain_row):
    inner_sum = gradient * gain_row
    mean_one = jnp.mean(inner_sum, axis=-1, keepdims=True)
    mean_two = jnp.mean(inner_sum * scaled, axis=-1, keepdims=True)
    back = inverse * (inner_sum - mean_one - scaled * mean_two)
    return (back, jnp.sum(gradient * scaled, axis=0), jnp.sum(gradient, axis=0))


def product(left_side, right_side):
    return jnp.dot(left_side, right_side, preferred_element_type=jnp.float32)


def contract_rows(left_side, right_side):
    return lax.dot_general(
        left_side, right_side, (((0,), (0,)), ((), ())), preferred_element_type=jnp.float32
    )


def times_transpose(left_side, right_side):
    return lax.dot_general(
        left_side, right_side, (((1,), (1,)), ((), ())), preferred_element_type=jnp.float32
    )


def head_scores(packed, lengths):
    seq_count, length, _, group_width = packed.shape
    split_heads = packed.reshape(seq_count, length, 3, group_width // HD, HD)
    query_rows = split_heads[:, :, 0]
    key_rows = split_heads[:, :, 1]
    value_rows = split_heads[:, :, 2]
    scores = jnp.einsum(
        "bqhd,bkhd->bhqk", query_rows, key_rows, preferred_element_type=jnp.float32
    ) * HD ** (-0.5)
    places = lax.broadcasted_iota(jnp.int32, (seq_count, length), 1)
    key_valid = (places < lengths[:, None])[:, None, None, :]
    scores = jnp.where(key_valid, scores, -1000000000.0)
    return (scores, query_rows, key_rows, value_rows)


def plain_attend(packed, lengths):
    seq_count, length, _, group_width = packed.shape
    scores, query_rows, key_rows, value_rows = head_scores(packed, lengths)
    log_total = jax.nn.logsumexp(scores, axis=-1, keepdims=True)
    weights = jnp.exp(scores - log_total).astype(jnp.bfloat16)
    context = jnp.einsum("bhqk,bkhd->bqhd", weights, value_rows, preferred_element_type=jnp.float32)
    return (context.astype(jnp.bfloat16).reshape(seq_count, length, group_width), log_total)


def plain_attend_back(packed, lengths, log_total, grad_context):
    seq_count, length, _, group_width = packed.shape
    scores, query_rows, key_rows, value_rows = head_scores(packed, lengths)
    probabilities = jnp.exp(scores - log_total)
    weights = probabilities.astype(jnp.bfloat16)
    grad_heads = grad_context.reshape(seq_count, length, group_width // HD, HD)
    grad_values = jnp.einsum(
        "bhqk,bqhd->bkhd", weights, grad_heads, preferred_element_type=jnp.float32
    )
    grad_probs = jnp.einsum(
        "bqhd,bkhd->bhqk", grad_heads, value_rows, preferred_element_type=jnp.float32
    )
    inner_sum = jnp.sum(probabilities * grad_probs, axis=-1, keepdims=True)
    grad_scores = (probabilities * (grad_probs - inner_sum)).astype(jnp.bfloat16)
    score_scale = HD ** (-0.5)
    grad_query = (
        jnp.einsum("bhqk,bkhd->bqhd", grad_scores, key_rows, preferred_element_type=jnp.float32)
        * score_scale
    )
    grad_keys = (
        jnp.einsum("bhqk,bqhd->bkhd", grad_scores, query_rows, preferred_element_type=jnp.float32)
        * score_scale
    )
    joined = jnp.stack([grad_query, grad_keys, grad_values], axis=2).astype(jnp.bfloat16)
    return joined.reshape(seq_count, length, 3, group_width)


def body(
    x_long,
    x_short,
    len_long,
    len_short,
    w_attn_in,
    w_attn_out,
    w_ffn_in,
    w_ffn_out,
    bias_vec,
    gain_vec,
    bias_ffn,
    cot_long,
    cot_short,
):
    long_shape = x_long.shape
    short_shape = x_short.shape
    count_long = long_shape[0] * long_shape[1]
    model_width = long_shape[2]

    def split_long(token_rows, tail):
        return token_rows[:count_long].reshape((long_shape[0], long_shape[1]) + tail)

    def split_short(token_rows, tail):
        return token_rows[count_long:].reshape((short_shape[0], short_shape[1]) + tail)

    token_rows = jnp.concatenate(
        [x_long.reshape(-1, model_width), x_short.reshape(-1, model_width)], axis=0
    )
    saved = []
    for layer_idx in range(LAYERS):
        biases = bias_vec[layer_idx].astype(jnp.float32)
        gain_rows = gain_vec[layer_idx].astype(jnp.float32)
        packed_bias = jnp.concatenate([biases[0], jnp.zeros_like(biases[0]), biases[1]])
        packed = (product(token_rows, w_attn_in[layer_idx]) + packed_bias).astype(jnp.bfloat16)
        heads_long, heads_short = (
            lax.all_to_all(
                split_long(packed, (3, model_width)), "seq", split_axis=3, concat_axis=1, tiled=True
            ),
            lax.all_to_all(
                split_short(packed, (3, model_width)),
                "seq",
                split_axis=3,
                concat_axis=1,
                tiled=True,
            ),
        )
        context_long, total_long = plain_attend(heads_long, len_long)
        context_short, total_short = plain_attend(heads_short, len_short)
        back_long, back_short = (
            lax.all_to_all(context_long, "seq", split_axis=1, concat_axis=2, tiled=True),
            lax.all_to_all(context_short, "seq", split_axis=1, concat_axis=2, tiled=True),
        )
        context = jnp.concatenate(
            [back_long.reshape(-1, model_width), back_short.reshape(-1, model_width)], axis=0
        )
        branch = product(context, w_attn_out[layer_idx]) + biases[2]
        normed, scaled_one, inverse_one = norm_rows(
            token_rows.astype(jnp.float32) + branch, gain_rows[0], biases[3]
        )
        normed = normed.astype(jnp.bfloat16)
        hidden_pre = product(normed, w_ffn_in[layer_idx]) + bias_ffn[layer_idx].astype(jnp.float32)
        hidden = jax.nn.gelu(hidden_pre, approximate=False).astype(jnp.bfloat16)
        feed_out = product(hidden, w_ffn_out[layer_idx]) + biases[4]
        layer_out, scaled_two, inverse_two = norm_rows(
            normed.astype(jnp.float32) + feed_out, gain_rows[1], biases[5]
        )
        saved.append(
            (
                token_rows,
                heads_long,
                heads_short,
                total_long,
                total_short,
                context,
                scaled_one,
                inverse_one,
                normed,
                hidden_pre,
                hidden,
                scaled_two,
                inverse_two,
            )
        )
        token_rows = layer_out.astype(jnp.bfloat16)
    y_long = token_rows[:count_long].reshape(long_shape)
    y_short = token_rows[count_long:].reshape(short_shape)
    grad_rows = jnp.concatenate(
        [cot_long.reshape(-1, model_width), cot_short.reshape(-1, model_width)], axis=0
    ).astype(jnp.float32)
    layer_grads = [None] * LAYERS
    for layer_idx in reversed(range(LAYERS)):
        (
            rows_in,
            heads_long,
            heads_short,
            total_long,
            total_short,
            context,
            scaled_one,
            inverse_one,
            normed,
            hidden_pre,
            hidden,
            scaled_two,
            inverse_two,
        ) = saved[layer_idx]
        gain_rows = gain_vec[layer_idx].astype(jnp.float32)
        grad_two, grad_gain_two, grad_shift_two = plain_norm_back(
            grad_rows, scaled_two, inverse_two, gain_rows[1]
        )
        grad_feed = grad_two.astype(jnp.bfloat16)
        grad_bias_down = jnp.sum(grad_feed.astype(jnp.float32), axis=0)
        grad_down = contract_rows(hidden, grad_feed)
        grad_hidden = times_transpose(grad_feed, w_ffn_out[layer_idx])
        gelu_value, gelu_back = jax.vjp(partial(jax.nn.gelu, approximate=False), hidden_pre)
        grad_pre = gelu_back(grad_hidden)[0].astype(jnp.bfloat16)
        grad_bias_up = jnp.sum(grad_pre.astype(jnp.float32), axis=0)
        grad_up = contract_rows(normed, grad_pre)
        grad_normed = grad_two + times_transpose(grad_pre, w_ffn_in[layer_idx])
        grad_one, grad_gain_one, grad_shift_one = plain_norm_back(
            grad_normed, scaled_one, inverse_one, gain_rows[0]
        )
        grad_branch = grad_one.astype(jnp.bfloat16)
        grad_bias_out = jnp.sum(grad_branch.astype(jnp.float32), axis=0)
        grad_out = contract_rows(context, grad_branch)
        grad_context = times_transpose(grad_branch, w_attn_out[layer_idx]).astype(jnp.bfloat16)
        grad_heads_long, grad_heads_short = (
            lax.all_to_all(
                split_long(grad_context, (model_width,)),
                "seq",
                split_axis=2,
                concat_axis=1,
                tiled=True,
            ),
            lax.all_to_all(
                split_short(grad_context, (model_width,)),
                "seq",
                split_axis=2,
                concat_axis=1,
                tiled=True,
            ),
        )
        joined_long = plain_attend_back(heads_long, len_long, total_long, grad_heads_long)
        joined_short = plain_attend_back(heads_short, len_short, total_short, grad_heads_short)
        tokens_long, tokens_short = (
            lax.all_to_all(joined_long, "seq", split_axis=1, concat_axis=3, tiled=True),
            lax.all_to_all(joined_short, "seq", split_axis=1, concat_axis=3, tiled=True),
        )
        grad_packed = jnp.concatenate(
            [tokens_long.reshape(-1, 3 * model_width), tokens_short.reshape(-1, 3 * model_width)],
            axis=0,
        )
        packed_sums = jnp.sum(grad_packed.astype(jnp.float32), axis=0)
        grad_in = contract_rows(rows_in, grad_packed)
        grad_rows = grad_one + times_transpose(grad_packed, w_attn_in[layer_idx])
        grad_bias = jnp.stack(
            [
                packed_sums[:model_width],
                packed_sums[2 * model_width :],
                grad_bias_out,
                grad_shift_one,
                grad_bias_down,
                grad_shift_two,
            ]
        )
        grad_gain = jnp.stack([grad_gain_one, grad_gain_two])
        layer_grads[layer_idx] = (
            grad_in,
            grad_out,
            grad_up,
            grad_down,
            grad_bias,
            grad_gain,
            grad_bias_up,
        )
    dx_long = grad_rows[:count_long].reshape(long_shape)
    dx_short = grad_rows[count_long:].reshape(short_shape)
    local_in = jnp.stack([entry[0] for entry in layer_grads])
    local_out = jnp.stack([entry[1] for entry in layer_grads])
    local_up = jnp.stack([entry[2] for entry in layer_grads])
    local_down = jnp.stack([entry[3] for entry in layer_grads])
    local_bias = jnp.stack([entry[4] for entry in layer_grads])
    local_gain = jnp.stack([entry[5] for entry in layer_grads])
    local_ffn = jnp.stack([entry[6] for entry in layer_grads])
    part_in, part_out, part_up, part_down = (local_in, local_out, local_up, local_down)
    sum_in, sum_out, sum_up, sum_down, sum_bias, sum_gain, sum_ffn = (
        lax.psum_scatter(part_in, "dp", scatter_dimension=2, tiled=True),
        lax.psum_scatter(part_out, "dp", scatter_dimension=2, tiled=True),
        lax.psum_scatter(part_up, "dp", scatter_dimension=2, tiled=True),
        lax.psum_scatter(part_down, "dp", scatter_dimension=2, tiled=True),
        lax.psum_scatter(local_bias, "dp", scatter_dimension=2, tiled=True),
        lax.psum_scatter(local_gain, "dp", scatter_dimension=2, tiled=True),
        lax.psum_scatter(local_ffn, "dp", scatter_dimension=1, tiled=True),
    )
    sum_in, sum_out, sum_up, sum_down = (
        lax.psum_scatter(
            sum_in.astype(jnp.bfloat16), "seq", scatter_dimension=1, tiled=True
        ).astype(jnp.float32),
        lax.psum_scatter(
            sum_out.astype(jnp.bfloat16), "seq", scatter_dimension=1, tiled=True
        ).astype(jnp.float32),
        lax.psum_scatter(
            sum_up.astype(jnp.bfloat16), "seq", scatter_dimension=1, tiled=True
        ).astype(jnp.float32),
        lax.psum_scatter(
            sum_down.astype(jnp.bfloat16), "seq", scatter_dimension=1, tiled=True
        ).astype(jnp.float32),
    )
    sum_bias, sum_gain, sum_ffn = lax.psum((sum_bias, sum_gain, sum_ffn), "seq")
    return (
        y_long,
        y_short,
        dx_long,
        dx_short,
        sum_in,
        sum_out,
        sum_up,
        sum_down,
        sum_bias,
        sum_gain,
        sum_ffn,
    )


def fast_body(
    x_long, x_short, len_long, len_short, w_attn_in, w_attn_out, w_ffn_in, w_ffn_out,
    bias_vec, gain_vec, bias_ffn, cot_long, cot_short,
):
    weights = (w_attn_in, w_attn_out, w_ffn_in, w_ffn_out)
    outs = list(
        run_kernels(
            len_long, len_short, x_long, x_short, cot_long, cot_short, weights,
            bias_vec.transpose(1, 0, 2), gain_vec, bias_ffn,
        )
    )
    outs[7] = outs[7].transpose(0, 2, 1)
    outs[8] = outs[8].transpose(1, 0, 2)
    return tuple(outs)


def solution(mesh):
    tokens = P("dp", "seq", None)
    matrix = P(None, "seq", "dp")
    vector = P(None, None, "dp")
    return jax.shard_map(
        fast_body if mesh.shape["dp"] == 8 and mesh.shape["seq"] == 4 else body,
        mesh=mesh,
        in_specs=(tokens, tokens, P("dp"), P("dp")) + (P(),) * 7 + (tokens, tokens),
        out_specs=(tokens,) * 4 + (matrix,) * 4 + (vector, vector, P(None, "dp")),
        check_vma=False,
    )
```
